32 devices in a mesh: groups: 2 (over x), rows: 4 (over y, core), cols: 4 (over z).
Axes of the slice: x: 2, y: 2, z: 4, core: 2. Of those that a mesh axis runs over, the one named last changes fastest.
Arguments:
- tokens: bfloat16 [128, 32, 512], P(('groups', 'rows'), 'cols'), parts along dimension 0, may hold values from -6 to 6
- top_state: bfloat16 [64, 16, 2048], P(('groups', 'cols')), parts along dimension 0, may hold values from -4 to 4
- in_weight: bfloat16 [512, 1024], replicated, may hold values from -0.25 to 0.25
- conv_weight: float32 [9, 512], replicated, may hold values from -2 to 2
- bc_weight: bfloat16 [512, 256], replicated, may hold values from -0.25 to 0.25
- step_weight: bfloat16 [512, 32], replicated, may hold values from -0.25 to 0.25
- step_bias: float32 [32], replicated, may hold values from -2 to 0.5
- across_rate: float32 [16], replicated, may hold values from 0.03125 to 0.3
- down_rate: float32 [16], replicated, may hold values from 0.015625 to 0.3
- skip_gain: float32 [16], replicated, may hold values from 0.5 to 1.5
- norm_gain: float32 [512], replicated, may hold values from 0.1 to 1.9
- out_weight: bfloat16 [512, 512], replicated, may hold values from -0.25 to 0.25
Outputs:
- layer_out: bfloat16 [128, 32, 512], P(('groups', 'rows'), 'cols'), parts along dimension 0
The draws below stay inside these ranges and needn't reach their ends.
There are 2 independent parts, one for each index of `groups`. The reference program is written for one: setup_inputs(seed, part) draws one part's arguments, and reference() takes and returns one part's arrays. A program takes and returns all parts, laid end to end along the dimension named above; an argument that names none is the same for every part. Nothing has to cross between parts.
All inputs are finite; a program needn't handle non-finite values.
Results may differ from the reference program's by a relative error of at most 0.0095.
Values may be sent and summed in bfloat16 or wider, within the bound.
A program may use at most 128 MiB of HBM per device.

```python
import math
import jax
import jax.numpy as jnp
from jax import lax

D = 512
HEADS = 16
HEAD_DIM = 32
STATE = 64
INNER = 512
HEIGHT = 64
WIDTH = 32


def block_levels(stream_key, extent, shards, least, high):
    gain = 1.0
    for axis_at, parts in shards:
        draws = jax.random.uniform(jax.random.fold_in(jax.random.fold_in(stream_key, 6), axis_at), (parts,), jnp.float32, least / len(shards), high / len(shards))
        gain = gain * jnp.repeat(jnp.exp(draws), extent[axis_at] // parts).reshape((-1,) + (1,) * (len(extent) - 1 - axis_at))
    return gain


def gaussian(stream_key, dims, deviation, bound, cuts=(), held_as=jnp.bfloat16):
    values = deviation * jax.random.normal(stream_key, dims, jnp.float32)
    if cuts:
        values = values * block_levels(stream_key, dims, cuts, -0.22, 0.18)
    return jnp.clip(values, -bound, bound).astype(held_as)


def setup_inputs(seed: int = 0, part: int = 0) -> dict:
    splits = jax.random.split(jax.random.key(seed), 13)
    part_keys = jax.random.split(jax.random.fold_in(splits[12], part), 13)
    tokens = gaussian(part_keys[0], (HEIGHT, WIDTH, D), 1.0, 6.0, ((0, 4), (1, 4)))
    top_state = gaussian(part_keys[1], (WIDTH, HEADS, HEAD_DIM * STATE), 0.3, 4.0, ((0, 4),))
    in_weight = gaussian(splits[2], (D, 2 * INNER), D ** -0.5, 0.25)
    conv_weight = gaussian(splits[3], (9, INNER), 9 ** -0.5, 2.0, (), jnp.float32)
    bc_weight = gaussian(splits[4], (INNER, 4 * STATE), INNER ** -0.5, 0.25)
    step_weight = gaussian(splits[5], (INNER, 2 * HEADS), INNER ** -0.5, 0.25)
    step_bias = jnp.clip(jax.random.uniform(splits[6], (2 * HEADS,), jnp.float32, -2.0, 0.5), -2.0, 0.5)
    across_rate = jnp.clip(jnp.exp(jax.random.uniform(splits[7], (HEADS,), jnp.float32, math.log(0.03125), math.log(0.3))), 0.03125, 0.3)
    down_rate = jnp.clip(jnp.exp(jax.random.uniform(splits[8], (HEADS,), jnp.float32, math.log(0.015625), math.log(0.3))), 0.015625, 0.3)
    skip_gain = jnp.clip(jax.random.uniform(splits[9], (HEADS,), jnp.float32, 0.5, 1.5), 0.5, 1.5)
    norm_gain = jnp.clip(1.0 + 0.18 * jax.random.normal(splits[10], (INNER,), jnp.float32), 0.1, 1.9)
    out_weight = gaussian(splits[11], (INNER, D), INNER ** -0.5, 0.25)
    return dict(tokens=tokens, top_state=top_state, in_weight=in_weight, conv_weight=conv_weight, bc_weight=bc_weight, step_weight=step_weight, step_bias=step_bias, across_rate=across_rate, down_rate=down_rate, skip_gain=skip_gain, norm_gain=norm_gain, out_weight=out_weight)


def sweep(decay, steps, values, b_in, c_in, start):

    def advance(state, items):
        rate, size, entry, b_row, c_row = items
        state = rate[..., None, None] * state + (size[..., None] * entry)[..., None] * b_row[:, None, None, :]
        emitted = jnp.einsum('akpn,an->akp', state, c_row, precision=lax.Precision.HIGHEST)
        return (state, emitted)
    final, emitted = lax.scan(advance, start, (decay, steps, values, b_in, c_in))
    return emitted

def reference(tokens, top_state, in_weight, conv_weight, bc_weight, step_weight, step_bias, across_rate, down_rate, skip_gain, norm_gain, out_weight):
    height = tokens.shape[0]
    width = tokens.shape[1]
    projected = jnp.dot(tokens.reshape(-1, D), in_weight, preferred_element_type=jnp.float32).reshape(height, width, 2 * INNER)
    mixer_in = projected[..., :INNER].astype(jnp.bfloat16)
    gate_in = projected[..., INNER:].astype(jnp.bfloat16)
    padded = jnp.pad(mixer_in.astype(jnp.float32), ((1, 1), (1, 1), (0, 0)))
    summed = jnp.zeros((height, width, INNER), jnp.float32)
    for row_off in range(3):
        for col_off in range(3):
            summed = summed + conv_weight[3 * row_off + col_off] * padded[row_off:row_off + height, col_off:col_off + width]
    values_low = jax.nn.silu(summed).astype(jnp.bfloat16)
    flat = values_low.reshape(-1, INNER)
    maps = jnp.dot(flat, bc_weight, preferred_element_type=jnp.float32).reshape(height, width, 4 * STATE)
    steps = jax.nn.softplus(jnp.dot(flat, step_weight, preferred_element_type=jnp.float32) + step_bias).reshape(height, width, 2 * HEADS)
    values = values_low.astype(jnp.float32).reshape(height, width, HEADS, HEAD_DIM)
    step_across = steps[..., :HEADS]
    step_down = steps[..., HEADS:]
    decay_across = jnp.exp(-step_across * across_rate)
    decay_down = jnp.exp(-step_down * down_rate)
    b_across = maps[..., :STATE]
    c_across = maps[..., STATE:2 * STATE]
    b_down = maps[..., 2 * STATE:3 * STATE]
    c_down = maps[..., 3 * STATE:]
    moved = [jnp.moveaxis(item, 1, 0) for item in (decay_across, step_across, values, b_across, c_across)]
    start_across = jnp.zeros((height, HEADS, HEAD_DIM, STATE), jnp.float32)
    y_across = jnp.moveaxis(sweep(moved[0], moved[1], moved[2], moved[3], moved[4], start_across), 0, 1)
    start_down = top_state.astype(jnp.float32).reshape(width, HEADS, HEAD_DIM, STATE)
    y_down = sweep(decay_down, step_down, values, b_down, c_down, start_down)
    mixed = y_across + y_down + skip_gain[:, None] * values
    gated = mixed.reshape(height, width, INNER) * jax.nn.silu(gate_in.astype(jnp.float32))
    scale = lax.rsqrt(lax.optimization_barrier(jnp.mean(gated * gated, axis=-1, keepdims=True)) + 1e-05)
    normed = (gated * scale * norm_gain).astype(jnp.bfloat16)
    result = jnp.dot(normed.reshape(-1, INNER), out_weight, preferred_element_type=jnp.float32)
    return result.astype(jnp.bfloat16).reshape(height, width, D)
```

```python
import functools

import jax
import jax.numpy as jnp
from jax import lax
from jax.experimental import pallas as pl
from jax.experimental.pallas import tpu as pltpu
from jax.sharding import PartitionSpec as P

F32 = jnp.float32
BF16 = jnp.bfloat16
NEIGHBOURS = ((-1, 0), (1, 0), (0, -1), (0, 1), (-1, -1), (-1, 1), (1, -1), (1, 1))
OPPOSITE = (1, 0, 3, 2, 7, 6, 5, 4)
STRIP = 16
LANES = 128


def dot(a, b):
    return jnp.dot(a, b, preferred_element_type=F32)


def dot_nt(a, b):
    return lax.dot_general(a, b, (((1,), (1,)), ((), ())), preferred_element_type=F32)


def split_dot(mask, x):
    high = x.astype(BF16)
    rest = x - high.astype(F32)
    middle = rest.astype(BF16)
    low = (rest - middle.astype(F32)).astype(BF16)
    return dot(mask, high) + dot(mask, middle) + dot(mask, low)


def split_sum(x, mask):
    high = x.astype(BF16)
    rest = x - high.astype(F32)
    middle = rest.astype(BF16)
    low = (rest - middle.astype(F32)).astype(BF16)
    return dot(high, mask) + dot(middle, mask) + dot(low, mask)


def expand(x, spread):
    high = x.astype(BF16)
    low = (x - high.astype(F32)).astype(BF16)
    return dot(high, spread) + dot(low, spread)


def softplus(x):
    return jnp.maximum(x, 0.0) + jnp.log1p(jnp.exp(-jnp.abs(x)))


def silu(x):
    return x / (1.0 + jnp.exp(-x))


def kernel(
    nr, nc, R, C, heads,
    tok_h, top_h, win_h, wbc_h, wout_h, conv_h, wst_h, bias_h, rate_a_h, rate_d_h, skip_h, gain_h, out,
    conv, wst_t, step_bias, rate_a, rate_d, skip, gain,
    tok, top, win, wbc, wout, wst, param, edge, halo, halo_f, pad, gate, vals, rva, rvd, acc, weighted, y_ref,
    ld_sem, sm_sem, hs_sem, hr_sem, as_sem, ar_sem, ds_sem, dr_sem,
):
    count = R * C
    inner = wout.shape[0]
    state = wbc.shape[1] // 4
    width = inner // heads
    i = lax.axis_index("rows")
    j = lax.axis_index("cols")
    mesh = pl.DeviceIdType.MESH

    def exists(k):
        di, dj = NEIGHBOURS[k]
        a, b = i + di, j + dj
        return (a >= 0) & (a < nr) & (b >= 0) & (b < nc)

    def target(k):
        di, dj = NEIGHBOURS[k]
        return {"rows": i + di, "cols": j + dj}

    loads = [
        pltpu.make_async_copy(a, b, ld_sem.at[n])
        for n, (a, b) in enumerate(
            ((tok_h, tok), (win_h, win), (wbc_h, wbc), (top_h, top), (wout_h, wout))
        )
    ]
    small = [
        pltpu.make_async_copy(a, b, sm_sem.at[n])
        for n, (a, b) in enumerate(
            (
                (wst_h, wst_t), (bias_h, step_bias), (rate_a_h, rate_a), (rate_d_h, rate_d),
                (skip_h, skip), (conv_h, conv), (gain_h, gain),
            )
        )
    ]
    loads[0].start()
    loads[1].start()
    for load in small:
        load.start()
    for load in loads[2:]:
        load.start()

    barrier = pltpu.get_barrier_semaphore()
    for d in range(1, nc):
        pl.semaphore_signal(
            barrier, inc=1, device_id={"cols": lax.rem(j + d, nc)}, device_id_type=mesh
        )
    for d in range(1, nr):
        pl.semaphore_signal(
            barrier, inc=1, device_id={"rows": lax.rem(i + d, nr)}, device_id_type=mesh
        )
    for k in range(4, 8):
        @pl.when(exists(k))
        def _(k=k):
            pl.semaphore_signal(barrier, inc=1, device_id=target(k), device_id_type=mesh)

    pos = lax.broadcasted_iota(jnp.int32, (2 * R, count), 0)
    src = lax.broadcasted_iota(jnp.int32, (2 * R, count), 1)
    wanted = jnp.where(pos < R, pos * C, (pos - R) * C + C - 1)
    wst[...] = jnp.zeros_like(wst)
    param[...] = jnp.zeros_like(param)
    loads[0].wait()
    edge[...] = dot((src == wanted).astype(F32).astype(BF16), tok[...]).astype(BF16)
    for load in small[:5]:
        load.wait()
    wst[pl.ds(0, 2 * heads), :] = wst_t[...]
    param[0:1, 0 : 2 * heads] = step_bias[...]
    param[1:2, 0:heads] = rate_a[...]
    param[1:2, heads : 2 * heads] = rate_d[...]
    param[2:3, 0:heads] = skip[...]
    corners = sum(jnp.where(exists(k), 1, 0) for k in range(4, 8))
    pl.semaphore_wait(barrier, nc - 1 + nr - 1 + corners)

    def halo_copy(k):
        di, dj = NEIGHBOURS[k]
        if di < 0:
            piece = tok.at[pl.ds(0, STRIP)]
        elif di > 0:
            piece = tok.at[pl.ds(count - STRIP, STRIP)]
        else:
            piece = edge.at[pl.ds(0 if dj < 0 else R, STRIP)]
        return pltpu.make_async_remote_copy(
            src_ref=piece,
            dst_ref=halo.at[pl.ds(OPPOSITE[k] * STRIP, STRIP)],
            send_sem=hs_sem.at[k],
            recv_sem=hr_sem.at[OPPOSITE[k]],
            device_id=target(k),
            device_id_type=mesh,
        )

    for k in range(8):
        @pl.when(exists(k))
        def _(k=k):
            halo_copy(k).start()

        @pl.when(jnp.logical_not(exists(k)))
        def _(k=k):
            halo[pl.ds(k * STRIP, STRIP)] = jnp.zeros((STRIP, halo.shape[1]), BF16)

    loads[1].wait()
    projected = dot(tok[...], win[...])
    gate[...] = silu(projected[:, inner:].astype(BF16).astype(F32))
    mixer = projected[:, :inner].astype(BF16).astype(F32)
    pad[pl.ds(1, R), pl.ds(8, C), :] = mixer.reshape(R, C, inner)

    for k in range(8):
        @pl.when(exists(k))
        def _(k=k):
            pltpu.make_async_remote_copy(
                src_ref=edge.at[pl.ds(0, STRIP)],
                dst_ref=halo.at[pl.ds(k * STRIP, STRIP)],
                send_sem=hs_sem.at[k],
                recv_sem=hr_sem.at[k],
                device_id=target(k),
                device_id_type=mesh,
            ).wait_recv()

    halo_f[...] = dot(halo[...], win[:, :inner]).astype(BF16).astype(F32)

    def halo_rows(k, first, n):
        return halo_f[pl.ds(k * STRIP + first, n), :]

    pad[0, pl.ds(8, C), :] = halo_rows(0, STRIP - C, C)
    pad[R + 1, pl.ds(8, C), :] = halo_rows(1, 0, C)
    for r in range(R):
        pad[1 + r, pl.ds(7, 1), :] = halo_rows(2, r, 1)
        pad[1 + r, pl.ds(8 + C, 1), :] = halo_rows(3, r, 1)
    pad[0, pl.ds(7, 1), :] = halo_rows(4, STRIP - 1, 1)
    pad[0, pl.ds(8 + C, 1), :] = halo_rows(5, STRIP - C, 1)
    pad[R + 1, pl.ds(7, 1), :] = halo_rows(6, C - 1, 1)
    pad[R + 1, pl.ds(8 + C, 1), :] = halo_rows(7, 0, 1)

    small[5].wait()
    small[6].wait()
    summed = jnp.zeros((R, C, inner), F32)
    for b in range(3):
        moved = pad[:, pl.ds(7 + b, C), :]
        for a in range(3):
            tap = conv[pl.ds(3 * a + b, 1), :].reshape(1, 1, inner)
            summed = summed + tap * moved[a : a + R]
    values_f = silu(summed).reshape(count, inner).astype(BF16).astype(F32)
    vals[...] = values_f.astype(BF16)

    def send_a(d):
        return pltpu.make_async_remote_copy(
            src_ref=vals,
            dst_ref=rva.at[j],
            send_sem=as_sem.at[d],
            recv_sem=ar_sem.at[j],
            device_id={"cols": j + d},
            device_id_type=mesh,
        )

    relay = nc >= 4

    def sends_a(d):
        direct = j + d < nc
        return direct & (j != nc - 3) if relay and d == 2 else direct

    def arrival_a(slot):
        return pltpu.make_async_remote_copy(
            src_ref=vals, dst_ref=rva.at[slot], send_sem=as_sem.at[0],
            recv_sem=ar_sem.at[slot], device_id={"cols": slot}, device_id_type=mesh,
        )

    def relayed():
        return pltpu.make_async_remote_copy(
            src_ref=rva.at[nc - 3], dst_ref=rva.at[nc - 3], send_sem=as_sem.at[0],
            recv_sem=ar_sem.at[nc - 3], device_id={"cols": j + 1}, device_id_type=mesh,
        )

    def send_d(d):
        return pltpu.make_async_remote_copy(
            src_ref=vals,
            dst_ref=rvd.at[i],
            send_sem=ds_sem.at[d],
            recv_sem=dr_sem.at[i],
            device_id={"rows": i + d},
            device_id_type=mesh,
        )

    for d in range(1, max(nc, nr)):
        if d < nc:
            if d == 1:
                @pl.when(sends_a(d))
                def _(d=d):
                    send_a(d).start()
        if d == 1:
            @pl.when(i + d < nr)
            def _(d=d):
                send_d(d).start()

    q = lax.broadcasted_iota(jnp.int32, (count, count), 0)
    k_ = lax.broadcasted_iota(jnp.int32, (count, count), 1)
    same_row = lax.div(q, C) == lax.div(k_, C)
    same_col = lax.rem(q, C) == lax.rem(k_, C)
    upto = k_ <= q
    after = k_ > q

    def as_mask(m):
        return jnp.where(m, 1.0, 0.0).astype(BF16)

    lane = lax.broadcasted_iota(jnp.int32, (count, LANES), 1)
    spot = lax.broadcasted_iota(jnp.int32, (LANES, inner), 0)
    head = lax.div(lax.broadcasted_iota(jnp.int32, (LANES, inner), 1), width)
    spread_a = as_mask(spot == head)
    spread_d = as_mask(spot == head + heads)
    bias = param[0:1, :]
    rate = param[1:2, :]

    loads[2].wait()
    maps = dot(vals[...], wbc[...])
    steps = softplus(dot_nt(vals[...], wst[...]) + bias)
    log_decay = -steps * rate
    cum_a = split_dot(as_mask(same_row & upto), log_decay)
    cum_d = split_dot(as_mask(same_col & upto), log_decay)
    map_a = maps[:, : 2 * state]
    map_d = maps[:, 2 * state : 4 * state]
    c_a = jnp.where(lane < state, pltpu.roll(map_a, state, 1), 0.0).astype(BF16)
    c_d = jnp.where(lane < state, pltpu.roll(map_d, state, 1), 0.0).astype(BF16)
    score_a = jnp.where(same_row & upto, dot_nt(c_a, map_a.astype(BF16)), 0.0)
    score_d = jnp.where(same_col & upto, dot_nt(c_d, map_d.astype(BF16)), 0.0)
    weighted[pl.ds(0, count), :] = (values_f * expand(steps, spread_a)).astype(BF16)
    weighted[pl.ds(count, count), :] = (values_f * expand(steps, spread_d)).astype(BF16)
    cum_at = cum_a.T
    cum_dt = cum_d.T
    per_group = LANES // width
    for g in range(inner // LANES):
        total = jnp.zeros((count, LANES), F32)
        for e in range(per_group):
            h = g * per_group + e
            diff_a = cum_a[:, h : h + 1] - cum_at[h : h + 1, :]
            hd = heads + h
            diff_d = cum_d[:, hd : hd + 1] - cum_dt[hd : hd + 1, :]
            mix_a = (jnp.exp(jnp.minimum(diff_a, 0.0)) * score_a).astype(BF16)
            mix_d = (jnp.exp(jnp.minimum(diff_d, 0.0)) * score_d).astype(BF16)
            mix = jnp.concatenate([mix_a, mix_d], axis=1)
            part = dot(mix, weighted[:, g * LANES : (g + 1) * LANES])
            total = jnp.where(lax.div(lane, width) == e, part, total)
        y_ref[:, g * LANES : (g + 1) * LANES] = total

    for d in range(nc - 1, 1, -1):
        @pl.when(sends_a(d))
        def _(d=d):
            send_a(d).start()

    for d in range(nr - 1, 1, -1):
        @pl.when(i + d < nr)
        def _(d=d):
            send_d(d).start()

    if relay:
        @pl.when(j == nc - 2)
        def _():
            arrival_a(nc - 3).wait_recv()
            relayed().start()

    loads[3].wait()
    column = lax.rem(q, C)
    c_high = pltpu.roll(c_d.astype(F32), state, 1)
    pairs = width * state // LANES
    halves = []
    for c_half in (c_d.astype(F32), c_high):
        half = jnp.zeros((count, pairs * heads), F32)
        for c in range(C):
            rows = jnp.where(column == c, c_half, 0.0).astype(BF16)
            block = jnp.concatenate(
                [top[c, :, n * LANES : (n + 1) * LANES] for n in range(pairs)], axis=0
            )
            half = half + dot_nt(rows, block)
        halves.append(half)
    lane_from = lax.broadcasted_iota(jnp.int32, (inner, inner), 0)
    lane_to = lax.broadcasted_iota(jnp.int32, (inner, inner), 1)
    half_size = pairs * heads
    parity = lax.div(lane_from, half_size)
    pair = lax.div(lax.rem(lane_from, half_size), heads)
    moves = as_mask(lax.rem(lane_from, heads) * width + 2 * pair + parity == lane_to)
    from_top = expand(jnp.concatenate(halves, axis=1), moves)

    def remote(buffer, slot, c_map, first, same, spread, gap):
        block = buffer[slot]
        m = dot(block, wbc[:, first : first + 2 * state]).astype(BF16)
        s = softplus(dot_nt(block, wst[...]) + bias)
        ld = -s * rate
        tail = split_dot(as_mask(same & after), ld)
        whole = split_dot(as_mask(same), ld)
        weight = s * jnp.exp(tail + gap)
        entry = (block.astype(F32) * expand(weight, spread)).astype(BF16)
        score = jnp.where(same, dot_nt(c_map, m), 0.0).astype(BF16)
        acc[...] += dot(score, entry)
        return gap + whole

    acc[...] = jnp.zeros_like(acc)

    def hop_d(t, gap):
        slot = i - 1 - t
        pltpu.make_async_remote_copy(
            src_ref=vals, dst_ref=rvd.at[slot], send_sem=ds_sem.at[0],
            recv_sem=dr_sem.at[slot], device_id={"rows": slot}, device_id_type=mesh,
        ).wait_recv()
        return remote(rvd, slot, c_d, 2 * state, same_col, spread_d, gap)

    gap_d = lax.fori_loop(0, i, hop_d, jnp.zeros((count, LANES), F32))
    y_ref[...] += (
        expand(jnp.exp(cum_d), spread_d) * acc[...]
        + expand(jnp.exp(cum_d + gap_d), spread_d) * from_top
        + split_sum(param[0:8, :], spread_a)[2:3, :] * vals[...].astype(F32)
    )
    acc[...] = jnp.zeros_like(acc)

    def hop_a(t, gap):
        slot = j - 1 - t
        waits = (j != nc - 2) | (slot != nc - 3) if relay else slot >= 0

        @pl.when(waits)
        def _():
            arrival_a(slot).wait_recv()

        return remote(rva, slot, c_a, 0, same_row, spread_a, gap)

    lax.fori_loop(0, j, hop_a, jnp.zeros((count, LANES), F32))
    y = y_ref[...] + expand(jnp.exp(cum_a), spread_a) * acc[...]
    gated = y * gate[...]
    scale = lax.rsqrt(jnp.mean(gated * gated, axis=-1, keepdims=True) + 1e-05)
    normed = (gated * scale * gain[...]).astype(BF16)
    loads[4].wait()
    out[...] = dot(normed, wout[...]).astype(BF16)

    if relay:
        @pl.when(j == nc - 2)
        def _():
            relayed().wait_send()
    for k in range(8):
        @pl.when(exists(k))
        def _(k=k):
            halo_copy(k).wait_send()
    for d in range(1, nc):
        @pl.when(sends_a(d))
        def _(d=d):
            send_a(d).wait_send()
    for d in range(1, nr):
        @pl.when(i + d < nr)
        def _(d=d):
            send_d(d).wait_send()


def shards(
    nr, nc,
    tokens, top_state, in_weight, conv_weight, bc_weight, step_weight, step_bias,
    across_rate, down_rate, skip_gain, norm_gain, out_weight,
):
    R, C, model = tokens.shape
    inner = out_weight.shape[0]
    heads = across_rate.shape[0]
    count = R * C
    vmem = pl.BlockSpec(memory_space=pltpu.VMEM)
    result = pl.pallas_call(
        functools.partial(kernel, nr, nc, R, C, heads),
        out_shape=jax.ShapeDtypeStruct((count, model), BF16),
        in_specs=[pl.BlockSpec(memory_space=pltpu.HBM)] * 12,
        out_specs=vmem,
        scratch_shapes=[
            pltpu.VMEM(conv_weight.shape, F32),
            pltpu.VMEM((2 * heads, inner), BF16),
            pltpu.VMEM((1, 2 * heads), F32),
            pltpu.VMEM((1, heads), F32),
            pltpu.VMEM((1, heads), F32),
            pltpu.VMEM((1, heads), F32),
            pltpu.VMEM((1, inner), F32),
            pltpu.VMEM((count, model), BF16),
            pltpu.VMEM(top_state.shape, BF16),
            pltpu.VMEM(in_weight.shape, BF16),
            pltpu.VMEM(bc_weight.shape, BF16),
            pltpu.VMEM(out_weight.shape, BF16),
            pltpu.VMEM((LANES, inner), BF16),
            pltpu.VMEM((8, LANES), F32),
            pltpu.VMEM((2 * R, model), BF16),
            pltpu.VMEM((8 * STRIP, model), BF16),
            pltpu.VMEM((8 * STRIP, inner), F32),
            pltpu.VMEM((R + 2, 24, inner), F32),
            pltpu.VMEM((count, inner), F32),
            pltpu.VMEM((count, inner), BF16),
            pltpu.VMEM((nc, count, inner), BF16),
            pltpu.VMEM((nr, count, inner), BF16),
            pltpu.VMEM((count, inner), F32),
            pltpu.VMEM((2 * count, inner), BF16),
            pltpu.VMEM((count, inner), F32),
            pltpu.SemaphoreType.DMA((5,)),
            pltpu.SemaphoreType.DMA((7,)),
            pltpu.SemaphoreType.DMA((8,)),
            pltpu.SemaphoreType.DMA((8,)),
            pltpu.SemaphoreType.DMA((nc,)),
            pltpu.SemaphoreType.DMA((nc,)),
            pltpu.SemaphoreType.DMA((nr,)),
            pltpu.SemaphoreType.DMA((nr,)),
        ],
        compiler_params=pltpu.CompilerParams(
            collective_id=0, has_side_effects=True, vmem_limit_bytes=48000 * 1024
        ),
    )(
        *(
            pltpu.with_memory_space_constraint(x, pltpu.HBM)
            for x in (
                tokens.reshape(count, model),
                top_state,
                in_weight,
                bc_weight,
                out_weight,
                conv_weight,
                step_weight.T,
                step_bias[None],
                across_rate[None],
                down_rate[None],
                skip_gain[None],
                norm_gain[None],
            )
        )
    )
    return result.reshape(R, C, model)


def solution(mesh):
    in_specs = (
        P(("groups", "rows"), "cols", None),
        P(("groups", "cols"), None, None),
    ) + (P(),) * 10
    out_specs = P(("groups", "rows"), "cols", None)
    return jax.shard_map(
        functools.partial(shards, mesh.shape["rows"], mesh.shape["cols"]),
        mesh=mesh, in_specs=in_specs, out_specs=out_specs, check_vma=False,
    )
```

```python
import functools

import jax
import jax.numpy as jnp
from jax import lax
from jax.experimental import pallas as pl
from jax.experimental.pallas import tpu as pltpu
from jax.sharding import PartitionSpec as P

F32 = jnp.float32
BF16 = jnp.bfloat16
NEIGHBOURS = ((-1, 0), (1, 0), (0, -1), (0, 1), (-1, -1), (-1, 1), (1, -1), (1, 1))
OPPOSITE = (1, 0, 3, 2, 7, 6, 5, 4)
STRIP = 16
LANES = 128


def dot(a, b):
    return jnp.dot(a, b, preferred_element_type=F32)


def dot_nt(a, b):
    return lax.dot_general(a, b, (((1,), (1,)), ((), ())), preferred_element_type=F32)


def softplus(x):
    return jnp.maximum(x, 0.0) + jnp.log1p(jnp.exp(-jnp.abs(x)))


def silu(x):
    return x / (1.0 + jnp.exp(-x))


def kernel(
    nr, nc, R, C, heads,
    tok_h, top_h, win_h, wbc_h, wout_h, conv_h, wst_h, bias_h, rate_a_h, rate_d_h, skip_h, gain_h, out,
    conv, wst_t, step_bias, rate_a, rate_d, skip, gain,
    tok, top, win, wbc, wout, wall, param, edge, halo, halo_f, pad, gate, vals, rva, rvd, acc_a, acc_d,
    weighted, y_ref, masks, same_f, upto_f, spread_r, moves_r, top_r, grow_a, grow_d, exit_y, exit_d,
    cbuf, ysend, yrecv,
    ld_sem, sm_sem, hs_sem, hr_sem, as_sem, ar_sem, ds_sem, dr_sem, rl_sem, q_sem, far_sem,
):
    count = R * C
    inner = wout.shape[0]
    state = wbc.shape[1] // 4
    width = inner // heads
    group = 2 * heads
    penult, last = nc - 2, nc - 1
    i = lax.axis_index("rows")
    j = lax.axis_index("cols")
    mesh = pl.DeviceIdType.MESH

    def exists(k):
        di, dj = NEIGHBOURS[k]
        a, b = i + di, j + dj
        return (a >= 0) & (a < nr) & (b >= 0) & (b < nc)

    def target(k):
        di, dj = NEIGHBOURS[k]
        return {"rows": i + di, "cols": j + dj}

    loads = [
        pltpu.make_async_copy(a, b, ld_sem.at[n])
        for n, (a, b) in enumerate(
            ((tok_h, tok), (win_h, win), (wbc_h, wbc), (top_h, top), (wout_h, wout))
        )
    ]
    small = [
        pltpu.make_async_copy(a, b, sm_sem.at[n])
        for n, (a, b) in enumerate(
            (
                (wst_h, wst_t), (bias_h, step_bias), (rate_a_h, rate_a), (rate_d_h, rate_d),
                (skip_h, skip), (conv_h, conv), (gain_h, gain),
            )
        )
    ]
    loads[0].start()
    loads[1].start()
    for load in small:
        load.start()
    for load in loads[2:]:
        load.start()

    barrier = pltpu.get_barrier_semaphore()
    for d in range(1, nr):
        pl.semaphore_signal(
            barrier, inc=1, device_id={"rows": lax.rem(i + d, nr)}, device_id_type=mesh
        )
    for k in range(2, 8):
        @pl.when(exists(k))
        def _(k=k):
            pl.semaphore_signal(barrier, inc=1, device_id=target(k), device_id_type=mesh)

    def as_mask(m):
        return jnp.where(m, 1.0, 0.0).astype(BF16)

    pos = lax.broadcasted_iota(jnp.int32, (2 * R, count), 0)
    src = lax.broadcasted_iota(jnp.int32, (2 * R, count), 1)
    wanted = jnp.where(pos < R, pos * C, (pos - R) * C + C - 1)
    param[...] = jnp.zeros_like(param)
    loads[0].wait()
    edge[...] = dot(as_mask(src == wanted), tok[...]).astype(BF16)
    around = sum(jnp.where(exists(k), 1, 0) for k in range(2, 8))
    pl.semaphore_wait(barrier, nr - 1 + around)

    def halo_copy(k):
        di, dj = NEIGHBOURS[k]
        if di < 0:
            piece = tok.at[pl.ds(0, STRIP)]
        elif di > 0:
            piece = tok.at[pl.ds(count - STRIP, STRIP)]
        else:
            piece = edge.at[pl.ds(0 if dj < 0 else R, STRIP)]
        return pltpu.make_async_remote_copy(
            src_ref=piece,
            dst_ref=halo.at[pl.ds(OPPOSITE[k] * STRIP, STRIP)],
            send_sem=hs_sem.at[k],
            recv_sem=hr_sem.at[OPPOSITE[k]],
            device_id=target(k),
            device_id_type=mesh,
        )

    for k in range(8):
        @pl.when(exists(k))
        def _(k=k):
            halo_copy(k).start()

        @pl.when(jnp.logical_not(exists(k)))
        def _(k=k):
            halo[pl.ds(k * STRIP, STRIP)] = jnp.zeros((STRIP, halo.shape[1]), BF16)

    def tell_left(amount):
        pl.semaphore_signal(far_sem, inc=amount, device_id={"cols": j - 1}, device_id_type=mesh)

    @pl.when((j >= 1) & (j + 1 <= penult))
    def _():
        tell_left(1)

    loads[1].wait()
    projected = dot(tok[...], win[...])
    gate[...] = silu(projected[:, inner:].astype(BF16).astype(F32))
    mixer = projected[:, :inner].astype(BF16).astype(F32)
    pad[pl.ds(1, R), pl.ds(8, C), :] = mixer.reshape(R, C, inner)

    for load in small[:5]:
        load.wait()
    for g in range(LANES // group):
        param[0:1, g * group : (g + 1) * group] = step_bias[...]
        param[1:2, g * group : g * group + heads] = rate_a[...]
        param[1:2, g * group + heads : (g + 1) * group] = rate_d[...]
    param[2:3, 0:heads] = skip[...]
    bias = param[0:1, :]
    rate = param[1:2, :]
    loads[2].wait()
    wall[:, 0:LANES] = wbc[:, 0:LANES]
    wall[:, LANES : 2 * LANES] = jnp.concatenate([wst_t[...]] * (LANES // group), axis=0).astype(F32).T.astype(BF16)
    wall[:, 2 * LANES : 3 * LANES] = wbc[:, LANES : 2 * LANES]

    q = lax.broadcasted_iota(jnp.int32, (count, count), 0)
    k_ = lax.broadcasted_iota(jnp.int32, (count, count), 1)
    same_row = lax.div(q, C) == lax.div(k_, C)
    same_col = lax.rem(q, C) == lax.rem(k_, C)
    for n, same in enumerate((same_row, same_col)):
        masks[n, pl.ds(0, count), :] = as_mask(same & (k_ <= q))
        masks[n, pl.ds(count, count), :] = as_mask(same & (k_ > q))
        masks[n, pl.ds(2 * count, count), :] = as_mask(same)
        same_f[n] = jnp.where(same, 1.0, 0.0)
        upto_f[n] = jnp.where(same & (k_ <= q), 1.0, 0.0)
    spot = lax.broadcasted_iota(jnp.int32, (LANES, inner), 0)
    head = lax.div(lax.broadcasted_iota(jnp.int32, (LANES, inner), 1), width)
    for n in range(2):
        row = head + n * heads
        spread_r[n] = as_mask((spot == row) | (spot == row + group))
    lane_from = lax.broadcasted_iota(jnp.int32, (inner, inner), 0)
    lane_to = lax.broadcasted_iota(jnp.int32, (inner, inner), 1)
    pairs = width * state // LANES
    half_size = pairs * heads
    parity = lax.div(lane_from, half_size)
    pair = lax.div(lax.rem(lane_from, half_size), heads)
    moves_r[...] = as_mask(lax.rem(lane_from, heads) * width + 2 * pair + parity == lane_to)
    loads[3].wait()
    for c in range(C):
        for n in range(pairs):
            top_r[pl.ds(n * heads, heads), c * LANES : (c + 1) * LANES] = top[c, :, n * LANES : (n + 1) * LANES]

    lane = lax.broadcasted_iota(jnp.int32, (count, LANES), 1)
    low_lanes = lax.rem(lax.div(lane, group), 2) == 1

    def halves_of(x):
        return jnp.where(low_lanes, x - x.astype(BF16).astype(F32), x).astype(BF16)

    def masked_sum(mask, x):
        r = dot(mask, x)
        return r + pltpu.roll(r, group, 1)

    for k in range(8):
        @pl.when(exists(k))
        def _(k=k):
            pltpu.make_async_remote_copy(
                src_ref=edge.at[pl.ds(0, STRIP)],
                dst_ref=halo.at[pl.ds(k * STRIP, STRIP)],
                send_sem=hs_sem.at[k],
                recv_sem=hr_sem.at[k],
                device_id=target(k),
                device_id_type=mesh,
            ).wait_recv()

    halo_f[...] = dot(halo[...], win[:, :inner]).astype(BF16).astype(F32)

    def halo_rows(k, first, n):
        return halo_f[pl.ds(k * STRIP + first, n), :]

    pad[0, pl.ds(8, C), :] = halo_rows(0, STRIP - C, C)
    pad[R + 1, pl.ds(8, C), :] = halo_rows(1, 0, C)
    for r in range(R):
        pad[1 + r, pl.ds(7, 1), :] = halo_rows(2, r, 1)
        pad[1 + r, pl.ds(8 + C, 1), :] = halo_rows(3, r, 1)
    pad[0, pl.ds(7, 1), :] = halo_rows(4, STRIP - 1, 1)
    pad[0, pl.ds(8 + C, 1), :] = halo_rows(5, STRIP - C, 1)
    pad[R + 1, pl.ds(7, 1), :] = halo_rows(6, C - 1, 1)
    pad[R + 1, pl.ds(8 + C, 1), :] = halo_rows(7, 0, 1)

    small[5].wait()
    small[6].wait()
    summed = jnp.zeros((R, C, inner), F32)
    for b in range(3):
        moved = pad[:, pl.ds(7 + b, C), :]
        for a in range(3):
            tap = conv[pl.ds(3 * a + b, 1), :].reshape(1, 1, inner)
            summed = summed + tap * moved[a : a + R]
    values_f = silu(summed).reshape(count, inner).astype(BF16).astype(F32)
    vals[...] = values_f.astype(BF16)

    def send_a(d):
        return pltpu.make_async_remote_copy(
            src_ref=vals, dst_ref=rva.at[j], send_sem=as_sem.at[d], recv_sem=ar_sem.at[j],
            device_id={"cols": j + d}, device_id_type=mesh,
        )

    def arrival_a(slot):
        return pltpu.make_async_remote_copy(
            src_ref=vals, dst_ref=rva.at[slot], send_sem=as_sem.at[0],
            recv_sem=ar_sem.at[slot], device_id={"cols": slot}, device_id_type=mesh,
        )

    def send_d(d):
        return pltpu.make_async_remote_copy(
            src_ref=vals, dst_ref=rvd.at[i], send_sem=ds_sem.at[d], recv_sem=dr_sem.at[i],
            device_id={"rows": i + d}, device_id_type=mesh,
        )

    def sends_d(d):
        return (i + d < nr) & (lax.rem(i, 2) == 0) if d == 1 else i + d < nr

    hops_d = [1] + list(range(2, nr, 2))
    sibling = i + 1 - 2 * lax.rem(i, 2)

    def relay_d(slot):
        return pltpu.make_async_remote_copy(
            src_ref=rvd.at[slot], dst_ref=rvd.at[slot], send_sem=rl_sem.at[slot],
            recv_sem=dr_sem.at[slot], device_id={"rows": sibling}, device_id_type=mesh,
        )

    def arrival_d(slot):
        return pltpu.make_async_remote_copy(
            src_ref=vals, dst_ref=rvd.at[slot], send_sem=ds_sem.at[0],
            recv_sem=dr_sem.at[slot], device_id={"rows": slot}, device_id_type=mesh,
        )

    query = pltpu.make_async_remote_copy(
        src_ref=cbuf.at[pl.ds(0, count)], dst_ref=cbuf.at[pl.ds(count, count)], send_sem=q_sem.at[0],
        recv_sem=q_sem.at[1], device_id={"cols": j - 1}, device_id_type=mesh,
    )
    answer = pltpu.make_async_remote_copy(
        src_ref=ysend, dst_ref=yrecv, send_sem=q_sem.at[2],
        recv_sem=q_sem.at[3], device_id={"cols": j + 1}, device_id_type=mesh,
    )

    further = max(0, nc - 3)
    for n in range(1, further + 1):
        @pl.when(further - j == n)
        def _(n=n):
            pl.semaphore_wait(far_sem, n)

            @pl.when(j >= 1)
            def _():
                tell_left(n)

    for d in range(nc - 2, 0, -1):
        @pl.when(j + d <= penult)
        def _(d=d):
            send_a(d).start()

    for d in hops_d[1:] + hops_d[:1]:
        @pl.when(sends_d(d))
        def _(d=d):
            send_d(d).start()

    full = dot(vals[...], wall[...])
    map_a = full[:, :LANES]
    map_d = full[:, 2 * LANES :]
    c_a = jnp.where(lane < state, pltpu.roll(map_a, state, 1), 0.0).astype(BF16)
    c_d = jnp.where(lane < state, pltpu.roll(map_d, state, 1), 0.0).astype(BF16)
    cbuf[pl.ds(0, count), :] = c_a

    @pl.when(j == last)
    def _():
        query.start()

    steps = softplus(full[:, LANES : 2 * LANES] + bias)
    log_decay = halves_of(-steps * rate)
    cum_a = masked_sum(masks[0, pl.ds(0, count), :], log_decay)
    cum_d = masked_sum(masks[1, pl.ds(0, count), :], log_decay)
    score_a = dot_nt(c_a, map_a.astype(BF16)) * upto_f[0]
    score_d = dot_nt(c_d, map_d.astype(BF16)) * upto_f[1]
    step_halves = halves_of(steps)
    weighted[pl.ds(0, count), :] = (values_f * dot(step_halves, spread_r[0])).astype(BF16)
    weighted[pl.ds(count, count), :] = (values_f * dot(step_halves, spread_r[1])).astype(BF16)
    cum_at = cum_a.T
    cum_dt = cum_d.T
    per_group = LANES // width
    for g in range(inner // LANES):
        total = jnp.zeros((count, LANES), F32)
        for e in range(per_group):
            h = g * per_group + e
            diff_a = cum_a[:, h : h + 1] - cum_at[h : h + 1, :]
            hd = heads + h
            diff_d = cum_d[:, hd : hd + 1] - cum_dt[hd : hd + 1, :]
            mix_a = (jnp.exp(jnp.minimum(diff_a, 0.0)) * score_a).astype(BF16)
            mix_d = (jnp.exp(jnp.minimum(diff_d, 0.0)) * score_d).astype(BF16)
            mix = jnp.concatenate([mix_a, mix_d], axis=1)
            part = dot(mix, weighted[:, g * LANES : (g + 1) * LANES])
            total = jnp.where(lax.div(lane, width) == e, part, total)
        y_ref[:, g * LANES : (g + 1) * LANES] = total

    column = lax.rem(q, C)
    c_low = c_d.astype(F32)
    c_high = pltpu.roll(c_low, state, 1)
    picked = jnp.concatenate(
        [
            jnp.concatenate([jnp.where(column == c, h, 0.0).astype(BF16) for c in range(C)], axis=1)
            for h in (c_low, c_high)
        ],
        axis=0,
    )
    halves = dot_nt(picked, top_r[...])
    acc_d[...] = dot(
        jnp.concatenate([halves[:count], halves[count:]], axis=1).astype(BF16), moves_r[...]
    )
    grow_a[...] = dot(halves_of(jnp.exp(cum_a)), spread_r[0])
    grow_d[...] = dot(halves_of(jnp.exp(cum_d)), spread_r[1])
    skips = dot(halves_of(jnp.broadcast_to(param[2:3, :], (count, LANES))), spread_r[0])
    y_ref[...] += skips * vals[...].astype(F32)

    def leaving(n, steps, log_decay):
        r = masked_sum(masks[n, pl.ds(count, 2 * count), :], log_decay)
        weight = halves_of(steps * jnp.exp(r[:count]))
        whole = halves_of(jnp.exp(r[count:]))
        return dot(jnp.concatenate([weight, whole], axis=0), spread_r[n])

    def remote(buffer, slot, n, queries, acc):
        block = buffer[slot]
        made = dot(block, wall[:, n * LANES : (n + 2) * LANES])
        m = made[:, n * LANES : (n + 1) * LANES].astype(BF16)
        s = softplus(made[:, (1 - n) * LANES : (2 - n) * LANES] + bias)
        e = leaving(n, s, halves_of(-s * rate))
        entry = (block.astype(F32) * e[:count]).astype(BF16)
        score = dot_nt(queries, m)
        for p in range(queries.shape[0] // count):
            rows = pl.ds(p * count, count)
            part = (score[p * count : (p + 1) * count] * same_f[n]).astype(BF16)
            acc[rows, :] = acc[rows, :] * e[count:] + dot(part, entry)

    acc_a[...] = jnp.zeros_like(acc_a)

    @pl.when(j == penult)
    def _():
        e = leaving(0, steps, log_decay)
        entry = (vals[...].astype(F32) * e[:count]).astype(BF16)
        exit_d[...] = e[count:]
        query.wait_recv()
        score = dot_nt(cbuf[pl.ds(count, count), :], map_a.astype(BF16)) * same_f[0]
        exit_y[...] = dot(score.astype(BF16), entry)

    def pass_on(t, carry):
        slot = lax.rem(i, 2) + 2 * t
        arrival_d(slot).wait_recv()
        relay_d(slot).start()
        return carry

    straight = lax.div(i, 2)
    lax.fori_loop(0, straight, pass_on, 0)

    @pl.when(j == penult)
    def _():
        def hop(slot, carry):
            arrival_a(slot).wait_recv()
            remote(rva, slot, 0, cbuf[...], acc_a)
            return carry

        lax.fori_loop(0, j, hop, 0)
        ysend[...] = (acc_a[pl.ds(count, count), :] * exit_d[...] + exit_y[...]).astype(BF16)
        answer.start()

    def hop_d(slot, carry):
        @pl.when(lax.rem(slot + i, 2) == 1)
        def _():
            arrival_d(slot).wait_recv()

        remote(rvd, slot, 1, c_d, acc_d)
        return carry

    lax.fori_loop(0, i, hop_d, 0)

    @pl.when(j < penult)
    def _():
        def hop(slot, carry):
            arrival_a(slot).wait_recv()
            remote(rva, slot, 0, cbuf[pl.ds(0, count), :], acc_a)
            return carry

        lax.fori_loop(0, j, hop, 0)

    @pl.when(j == last)
    def _():
        answer.wait_recv()
        acc_a[pl.ds(0, count), :] = yrecv[...].astype(F32)

    y = y_ref[...] + grow_a[...] * acc_a[pl.ds(0, count), :] + grow_d[...] * acc_d[...]
    gated = y * gate[...]
    scale = lax.rsqrt(jnp.mean(gated * gated, axis=-1, keepdims=True) + 1e-05)
    normed = (gated * scale * gain[...]).astype(BF16)
    loads[4].wait()
    out[...] = dot(normed, wout[...]).astype(BF16)

    for k in range(8):
        @pl.when(exists(k))
        def _(k=k):
            halo_copy(k).wait_send()
    for d in range(1, nc - 1):
        @pl.when(j + d <= penult)
        def _(d=d):
            send_a(d).wait_send()
    for d in hops_d:
        @pl.when(sends_d(d))
        def _(d=d):
            send_d(d).wait_send()

    def passed_on(t, carry):
        relay_d(lax.rem(i, 2) + 2 * t).wait_send()
        return carry

    lax.fori_loop(0, straight, passed_on, 0)

    @pl.when(j == last)
    def _():
        query.wait_send()

    @pl.when(j == penult)
    def _():
        answer.wait_send()


def shards(
    nr, nc,
    tokens, top_state, in_weight, conv_weight, bc_weight, step_weight, step_bias,
    across_rate, down_rate, skip_gain, norm_gain, out_weight,
):
    R, C, model = tokens.shape
    inner = out_weight.shape[0]
    heads = across_rate.shape[0]
    count = R * C
    vmem = pl.BlockSpec(memory_space=pltpu.VMEM)
    result = pl.pallas_call(
        functools.partial(kernel, nr, nc, R, C, heads),
        out_shape=jax.ShapeDtypeStruct((count, model), BF16),
        in_specs=[pl.BlockSpec(memory_space=pltpu.HBM)] * 12,
        out_specs=vmem,
        scratch_shapes=[
            pltpu.VMEM(conv_weight.shape, F32),
            pltpu.VMEM((2 * heads, inner), BF16),
            pltpu.VMEM((1, 2 * heads), F32),
            pltpu.VMEM((1, heads), F32),
            pltpu.VMEM((1, heads), F32),
            pltpu.VMEM((1, heads), F32),
            pltpu.VMEM((1, inner), F32),
            pltpu.VMEM((count, model), BF16),
            pltpu.VMEM(top_state.shape, BF16),
            pltpu.VMEM(in_weight.shape, BF16),
            pltpu.VMEM(bc_weight.shape, BF16),
            pltpu.VMEM(out_weight.shape, BF16),
            pltpu.VMEM((inner, 3 * LANES), BF16),
            pltpu.VMEM((8, LANES), F32),
            pltpu.VMEM((2 * R, model), BF16),
            pltpu.VMEM((8 * STRIP, model), BF16),
            pltpu.VMEM((8 * STRIP, inner), F32),
            pltpu.VMEM((R + 2, 24, inner), F32),
            pltpu.VMEM((count, inner), F32),
            pltpu.VMEM((count, inner), BF16),
            pltpu.VMEM((nc, count, inner), BF16),
            pltpu.VMEM((nr, count, inner), BF16),
            pltpu.VMEM((2 * count, inner), F32),
            pltpu.VMEM((count, inner), F32),
            pltpu.VMEM((2 * count, inner), BF16),
            pltpu.VMEM((count, inner), F32),
            pltpu.VMEM((2, 3 * count, count), BF16),
            pltpu.VMEM((2, count, count), F32),
            pltpu.VMEM((2, count, count), F32),
            pltpu.VMEM((2, LANES, inner), BF16),
            pltpu.VMEM((inner, inner), BF16),
            pltpu.VMEM((top_state.shape[2] // LANES * heads, C * LANES), BF16),
            pltpu.VMEM((count, inner), F32),
            pltpu.VMEM((count, inner), F32),
            pltpu.VMEM((count, inner), F32),
            pltpu.VMEM((count, inner), F32),
            pltpu.VMEM((2 * count, LANES), BF16),
            pltpu.VMEM((count, inner), BF16),
            pltpu.VMEM((count, inner), BF16),
            pltpu.SemaphoreType.DMA((5,)),
            pltpu.SemaphoreType.DMA((7,)),
            pltpu.SemaphoreType.DMA((8,)),
            pltpu.SemaphoreType.DMA((8,)),
            pltpu.SemaphoreType.DMA((nc,)),
            pltpu.SemaphoreType.DMA((nc,)),
            pltpu.SemaphoreType.DMA((nr,)),
            pltpu.SemaphoreType.DMA((nr,)),
            pltpu.SemaphoreType.DMA((nr,)),
            pltpu.SemaphoreType.DMA((4,)),
            pltpu.SemaphoreType.REGULAR,
        ],
        compiler_params=pltpu.CompilerParams(
            collective_id=0, has_side_effects=True, vmem_limit_bytes=48000 * 1024
        ),
    )(
        *(
            pltpu.with_memory_space_constraint(x, pltpu.HBM)
            for x in (
                tokens.reshape(count, model),
                top_state,
                in_weight,
                bc_weight,
                out_weight,
                conv_weight,
                step_weight.T,
                step_bias[None],
                across_rate[None],
                down_rate[None],
                skip_gain[None],
                norm_gain[None],
            )
        )
    )
    return result.reshape(R, C, model)


def solution(mesh):
    in_specs = (
        P(("groups", "rows"), "cols", None),
        P(("groups", "cols"), None, None),
    ) + (P(),) * 10
    out_specs = P(("groups", "rows"), "cols", None)
    return jax.shard_map(
        functools.partial(shards, mesh.shape["rows"], mesh.shape["cols"]),
        mesh=mesh, in_specs=in_specs, out_specs=out_specs, check_vma=False,
    )
```

```python
import functools

import jax
import jax.numpy as jnp
from jax import lax
from jax.experimental import pallas as pl
from jax.experimental.pallas import tpu as pltpu
from jax.sharding import PartitionSpec as P

F32 = jnp.float32
BF16 = jnp.bfloat16
NEIGHBOURS = ((-1, 0), (1, 0), (0, -1), (0, 1), (-1, -1), (-1, 1), (1, -1), (1, 1))
OPPOSITE = (1, 0, 3, 2, 7, 6, 5, 4)
STRIP = 16
LANES = 128
CHUNKS = 4
BATCH = 3
CORNERS = 4


def dot(a, b):
    return jnp.dot(a, b, preferred_element_type=F32)


def dot_nt(a, b):
    return lax.dot_general(a, b, (((1,), (1,)), ((), ())), preferred_element_type=F32)


def softplus(x):
    return jnp.maximum(x, 0.0) + jnp.log1p(jnp.exp(-jnp.abs(x)))


def silu(x):
    return x / (1.0 + jnp.exp(-x))


def kernel(
    nr, nc, R, C, heads,
    tok_h, top_h, win_h, wbc_h, wout_h, conv_h, wst_h, bias_h, rate_a_h, rate_d_h, skip_h, gain_h, out,
    conv, wst_t, step_bias, rate_a, rate_d, skip, gain,
    tok, top, win, wbc, wout, wall, param, edge, halo, halo_f, pad, gate, vals, rva, rvd, acc_a, acc_d,
    weighted, y_ref, masks, mask_d, mask_a, same_a, same_f, upto_f, spread_r, moves_r, top_r, grow_a, grow_d, exit_y, exit_d,
    cbuf, ysend, yrecv, corner, far_corner,
    ld_sem, sm_sem, hs_sem, hr_sem, as_sem, ar_sem, ds_sem, dr_sem, rl_sem, q_sem, ys_sem, yr_sem, far_sem,
):
    count = R * C
    inner = wout.shape[0]
    state = wbc.shape[1] // 4
    width = inner // heads
    group = 2 * heads
    penult, last = nc - 2, nc - 1
    before = nc - 2
    piece_rows = count // CHUNKS
    i = lax.axis_index("rows")
    j = lax.axis_index("cols")
    mesh = pl.DeviceIdType.MESH

    def exists(k):
        di, dj = NEIGHBOURS[k]
        a, b = i + di, j + dj
        return (a >= 0) & (a < nr) & (b >= 0) & (b < nc)

    def target(k):
        di, dj = NEIGHBOURS[k]
        return {"rows": i + di, "cols": j + dj}

    loads = [
        pltpu.make_async_copy(a, b, ld_sem.at[n])
        for n, (a, b) in enumerate(
            ((tok_h, tok), (win_h, win), (wbc_h, wbc), (top_h, top), (wout_h, wout))
        )
    ]
    small = [
        pltpu.make_async_copy(a, b, sm_sem.at[n])
        for n, (a, b) in enumerate(
            (
                (wst_h, wst_t), (bias_h, step_bias), (rate_a_h, rate_a), (rate_d_h, rate_d),
                (skip_h, skip), (conv_h, conv), (gain_h, gain),
            )
        )
    ]
    loads[0].start()
    loads[1].start()
    for load in small:
        load.start()
    for load in loads[2:]:
        load.start()

    barrier = pltpu.get_barrier_semaphore()
    for d in range(1, nr):
        pl.semaphore_signal(
            barrier, inc=1, device_id={"rows": lax.rem(i + d, nr)}, device_id_type=mesh
        )
    for k in range(2, 8):
        @pl.when(exists(k))
        def _(k=k):
            pl.semaphore_signal(barrier, inc=1, device_id=target(k), device_id_type=mesh)

    def as_mask(m):
        return jnp.where(m, 1.0, 0.0).astype(BF16)

    pos = lax.broadcasted_iota(jnp.int32, (2 * R, count), 0)
    src = lax.broadcasted_iota(jnp.int32, (2 * R, count), 1)
    wanted = jnp.where(pos < R, pos * C, (pos - R) * C + C - 1)
    param[...] = jnp.zeros_like(param)
    loads[0].wait()
    edge[...] = dot(as_mask(src == wanted), tok[...]).astype(BF16)
    slot_at = lax.broadcasted_iota(jnp.int32, (CORNERS * STRIP, count), 0)
    token_at = lax.broadcasted_iota(jnp.int32, (CORNERS * STRIP, count), 1)
    which = lax.div(slot_at, STRIP)
    at_corner = token_at == lax.div(which, 2) * (count - C) + lax.rem(which, 2) * (C - 1)
    corner[...] = sum(
        dot(as_mask(at_corner & (lax.rem(slot_at, STRIP) == n)), tok[:, n * LANES : (n + 1) * LANES])
        for n in range(tok.shape[1] // LANES)
    ).astype(BF16)
    around = sum(jnp.where(exists(k), 1, 0) for k in range(2, 8))
    pl.semaphore_wait(barrier, nr - 1 + around)

    def halo_copy(k):
        di, dj = NEIGHBOURS[k]
        if k >= CORNERS:
            piece = corner.at[pl.ds((k - CORNERS) * STRIP, STRIP)]
            place = far_corner.at[pl.ds((OPPOSITE[k] - CORNERS) * STRIP, STRIP)]
        else:
            if di < 0:
                piece = tok.at[pl.ds(0, STRIP)]
            elif di > 0:
                piece = tok.at[pl.ds(count - STRIP, STRIP)]
            else:
                piece = edge.at[pl.ds(0 if dj < 0 else R, STRIP)]
            place = halo.at[pl.ds(OPPOSITE[k] * STRIP, STRIP)]
        return pltpu.make_async_remote_copy(
            src_ref=piece,
            dst_ref=place,
            send_sem=hs_sem.at[k],
            recv_sem=hr_sem.at[OPPOSITE[k]],
            device_id=target(k),
            device_id_type=mesh,
        )

    for k in (4, 5, 6, 7, 2, 3, 0, 1):
        @pl.when(exists(k))
        def _(k=k):
            halo_copy(k).start()

    for k in range(8):
        @pl.when(jnp.logical_not(exists(k)))
        def _(k=k):
            if k >= CORNERS:
                far_corner[pl.ds((k - CORNERS) * STRIP, STRIP)] = jnp.zeros((STRIP, LANES), BF16)
            else:
                halo[pl.ds(k * STRIP, STRIP)] = jnp.zeros((STRIP, halo.shape[1]), BF16)

    def tell_left(amount):
        pl.semaphore_signal(far_sem, inc=amount, device_id={"cols": j - 1}, device_id_type=mesh)

    @pl.when((j >= 1) & (j + 1 <= penult))
    def _():
        tell_left(1)

    loads[1].wait()
    projected = dot(tok[...], win[...])
    gate[...] = silu(projected[:, inner:].astype(BF16).astype(F32))
    mixer = projected[:, :inner].astype(BF16).astype(F32)
    pad[pl.ds(1, R), pl.ds(8, C), :] = mixer.reshape(R, C, inner)

    for load in small[:5]:
        load.wait()
    for g in range(LANES // group):
        param[0:1, g * group : (g + 1) * group] = step_bias[...]
        param[1:2, g * group : g * group + heads] = rate_a[...]
        param[1:2, g * group + heads : (g + 1) * group] = rate_d[...]
    param[2:3, 0:heads] = skip[...]
    bias = param[0:1, :]
    rate = param[1:2, :]
    loads[2].wait()
    wall[:, 0:LANES] = wbc[:, 0:LANES]
    wall[:, LANES : 2 * LANES] = jnp.concatenate([wst_t[...]] * (LANES // group), axis=0).astype(F32).T.astype(BF16)
    wall[:, 2 * LANES : 3 * LANES] = wbc[:, LANES : 2 * LANES]

    q = lax.broadcasted_iota(jnp.int32, (count, count), 0)
    k_ = lax.broadcasted_iota(jnp.int32, (count, count), 1)
    same_row = lax.div(q, C) == lax.div(k_, C)
    same_col = lax.rem(q, C) == lax.rem(k_, C)
    for n, same in enumerate((same_row, same_col)):
        masks[n, pl.ds(0, count), :] = as_mask(same & (k_ <= q))
        masks[n, pl.ds(count, count), :] = as_mask(same & (k_ > q))
        masks[n, pl.ds(2 * count, count), :] = as_mask(same)
        same_f[n] = jnp.where(same, 1.0, 0.0)
        upto_f[n] = jnp.where(same & (k_ <= q), 1.0, 0.0)
    p_d = lax.broadcasted_iota(jnp.int32, (BATCH * count, BATCH * count), 0)
    o_d = lax.broadcasted_iota(jnp.int32, (BATCH * count, BATCH * count), 1)
    near_d = lax.rem(p_d, C) == lax.rem(o_d, C)
    mask_d[pl.ds(0, BATCH * count), :] = as_mask(near_d & (o_d > p_d))
    mask_d[pl.ds(BATCH * count, count), :] = as_mask(near_d[:count])
    stacked = before * piece_rows
    p_a = lax.broadcasted_iota(jnp.int32, (stacked, stacked), 0)
    o_a = lax.broadcasted_iota(jnp.int32, (stacked, stacked), 1)
    near_a = lax.div(lax.rem(p_a, piece_rows), C) == lax.div(lax.rem(o_a, piece_rows), C)
    mask_a[...] = as_mask(near_a & (o_a > p_a))
    p_q = lax.broadcasted_iota(jnp.int32, (2 * piece_rows, stacked), 0)
    o_q = lax.broadcasted_iota(jnp.int32, (2 * piece_rows, stacked), 1)
    near_q = lax.div(lax.rem(p_q, piece_rows), C) == lax.div(lax.rem(o_q, piece_rows), C)
    same_a[...] = jnp.where(near_q, 1.0, 0.0)
    spot = lax.broadcasted_iota(jnp.int32, (LANES, inner), 0)
    head = lax.div(lax.broadcasted_iota(jnp.int32, (LANES, inner), 1), width)
    for n in range(2):
        row = head + n * heads
        spread_r[n] = as_mask((spot == row) | (spot == row + group))
    lane_from = lax.broadcasted_iota(jnp.int32, (inner, inner), 0)
    lane_to = lax.broadcasted_iota(jnp.int32, (inner, inner), 1)
    pairs = width * state // LANES
    half_size = pairs * heads
    parity = lax.div(lane_from, half_size)
    pair = lax.div(lax.rem(lane_from, half_size), heads)
    moves_r[...] = as_mask(lax.rem(lane_from, heads) * width + 2 * pair + parity == lane_to)
    loads[3].wait()
    for c in range(C):
        for n in range(pairs):
            top_r[pl.ds(n * heads, heads), c * LANES : (c + 1) * LANES] = top[c, :, n * LANES : (n + 1) * LANES]

    lane = lax.broadcasted_iota(jnp.int32, (count, LANES), 1)
    low_lanes = lax.rem(lax.div(lax.broadcasted_iota(jnp.int32, (1, LANES), 1), group), 2) == 1

    def halves_of(x):
        return jnp.where(low_lanes, x - x.astype(BF16).astype(F32), x).astype(BF16)

    def masked_sum(mask, x):
        r = dot(mask, x)
        return r + pltpu.roll(r, group, 1)

    for k in range(8):
        @pl.when(exists(k))
        def _(k=k):
            if k >= CORNERS:
                piece = corner.at[pl.ds(0, STRIP)]
                place = far_corner.at[pl.ds((k - CORNERS) * STRIP, STRIP)]
            else:
                piece = edge.at[pl.ds(0, STRIP)]
                place = halo.at[pl.ds(k * STRIP, STRIP)]
            pltpu.make_async_remote_copy(
                src_ref=piece,
                dst_ref=place,
                send_sem=hs_sem.at[k],
                recv_sem=hr_sem.at[k],
                device_id=target(k),
                device_id_type=mesh,
            ).wait_recv()

    packed = far_corner[...].astype(F32)
    rows = [
        jnp.concatenate(
            [packed[t * STRIP + n : t * STRIP + n + 1] for n in range(tok.shape[1] // LANES)], axis=1
        )
        for t in range(CORNERS)
    ]
    rows.append(jnp.zeros((STRIP - CORNERS, tok.shape[1]), F32))
    halo[pl.ds(4 * STRIP, STRIP), :] = jnp.concatenate(rows, axis=0).astype(BF16)
    halo_f[...] = dot(halo[...], win[:, :inner]).astype(BF16).astype(F32)

    def halo_rows(k, first, n):
        return halo_f[pl.ds(k * STRIP + first, n), :]

    pad[0, pl.ds(8, C), :] = halo_rows(0, STRIP - C, C)
    pad[R + 1, pl.ds(8, C), :] = halo_rows(1, 0, C)
    for r in range(R):
        pad[1 + r, pl.ds(7, 1), :] = halo_rows(2, r, 1)
        pad[1 + r, pl.ds(8 + C, 1), :] = halo_rows(3, r, 1)
    pad[0, pl.ds(7, 1), :] = halo_rows(4, 0, 1)
    pad[0, pl.ds(8 + C, 1), :] = halo_rows(4, 1, 1)
    pad[R + 1, pl.ds(7, 1), :] = halo_rows(4, 2, 1)
    pad[R + 1, pl.ds(8 + C, 1), :] = halo_rows(4, 3, 1)

    small[5].wait()
    small[6].wait()
    summed = jnp.zeros((R, C, inner), F32)
    for b in range(3):
        moved = pad[:, pl.ds(7 + b, C), :]
        for a in range(3):
            tap = conv[pl.ds(3 * a + b, 1), :].reshape(1, 1, inner)
            summed = summed + tap * moved[a : a + R]
    values_f = silu(summed).reshape(count, inner).astype(BF16).astype(F32)
    vals[...] = values_f.astype(BF16)

    def chunk_a(buffer, slot, c):
        rows = pl.ds(pl.multiple_of(c * piece_rows, piece_rows), piece_rows)
        return buffer.at[rows] if slot is None else buffer.at[slot, rows]

    def send_a(d, c):
        return pltpu.make_async_remote_copy(
            src_ref=chunk_a(vals, None, c), dst_ref=chunk_a(rva, j, c), send_sem=as_sem.at[d, c],
            recv_sem=ar_sem.at[j, c], device_id={"cols": j + d}, device_id_type=mesh,
        )

    def arrival_a(slot, c):
        return pltpu.make_async_remote_copy(
            src_ref=chunk_a(vals, None, c), dst_ref=chunk_a(rva, slot, c), send_sem=as_sem.at[0, c],
            recv_sem=ar_sem.at[slot, c], device_id={"cols": slot}, device_id_type=mesh,
        )

    def send_d(d):
        return pltpu.make_async_remote_copy(
            src_ref=vals, dst_ref=rvd.at[i], send_sem=ds_sem.at[d], recv_sem=dr_sem.at[i],
            device_id={"rows": i + d}, device_id_type=mesh,
        )

    def sends_d(d):
        return (i + d < nr) & (lax.rem(i, 2) == 0) if d == 1 else i + d < nr

    hops_d = [1] + list(range(2, nr, 2))
    sibling = i + 1 - 2 * lax.rem(i, 2)

    def relay_d(slot):
        return pltpu.make_async_remote_copy(
            src_ref=rvd.at[slot], dst_ref=rvd.at[slot], send_sem=rl_sem.at[slot],
            recv_sem=dr_sem.at[slot], device_id={"rows": sibling}, device_id_type=mesh,
        )

    def arrival_d(slot):
        return pltpu.make_async_remote_copy(
            src_ref=vals, dst_ref=rvd.at[slot], send_sem=ds_sem.at[0],
            recv_sem=dr_sem.at[slot], device_id={"rows": slot}, device_id_type=mesh,
        )

    query = pltpu.make_async_remote_copy(
        src_ref=cbuf.at[pl.ds(0, count)], dst_ref=cbuf.at[pl.ds(count, count)], send_sem=q_sem.at[0],
        recv_sem=q_sem.at[1], device_id={"cols": j - 1}, device_id_type=mesh,
    )
    def answer(c):
        return pltpu.make_async_remote_copy(
            src_ref=chunk_a(ysend, None, c), dst_ref=chunk_a(yrecv, None, c), send_sem=ys_sem.at[c],
            recv_sem=yr_sem.at[c], device_id={"cols": j + 1}, device_id_type=mesh,
        )

    further = max(0, nc - 3)
    for n in range(1, further + 1):
        @pl.when(further - j == n)
        def _(n=n):
            pl.semaphore_wait(far_sem, n)

            @pl.when(j >= 1)
            def _():
                tell_left(n)

    for c in range(CHUNKS):
        for d in range(nc - 2, 0, -1):
            @pl.when(j + d <= penult)
            def _(d=d, c=c):
                send_a(d, c).start()

    for d in hops_d[1:] + hops_d[:1]:
        @pl.when(sends_d(d))
        def _(d=d):
            send_d(d).start()

    full = dot(vals[...], wall[...])
    map_a = full[:, :LANES]
    map_d = full[:, 2 * LANES :]
    c_a = jnp.where(lane < state, pltpu.roll(map_a, state, 1), 0.0).astype(BF16)
    c_d = jnp.where(lane < state, pltpu.roll(map_d, state, 1), 0.0).astype(BF16)
    cbuf[pl.ds(0, count), :] = c_a

    @pl.when(j == last)
    def _():
        query.start()

    steps = softplus(full[:, LANES : 2 * LANES] + bias)
    log_decay = halves_of(-steps * rate)
    cum_a = masked_sum(masks[0, pl.ds(0, count), :], log_decay)
    cum_d = masked_sum(masks[1, pl.ds(0, count), :], log_decay)
    score_a = dot_nt(c_a, map_a.astype(BF16)) * upto_f[0]
    score_d = dot_nt(c_d, map_d.astype(BF16)) * upto_f[1]
    step_halves = halves_of(steps)
    weighted[pl.ds(0, count), :] = (values_f * dot(step_halves, spread_r[0])).astype(BF16)
    weighted[pl.ds(count, count), :] = (values_f * dot(step_halves, spread_r[1])).astype(BF16)
    cum_at = cum_a.T
    cum_dt = cum_d.T
    per_group = LANES // width
    for g in range(inner // LANES):
        total = jnp.zeros((count, LANES), F32)
        for e in range(per_group):
            h = g * per_group + e
            diff_a = cum_a[:, h : h + 1] - cum_at[h : h + 1, :]
            hd = heads + h
            diff_d = cum_d[:, hd : hd + 1] - cum_dt[hd : hd + 1, :]
            mix_a = (jnp.exp(jnp.minimum(diff_a, 0.0)) * score_a).astype(BF16)
            mix_d = (jnp.exp(jnp.minimum(diff_d, 0.0)) * score_d).astype(BF16)
            mix = jnp.concatenate([mix_a, mix_d], axis=1)
            part = dot(mix, weighted[:, g * LANES : (g + 1) * LANES])
            total = jnp.where(lax.div(lane, width) == e, part, total)
        y_ref[:, g * LANES : (g + 1) * LANES] = total

    column = lax.rem(q, C)
    c_low = c_d.astype(F32)
    c_high = pltpu.roll(c_low, state, 1)
    picked = jnp.concatenate(
        [
            jnp.concatenate([jnp.where(column == c, h, 0.0).astype(BF16) for c in range(C)], axis=1)
            for h in (c_low, c_high)
        ],
        axis=0,
    )
    halves = dot_nt(picked, top_r[...])
    acc_d[...] = dot(
        jnp.concatenate([halves[:count], halves[count:]], axis=1).astype(BF16), moves_r[...]
    )
    grow_a[...] = dot(halves_of(jnp.exp(cum_a)), spread_r[0])
    grow_d[...] = dot(halves_of(jnp.exp(cum_d)), spread_r[1])
    skips = dot(halves_of(jnp.broadcast_to(param[2:3, :], (count, LANES))), spread_r[0])
    y_ref[...] += skips * vals[...].astype(F32)

    def leaving(n, steps, log_decay):
        r = masked_sum(masks[n, pl.ds(count, 2 * count), :], log_decay)
        weight = halves_of(steps * jnp.exp(r[:count]))
        whole = halves_of(jnp.exp(r[count:]))
        return dot(jnp.concatenate([weight, whole], axis=0), spread_r[n])

    def across(slot):
        block = rva[slot]
        made = dot(block, wall[:, : 2 * LANES])
        s = softplus(made[:, LANES:] + bias)
        e = leaving(0, s, halves_of(-s * rate))
        entry = (block.astype(F32) * e[:count]).astype(BF16)
        score = dot_nt(cbuf[pl.ds(0, count), :], made[:, :LANES].astype(BF16)) * same_f[0]
        rows = pl.ds(0, count)
        acc_a[rows, :] = acc_a[rows, :] * e[count:] + dot(score.astype(BF16), entry)

    def down(first, m):
        total = m * count
        block = rvd[pl.ds(first, m)].reshape(total, inner)
        made = dot(block, wall[:, LANES:])
        s = softplus(made[:, :LANES] + bias)
        mask = jnp.concatenate(
            [mask_d[pl.ds(0, total), :total], mask_d[pl.ds(BATCH * count, count), :total]], axis=0
        )
        r = masked_sum(mask, halves_of(-s * rate))
        weight = halves_of(s * jnp.exp(r[:total]))
        whole = halves_of(jnp.exp(r[total:]))
        e = dot(jnp.concatenate([weight, whole], axis=0), spread_r[1])
        entry = (block.astype(F32) * e[:total]).astype(BF16)
        score = dot_nt(c_d, made[:, LANES:].astype(BF16))
        near = jnp.concatenate([same_f[1]] * m, axis=1)
        acc_d[...] = acc_d[...] * e[total:] + dot((score * near).astype(BF16), entry)

    def both(c):
        first = pl.multiple_of(c * piece_rows, piece_rows)
        rows = pl.ds(first, piece_rows)
        further_rows = pl.ds(pl.multiple_of(count + c * piece_rows, piece_rows), piece_rows)
        block = rva[pl.ds(0, before), rows, :].reshape(stacked, inner)
        made = dot(block, wall[:, : 2 * LANES])
        s = softplus(made[:, LANES:] + bias)
        r = masked_sum(mask_a[...], halves_of(-s * rate))
        e = dot(halves_of(s * jnp.exp(r)), spread_r[0])
        entry = (block.astype(F32) * e).astype(BF16)
        queries = jnp.concatenate([cbuf[rows, :], cbuf[further_rows, :]], axis=0)
        score = dot_nt(queries, made[:, :LANES].astype(BF16)) * same_a[...]
        part = dot(score.astype(BF16), entry)
        ysend[rows, :] = (part[piece_rows:] * exit_d[rows, :] + exit_y[rows, :]).astype(BF16)
        answer(c).start()
        acc_a[rows, :] = part[:piece_rows]

    acc_a[...] = jnp.zeros_like(acc_a)

    @pl.when(j == penult)
    def _():
        e = leaving(0, steps, log_decay)
        entry = (vals[...].astype(F32) * e[:count]).astype(BF16)
        exit_d[...] = e[count:]
        query.wait_recv()
        score = dot_nt(cbuf[pl.ds(count, count), :], map_a.astype(BF16)) * same_f[0]
        exit_y[...] = dot(score.astype(BF16), entry)

    def pass_on(t, carry):
        slot = lax.rem(i, 2) + 2 * t
        arrival_d(slot).wait_recv()
        relay_d(slot).start()
        return carry

    straight = lax.div(i, 2)
    lax.fori_loop(0, straight, pass_on, 0)

    @pl.when(j == penult)
    def _():
        def chunk(c, carry):
            for slot in range(before):
                arrival_a(slot, c).wait_recv()
            both(c)
            return carry

        lax.fori_loop(0, CHUNKS, chunk, 0)

    def batch(b, carry):
        first = b * BATCH
        for m in range(BATCH):
            @pl.when((first + m < i) & (lax.rem(first + m + i, 2) == 1))
            def _(m=m):
                arrival_d(first + m).wait_recv()
        for m in range(1, BATCH + 1):
            @pl.when(i - first == m if m < BATCH else i - first >= m)
            def _(m=m):
                down(first, m)
        return carry

    lax.fori_loop(0, lax.div(i + BATCH - 1, BATCH), batch, 0)

    @pl.when(j < penult)
    def _():
        def hop(slot, carry):
            for c in range(CHUNKS):
                arrival_a(slot, c).wait_recv()
            across(slot)
            return carry

        lax.fori_loop(0, j, hop, 0)

    @pl.when(j == last)
    def _():
        for c in range(CHUNKS):
            answer(c).wait_recv()
        acc_a[...] = yrecv[...].astype(F32)

    y = y_ref[...] + grow_a[...] * acc_a[...] + grow_d[...] * acc_d[...]
    gated = y * gate[...]
    scale = lax.rsqrt(jnp.mean(gated * gated, axis=-1, keepdims=True) + 1e-05)
    normed = (gated * scale * gain[...]).astype(BF16)
    loads[4].wait()
    out[...] = dot(normed, wout[...]).astype(BF16)

    for k in range(8):
        @pl.when(exists(k))
        def _(k=k):
            halo_copy(k).wait_send()
    for d in range(1, nc - 1):
        @pl.when(j + d <= penult)
        def _(d=d):
            for c in range(CHUNKS):
                send_a(d, c).wait_send()
    for d in hops_d:
        @pl.when(sends_d(d))
        def _(d=d):
            send_d(d).wait_send()

    def passed_on(t, carry):
        relay_d(lax.rem(i, 2) + 2 * t).wait_send()
        return carry

    lax.fori_loop(0, straight, passed_on, 0)

    @pl.when(j == last)
    def _():
        query.wait_send()

    @pl.when(j == penult)
    def _():
        for c in range(CHUNKS):
            answer(c).wait_send()


def shards(
    nr, nc,
    tokens, top_state, in_weight, conv_weight, bc_weight, step_weight, step_bias,
    across_rate, down_rate, skip_gain, norm_gain, out_weight,
):
    R, C, model = tokens.shape
    inner = out_weight.shape[0]
    heads = across_rate.shape[0]
    count = R * C
    vmem = pl.BlockSpec(memory_space=pltpu.VMEM)
    stacked = (nc - 2) * count // CHUNKS
    result = pl.pallas_call(
        functools.partial(kernel, nr, nc, R, C, heads),
        out_shape=jax.ShapeDtypeStruct((count, model), BF16),
        in_specs=[pl.BlockSpec(memory_space=pltpu.HBM)] * 12,
        out_specs=vmem,
        scratch_shapes=[
            pltpu.VMEM(conv_weight.shape, F32),
            pltpu.VMEM((2 * heads, inner), BF16),
            pltpu.VMEM((1, 2 * heads), F32),
            pltpu.VMEM((1, heads), F32),
            pltpu.VMEM((1, heads), F32),
            pltpu.VMEM((1, heads), F32),
            pltpu.VMEM((1, inner), F32),
            pltpu.VMEM((count, model), BF16),
            pltpu.VMEM(top_state.shape, BF16),
            pltpu.VMEM(in_weight.shape, BF16),
            pltpu.VMEM(bc_weight.shape, BF16),
            pltpu.VMEM(out_weight.shape, BF16),
            pltpu.VMEM((inner, 3 * LANES), BF16),
            pltpu.VMEM((8, LANES), F32),
            pltpu.VMEM((2 * R, model), BF16),
            pltpu.VMEM((5 * STRIP, model), BF16),
            pltpu.VMEM((5 * STRIP, inner), F32),
            pltpu.VMEM((R + 2, 24, inner), F32),
            pltpu.VMEM((count, inner), F32),
            pltpu.VMEM((count, inner), BF16),
            pltpu.VMEM((nc, count, inner), BF16),
            pltpu.VMEM((nr, count, inner), BF16),
            pltpu.VMEM((count, inner), F32),
            pltpu.VMEM((count, inner), F32),
            pltpu.VMEM((2 * count, inner), BF16),
            pltpu.VMEM((count, inner), F32),
            pltpu.VMEM((2, 3 * count, count), BF16),
            pltpu.VMEM(((BATCH + 1) * count, BATCH * count), BF16),
            pltpu.VMEM((stacked, stacked), BF16),
            pltpu.VMEM((2 * count // CHUNKS, stacked), F32),
            pltpu.VMEM((2, count, count), F32),
            pltpu.VMEM((2, count, count), F32),
            pltpu.VMEM((2, LANES, inner), BF16),
            pltpu.VMEM((inner, inner), BF16),
            pltpu.VMEM((top_state.shape[2] // LANES * heads, C * LANES), BF16),
            pltpu.VMEM((count, inner), F32),
            pltpu.VMEM((count, inner), F32),
            pltpu.VMEM((count, inner), F32),
            pltpu.VMEM((count, inner), F32),
            pltpu.VMEM((2 * count, LANES), BF16),
            pltpu.VMEM((count, inner), BF16),
            pltpu.VMEM((count, inner), BF16),
            pltpu.VMEM((CORNERS * STRIP, LANES), BF16),
            pltpu.VMEM((CORNERS * STRIP, LANES), BF16),
            pltpu.SemaphoreType.DMA((5,)),
            pltpu.SemaphoreType.DMA((7,)),
            pltpu.SemaphoreType.DMA((8,)),
            pltpu.SemaphoreType.DMA((8,)),
            pltpu.SemaphoreType.DMA((nc, CHUNKS)),
            pltpu.SemaphoreType.DMA((nc, CHUNKS)),
            pltpu.SemaphoreType.DMA((nr,)),
            pltpu.SemaphoreType.DMA((nr,)),
            pltpu.SemaphoreType.DMA((nr,)),
            pltpu.SemaphoreType.DMA((2,)),
            pltpu.SemaphoreType.DMA((CHUNKS,)),
            pltpu.SemaphoreType.DMA((CHUNKS,)),
            pltpu.SemaphoreType.REGULAR,
        ],
        compiler_params=pltpu.CompilerParams(
            collective_id=0, has_side_effects=True, vmem_limit_bytes=48000 * 1024
        ),
    )(
        *(
            pltpu.with_memory_space_constraint(x, pltpu.HBM)
            for x in (
                tokens.reshape(count, model),
                top_state,
                in_weight,
                bc_weight,
                out_weight,
                conv_weight,
                step_weight.T,
                step_bias[None],
                across_rate[None],
                down_rate[None],
                skip_gain[None],
                norm_gain[None],
            )
        )
    )
    return result.reshape(R, C, model)


def solution(mesh):
    in_specs = (
        P(("groups", "rows"), "cols", None),
        P(("groups", "cols"), None, None),
    ) + (P(),) * 10
    out_specs = P(("groups", "rows"), "cols", None)
    return jax.shard_map(
        functools.partial(shards, mesh.shape["rows"], mesh.shape["cols"]),
        mesh=mesh, in_specs=in_specs, out_specs=out_specs, check_vma=False,
    )
```

```python
import functools

import jax
import jax.numpy as jnp
from jax import lax
from jax.experimental import pallas as pl
from jax.experimental.pallas import tpu as pltpu
from jax.sharding import PartitionSpec as P

F32 = jnp.float32
BF16 = jnp.bfloat16
NEIGHBOURS = ((-1, 0), (1, 0), (0, -1), (0, 1), (-1, -1), (-1, 1), (1, -1), (1, 1))
OPPOSITE = (1, 0, 3, 2, 7, 6, 5, 4)
STRIP = 16
LANES = 128
CHUNKS = 4
ADDED = 3
BATCH = 3
CORNERS = 4


def dot(a, b):
    return jnp.dot(a, b, preferred_element_type=F32)


def dot_nt(a, b):
    return lax.dot_general(a, b, (((1,), (1,)), ((), ())), preferred_element_type=F32)


def softplus(x):
    return jnp.maximum(x, 0.0) + jnp.log1p(jnp.exp(-jnp.abs(x)))


def silu(x):
    return x / (1.0 + jnp.exp(-x))


def kernel(
    nr, nc, R, C, heads,
    tok_h, top_h, win_h, wbc_h, wout_h, conv_h, wst_h, bias_h, rate_a_h, rate_d_h, skip_h, gain_h, out,
    conv, wst_t, step_bias, rate_a, rate_d, skip, gain,
    tok, top, win, wbc, wout, wall, param, edge, halo, halo_f, pad, gate, vals, rva, rvd, acc_a, acc_d,
    weighted, y_ref, masks, mask_d, mask_a, same_a, same_f, upto_f, spread_r, moves_r, top_r, grow_a, grow_d, exit_y, exit_d,
    cbuf, ysend, yrecv, corner, far_corner,
    ld_sem, sm_sem, hs_sem, hr_sem, as_sem, ar_sem, ds_sem, dr_sem, rl_sem, q_sem, ys_sem, yr_sem, far_sem,
):
    count = R * C
    inner = wout.shape[0]
    state = wbc.shape[1] // 4
    width = inner // heads
    group = 2 * heads
    penult, last = nc - 2, nc - 1
    before = nc - 2
    piece_rows = count // CHUNKS
    i = lax.axis_index("rows")
    j = lax.axis_index("cols")
    mesh = pl.DeviceIdType.MESH

    def exists(k):
        di, dj = NEIGHBOURS[k]
        a, b = i + di, j + dj
        return (a >= 0) & (a < nr) & (b >= 0) & (b < nc)

    def target(k):
        di, dj = NEIGHBOURS[k]
        return {"rows": i + di, "cols": j + dj}

    loads = [
        pltpu.make_async_copy(a, b, ld_sem.at[n])
        for n, (a, b) in enumerate(
            ((tok_h, tok), (win_h, win), (wbc_h, wbc), (top_h, top), (wout_h, wout))
        )
    ]
    small = [
        pltpu.make_async_copy(a, b, sm_sem.at[n])
        for n, (a, b) in enumerate(
            (
                (wst_h, wst_t), (bias_h, step_bias), (rate_a_h, rate_a), (rate_d_h, rate_d),
                (skip_h, skip), (conv_h, conv), (gain_h, gain),
            )
        )
    ]
    loads[0].start()
    loads[1].start()
    for load in small:
        load.start()
    for load in loads[2:]:
        load.start()

    barrier = pltpu.get_barrier_semaphore()
    for d in range(1, nr):
        pl.semaphore_signal(
            barrier, inc=1, device_id={"rows": lax.rem(i + d, nr)}, device_id_type=mesh
        )
    for k in range(2, 8):
        @pl.when(exists(k))
        def _(k=k):
            pl.semaphore_signal(barrier, inc=1, device_id=target(k), device_id_type=mesh)

    def as_mask(m):
        return jnp.where(m, 1.0, 0.0).astype(BF16)

    pos = lax.broadcasted_iota(jnp.int32, (2 * R, count), 0)
    src = lax.broadcasted_iota(jnp.int32, (2 * R, count), 1)
    wanted = jnp.where(pos < R, pos * C, (pos - R) * C + C - 1)
    param[...] = jnp.zeros_like(param)
    loads[0].wait()
    edge[...] = dot(as_mask(src == wanted), tok[...]).astype(BF16)
    slot_at = lax.broadcasted_iota(jnp.int32, (CORNERS * STRIP, count), 0)
    token_at = lax.broadcasted_iota(jnp.int32, (CORNERS * STRIP, count), 1)
    which = lax.div(slot_at, STRIP)
    at_corner = token_at == lax.div(which, 2) * (count - C) + lax.rem(which, 2) * (C - 1)
    corner[...] = sum(
        dot(as_mask(at_corner & (lax.rem(slot_at, STRIP) == n)), tok[:, n * LANES : (n + 1) * LANES])
        for n in range(tok.shape[1] // LANES)
    ).astype(BF16)
    around = sum(jnp.where(exists(k), 1, 0) for k in range(2, 8))
    pl.semaphore_wait(barrier, nr - 1 + around)

    def halo_copy(k):
        di, dj = NEIGHBOURS[k]
        if k >= CORNERS:
            piece = corner.at[pl.ds((k - CORNERS) * STRIP, STRIP)]
            place = far_corner.at[pl.ds((OPPOSITE[k] - CORNERS) * STRIP, STRIP)]
        else:
            if di < 0:
                piece = tok.at[pl.ds(0, STRIP)]
            elif di > 0:
                piece = tok.at[pl.ds(count - STRIP, STRIP)]
            else:
                piece = edge.at[pl.ds(0 if dj < 0 else R, STRIP)]
            place = halo.at[pl.ds(OPPOSITE[k] * STRIP, STRIP)]
        return pltpu.make_async_remote_copy(
            src_ref=piece,
            dst_ref=place,
            send_sem=hs_sem.at[k],
            recv_sem=hr_sem.at[OPPOSITE[k]],
            device_id=target(k),
            device_id_type=mesh,
        )

    for k in (4, 5, 6, 7, 2, 3, 0, 1):
        @pl.when(exists(k))
        def _(k=k):
            halo_copy(k).start()

    for k in range(8):
        @pl.when(jnp.logical_not(exists(k)))
        def _(k=k):
            if k >= CORNERS:
                far_corner[pl.ds((k - CORNERS) * STRIP, STRIP)] = jnp.zeros((STRIP, LANES), BF16)
            else:
                halo[pl.ds(k * STRIP, STRIP)] = jnp.zeros((STRIP, halo.shape[1]), BF16)

    def tell_left(amount):
        pl.semaphore_signal(far_sem, inc=amount, device_id={"cols": j - 1}, device_id_type=mesh)

    @pl.when((j >= 1) & (j <= penult))
    def _():
        tell_left(1)

    loads[1].wait()
    projected = dot(tok[...], win[...])
    gate[...] = silu(projected[:, inner:].astype(BF16).astype(F32))
    mixer = projected[:, :inner].astype(BF16).astype(F32)
    pad[pl.ds(1, R), pl.ds(8, C), :] = mixer.reshape(R, C, inner)

    for n in range(1, nc - 1):
        @pl.when(penult - j == n)
        def _(n=n):
            pl.semaphore_wait(far_sem, n)

            @pl.when(j >= 1)
            def _():
                tell_left(n)

    for load in small[:5]:
        load.wait()
    for g in range(LANES // group):
        param[0:1, g * group : (g + 1) * group] = step_bias[...]
        param[1:2, g * group : g * group + heads] = rate_a[...]
        param[1:2, g * group + heads : (g + 1) * group] = rate_d[...]
    param[2:3, 0:heads] = skip[...]
    bias = param[0:1, :]
    rate = param[1:2, :]
    loads[2].wait()
    wall[:, 0:LANES] = wbc[:, 0:LANES]
    wall[:, LANES : 2 * LANES] = jnp.concatenate([wst_t[...]] * (LANES // group), axis=0).astype(F32).T.astype(BF16)
    wall[:, 2 * LANES : 3 * LANES] = wbc[:, LANES : 2 * LANES]

    q = lax.broadcasted_iota(jnp.int32, (count, count), 0)
    k_ = lax.broadcasted_iota(jnp.int32, (count, count), 1)
    same_row = lax.div(q, C) == lax.div(k_, C)
    same_col = lax.rem(q, C) == lax.rem(k_, C)
    for n, same in enumerate((same_row, same_col)):
        masks[n, pl.ds(0, count), :] = as_mask(same & (k_ <= q))
        masks[n, pl.ds(count, count), :] = as_mask(same & (k_ > q))
        masks[n, pl.ds(2 * count, count), :] = as_mask(same)
        same_f[n] = jnp.where(same, 1.0, 0.0)
        upto_f[n] = jnp.where(same & (k_ <= q), 1.0, 0.0)
    p_d = lax.broadcasted_iota(jnp.int32, (BATCH * count, BATCH * count), 0)
    o_d = lax.broadcasted_iota(jnp.int32, (BATCH * count, BATCH * count), 1)
    near_d = lax.rem(p_d, C) == lax.rem(o_d, C)
    mask_d[pl.ds(0, BATCH * count), :] = as_mask(near_d & (o_d > p_d))
    mask_d[pl.ds(BATCH * count, count), :] = as_mask(near_d[:count])
    stacked = last * piece_rows
    p_a = lax.broadcasted_iota(jnp.int32, (stacked, stacked), 0)
    o_a = lax.broadcasted_iota(jnp.int32, (stacked, stacked), 1)
    near_a = lax.div(lax.rem(p_a, piece_rows), C) == lax.div(lax.rem(o_a, piece_rows), C)
    mask_a[...] = as_mask(near_a & (o_a > p_a))
    p_q = lax.broadcasted_iota(jnp.int32, (2 * piece_rows, stacked), 0)
    o_q = lax.broadcasted_iota(jnp.int32, (2 * piece_rows, stacked), 1)
    near_q = lax.div(lax.rem(p_q, piece_rows), C) == lax.div(lax.rem(o_q, piece_rows), C)
    same_a[...] = jnp.where(near_q, 1.0, 0.0)
    spot = lax.broadcasted_iota(jnp.int32, (LANES, inner), 0)
    head = lax.div(lax.broadcasted_iota(jnp.int32, (LANES, inner), 1), width)
    for n in range(2):
        row = head + n * heads
        spread_r[n] = as_mask((spot == row) | (spot == row + group))
    lane_from = lax.broadcasted_iota(jnp.int32, (inner, inner), 0)
    lane_to = lax.broadcasted_iota(jnp.int32, (inner, inner), 1)
    pairs = width * state // LANES
    half_size = pairs * heads
    parity = lax.div(lane_from, half_size)
    pair = lax.div(lax.rem(lane_from, half_size), heads)
    moves_r[...] = as_mask(lax.rem(lane_from, heads) * width + 2 * pair + parity == lane_to)
    loads[3].wait()
    for c in range(C):
        for n in range(pairs):
            top_r[pl.ds(n * heads, heads), c * LANES : (c + 1) * LANES] = top[c, :, n * LANES : (n + 1) * LANES]

    lane = lax.broadcasted_iota(jnp.int32, (count, LANES), 1)
    low_lanes = lax.rem(lax.div(lax.broadcasted_iota(jnp.int32, (1, LANES), 1), group), 2) == 1

    def halves_of(x):
        return jnp.where(low_lanes, x - x.astype(BF16).astype(F32), x).astype(BF16)

    def masked_sum(mask, x):
        r = dot(mask, x)
        return r + pltpu.roll(r, group, 1)

    for k in range(8):
        @pl.when(exists(k))
        def _(k=k):
            if k >= CORNERS:
                piece = corner.at[pl.ds(0, STRIP)]
                place = far_corner.at[pl.ds((k - CORNERS) * STRIP, STRIP)]
            else:
                piece = edge.at[pl.ds(0, STRIP)]
                place = halo.at[pl.ds(k * STRIP, STRIP)]
            pltpu.make_async_remote_copy(
                src_ref=piece,
                dst_ref=place,
                send_sem=hs_sem.at[k],
                recv_sem=hr_sem.at[k],
                device_id=target(k),
                device_id_type=mesh,
            ).wait_recv()

    packed = far_corner[...].astype(F32)
    rows = [
        jnp.concatenate(
            [packed[t * STRIP + n : t * STRIP + n + 1] for n in range(tok.shape[1] // LANES)], axis=1
        )
        for t in range(CORNERS)
    ]
    rows.append(jnp.zeros((STRIP - CORNERS, tok.shape[1]), F32))
    halo[pl.ds(4 * STRIP, STRIP), :] = jnp.concatenate(rows, axis=0).astype(BF16)
    halo_f[...] = dot(halo[...], win[:, :inner]).astype(BF16).astype(F32)

    def halo_rows(k, first, n):
        return halo_f[pl.ds(k * STRIP + first, n), :]

    pad[0, pl.ds(8, C), :] = halo_rows(0, STRIP - C, C)
    pad[R + 1, pl.ds(8, C), :] = halo_rows(1, 0, C)
    for r in range(R):
        pad[1 + r, pl.ds(7, 1), :] = halo_rows(2, r, 1)
        pad[1 + r, pl.ds(8 + C, 1), :] = halo_rows(3, r, 1)
    pad[0, pl.ds(7, 1), :] = halo_rows(4, 0, 1)
    pad[0, pl.ds(8 + C, 1), :] = halo_rows(4, 1, 1)
    pad[R + 1, pl.ds(7, 1), :] = halo_rows(4, 2, 1)
    pad[R + 1, pl.ds(8 + C, 1), :] = halo_rows(4, 3, 1)

    small[5].wait()
    small[6].wait()
    summed = jnp.zeros((R, C, inner), F32)
    for b in range(3):
        moved = pad[:, pl.ds(7 + b, C), :]
        for a in range(3):
            tap = conv[pl.ds(3 * a + b, 1), :].reshape(1, 1, inner)
            summed = summed + tap * moved[a : a + R]
    values_f = silu(summed).reshape(count, inner).astype(BF16).astype(F32)
    vals[...] = values_f.astype(BF16)

    def chunk_a(buffer, slot, c):
        rows = pl.ds(pl.multiple_of(c * piece_rows, piece_rows), piece_rows)
        return buffer.at[rows] if slot is None else buffer.at[slot, rows]

    def send_a(d, c):
        return pltpu.make_async_remote_copy(
            src_ref=chunk_a(vals, None, c), dst_ref=chunk_a(rva, j, c), send_sem=as_sem.at[d, c],
            recv_sem=ar_sem.at[j, c], device_id={"cols": j + d}, device_id_type=mesh,
        )

    def arrival_a(slot, c):
        return pltpu.make_async_remote_copy(
            src_ref=chunk_a(vals, None, c), dst_ref=chunk_a(rva, slot, c), send_sem=as_sem.at[0, c],
            recv_sem=ar_sem.at[slot, c], device_id={"cols": slot}, device_id_type=mesh,
        )

    def send_d(d):
        return pltpu.make_async_remote_copy(
            src_ref=vals, dst_ref=rvd.at[i], send_sem=ds_sem.at[d], recv_sem=dr_sem.at[i],
            device_id={"rows": i + d}, device_id_type=mesh,
        )

    def sends_d(d):
        return (i + d < nr) & (lax.rem(i, 2) == 0) if d == 1 else i + d < nr

    hops_d = [1] + list(range(2, nr, 2))
    sibling = i + 1 - 2 * lax.rem(i, 2)

    def relay_d(slot):
        return pltpu.make_async_remote_copy(
            src_ref=rvd.at[slot], dst_ref=rvd.at[slot], send_sem=rl_sem.at[slot],
            recv_sem=dr_sem.at[slot], device_id={"rows": sibling}, device_id_type=mesh,
        )

    def arrival_d(slot):
        return pltpu.make_async_remote_copy(
            src_ref=vals, dst_ref=rvd.at[slot], send_sem=ds_sem.at[0],
            recv_sem=dr_sem.at[slot], device_id={"rows": slot}, device_id_type=mesh,
        )

    query = pltpu.make_async_remote_copy(
        src_ref=cbuf.at[pl.ds(0, count)], dst_ref=cbuf.at[pl.ds(count, count)], send_sem=q_sem.at[0],
        recv_sem=q_sem.at[1], device_id={"cols": j - 1}, device_id_type=mesh,
    )
    def answer(c):
        return pltpu.make_async_remote_copy(
            src_ref=chunk_a(ysend, None, c), dst_ref=chunk_a(yrecv, None, c), send_sem=ys_sem.at[c],
            recv_sem=yr_sem.at[c], device_id={"cols": j + 1}, device_id_type=mesh,
        )

    def furthest(c):
        return penult if c < ADDED else last

    for c in range(CHUNKS):
        for d in range(1, nc):
            @pl.when(j + d <= furthest(c))
            def _(d=d, c=c):
                send_a(d, c).start()

    for d in hops_d[1:] + hops_d[:1]:
        @pl.when(sends_d(d))
        def _(d=d):
            send_d(d).start()

    full = dot(vals[...], wall[...])
    map_a = full[:, :LANES]
    map_d = full[:, 2 * LANES :]
    c_a = jnp.where(lane < state, pltpu.roll(map_a, state, 1), 0.0).astype(BF16)
    c_d = jnp.where(lane < state, pltpu.roll(map_d, state, 1), 0.0).astype(BF16)
    cbuf[pl.ds(0, count), :] = c_a

    @pl.when(j == last)
    def _():
        query.start()

    steps = softplus(full[:, LANES : 2 * LANES] + bias)
    log_decay = halves_of(-steps * rate)
    cum_a = masked_sum(masks[0, pl.ds(0, count), :], log_decay)
    cum_d = masked_sum(masks[1, pl.ds(0, count), :], log_decay)
    score_a = dot_nt(c_a, map_a.astype(BF16)) * upto_f[0]
    score_d = dot_nt(c_d, map_d.astype(BF16)) * upto_f[1]
    step_halves = halves_of(steps)
    weighted[pl.ds(0, count), :] = (values_f * dot(step_halves, spread_r[0])).astype(BF16)
    weighted[pl.ds(count, count), :] = (values_f * dot(step_halves, spread_r[1])).astype(BF16)
    cum_at = cum_a.T
    cum_dt = cum_d.T
    per_group = LANES // width
    for g in range(inner // LANES):
        total = jnp.zeros((count, LANES), F32)
        for e in range(per_group):
            h = g * per_group + e
            diff_a = cum_a[:, h : h + 1] - cum_at[h : h + 1, :]
            hd = heads + h
            diff_d = cum_d[:, hd : hd + 1] - cum_dt[hd : hd + 1, :]
            mix_a = (jnp.exp(jnp.minimum(diff_a, 0.0)) * score_a).astype(BF16)
            mix_d = (jnp.exp(jnp.minimum(diff_d, 0.0)) * score_d).astype(BF16)
            mix = jnp.concatenate([mix_a, mix_d], axis=1)
            part = dot(mix, weighted[:, g * LANES : (g + 1) * LANES])
            total = jnp.where(lax.div(lane, width) == e, part, total)
        y_ref[:, g * LANES : (g + 1) * LANES] = total

    column = lax.rem(q, C)
    c_low = c_d.astype(F32)
    c_high = pltpu.roll(c_low, state, 1)
    picked = jnp.concatenate(
        [
            jnp.concatenate([jnp.where(column == c, h, 0.0).astype(BF16) for c in range(C)], axis=1)
            for h in (c_low, c_high)
        ],
        axis=0,
    )
    halves = dot_nt(picked, top_r[...])
    acc_d[...] = dot(
        jnp.concatenate([halves[:count], halves[count:]], axis=1).astype(BF16), moves_r[...]
    )
    grow_a[...] = dot(halves_of(jnp.exp(cum_a)), spread_r[0])
    grow_d[...] = dot(halves_of(jnp.exp(cum_d)), spread_r[1])
    skips = dot(halves_of(jnp.broadcast_to(param[2:3, :], (count, LANES))), spread_r[0])
    y_ref[...] += skips * vals[...].astype(F32)

    def leaving(n, steps, log_decay):
        r = masked_sum(masks[n, pl.ds(count, 2 * count), :], log_decay)
        weight = halves_of(steps * jnp.exp(r[:count]))
        whole = halves_of(jnp.exp(r[count:]))
        return dot(jnp.concatenate([weight, whole], axis=0), spread_r[n])

    def across(slot):
        block = rva[slot]
        made = dot(block, wall[:, : 2 * LANES])
        s = softplus(made[:, LANES:] + bias)
        e = leaving(0, s, halves_of(-s * rate))
        entry = (block.astype(F32) * e[:count]).astype(BF16)
        score = dot_nt(cbuf[pl.ds(0, count), :], made[:, :LANES].astype(BF16)) * same_f[0]
        rows = pl.ds(0, count)
        acc_a[rows, :] = acc_a[rows, :] * e[count:] + dot(score.astype(BF16), entry)

    def down(first, m):
        total = m * count
        block = rvd[pl.ds(first, m)].reshape(total, inner)
        made = dot(block, wall[:, LANES:])
        s = softplus(made[:, :LANES] + bias)
        mask = jnp.concatenate(
            [mask_d[pl.ds(0, total), :total], mask_d[pl.ds(BATCH * count, count), :total]], axis=0
        )
        r = masked_sum(mask, halves_of(-s * rate))
        weight = halves_of(s * jnp.exp(r[:total]))
        whole = halves_of(jnp.exp(r[total:]))
        e = dot(jnp.concatenate([weight, whole], axis=0), spread_r[1])
        entry = (block.astype(F32) * e[:total]).astype(BF16)
        score = dot_nt(c_d, made[:, LANES:].astype(BF16))
        near = jnp.concatenate([same_f[1]] * m, axis=1)
        acc_d[...] = acc_d[...] * e[total:] + dot((score * near).astype(BF16), entry)

    def left(c, blocks, added):
        rows = pl.ds(pl.multiple_of(c * piece_rows, piece_rows), piece_rows)
        total = blocks * piece_rows
        block = rva[pl.ds(0, blocks), rows, :].reshape(total, inner)
        made = dot(block, wall[:, : 2 * LANES])
        s = softplus(made[:, LANES:] + bias)
        r = masked_sum(mask_a[pl.ds(0, total), :total], halves_of(-s * rate))
        e = dot(halves_of(s * jnp.exp(r)), spread_r[0])
        entry = (block.astype(F32) * e).astype(BF16)
        queries = cbuf[rows, :]
        if added:
            far_rows = pl.ds(pl.multiple_of(count + c * piece_rows, piece_rows), piece_rows)
            queries = jnp.concatenate([queries, cbuf[far_rows, :]], axis=0)
        near = same_a[pl.ds(0, queries.shape[0]), :total]
        score = dot_nt(queries, made[:, :LANES].astype(BF16)) * near
        part = dot(score.astype(BF16), entry)
        if added:
            ysend[rows, :] = (part[piece_rows:] * exit_d[rows, :] + exit_y[rows, :]).astype(BF16)
            answer(c).start()
        acc_a[rows, :] = part[:piece_rows]

    acc_a[...] = jnp.zeros_like(acc_a)

    @pl.when(j == penult)
    def _():
        e = leaving(0, steps, log_decay)
        entry = (vals[...].astype(F32) * e[:count]).astype(BF16)
        exit_d[...] = e[count:]
        query.wait_recv()
        score = dot_nt(cbuf[pl.ds(count, count), :], map_a.astype(BF16)) * same_f[0]
        exit_y[...] = dot(score.astype(BF16), entry)

    def pass_on(t, carry):
        slot = lax.rem(i, 2) + 2 * t
        arrival_d(slot).wait_recv()
        relay_d(slot).start()
        return carry

    straight = lax.div(i, 2)
    lax.fori_loop(0, straight, pass_on, 0)

    @pl.when(j == penult)
    def _():
        def chunk(c, carry):
            for slot in range(before):
                arrival_a(slot, c).wait_recv()
            left(c, before, True)
            return carry

        lax.fori_loop(0, ADDED, chunk, 0)

    def batch(b, carry):
        first = b * BATCH
        for m in range(BATCH):
            @pl.when((first + m < i) & (lax.rem(first + m + i, 2) == 1))
            def _(m=m):
                arrival_d(first + m).wait_recv()
        for m in range(1, BATCH + 1):
            @pl.when(i - first == m if m < BATCH else i - first >= m)
            def _(m=m):
                down(first, m)
        return carry

    lax.fori_loop(0, lax.div(i + BATCH - 1, BATCH), batch, 0)

    @pl.when(j == penult)
    def _():
        for c in range(ADDED, CHUNKS):
            for slot in range(before):
                arrival_a(slot, c).wait_recv()
            left(c, before, False)

    @pl.when(j < penult)
    def _():
        def hop(slot, carry):
            for c in range(CHUNKS):
                arrival_a(slot, c).wait_recv()
            across(slot)
            return carry

        lax.fori_loop(0, j, hop, 0)

    @pl.when(j == last)
    def _():
        for c in range(ADDED, CHUNKS):
            for slot in range(last):
                arrival_a(slot, c).wait_recv()
            left(c, last, False)
        for c in range(ADDED):
            answer(c).wait_recv()
        rows = pl.ds(0, ADDED * piece_rows)
        acc_a[rows, :] = yrecv[rows, :].astype(F32)

    y = y_ref[...] + grow_a[...] * acc_a[...] + grow_d[...] * acc_d[...]
    gated = y * gate[...]
    scale = lax.rsqrt(jnp.mean(gated * gated, axis=-1, keepdims=True) + 1e-05)
    normed = (gated * scale * gain[...]).astype(BF16)
    loads[4].wait()
    out[...] = dot(normed, wout[...]).astype(BF16)

    for k in range(8):
        @pl.when(exists(k))
        def _(k=k):
            halo_copy(k).wait_send()
    for c in range(CHUNKS):
        for d in range(1, nc):
            @pl.when(j + d <= furthest(c))
            def _(d=d, c=c):
                send_a(d, c).wait_send()

    for d in hops_d:
        @pl.when(sends_d(d))
        def _(d=d):
            send_d(d).wait_send()

    def passed_on(t, carry):
        relay_d(lax.rem(i, 2) + 2 * t).wait_send()
        return carry

    lax.fori_loop(0, straight, passed_on, 0)

    @pl.when(j == last)
    def _():
        query.wait_send()

    @pl.when(j == penult)
    def _():
        for c in range(ADDED):
            answer(c).wait_send()


def shards(
    nr, nc,
    tokens, top_state, in_weight, conv_weight, bc_weight, step_weight, step_bias,
    across_rate, down_rate, skip_gain, norm_gain, out_weight,
):
    R, C, model = tokens.shape
    inner = out_weight.shape[0]
    heads = across_rate.shape[0]
    count = R * C
    vmem = pl.BlockSpec(memory_space=pltpu.VMEM)
    stacked = (nc - 1) * count // CHUNKS
    result = pl.pallas_call(
        functools.partial(kernel, nr, nc, R, C, heads),
        out_shape=jax.ShapeDtypeStruct((count, model), BF16),
        in_specs=[pl.BlockSpec(memory_space=pltpu.HBM)] * 12,
        out_specs=vmem,
        scratch_shapes=[
            pltpu.VMEM(conv_weight.shape, F32),
            pltpu.VMEM((2 * heads, inner), BF16),
            pltpu.VMEM((1, 2 * heads), F32),
            pltpu.VMEM((1, heads), F32),
            pltpu.VMEM((1, heads), F32),
            pltpu.VMEM((1, heads), F32),
            pltpu.VMEM((1, inner), F32),
            pltpu.VMEM((count, model), BF16),
            pltpu.VMEM(top_state.shape, BF16),
            pltpu.VMEM(in_weight.shape, BF16),
            pltpu.VMEM(bc_weight.shape, BF16),
            pltpu.VMEM(out_weight.shape, BF16),
            pltpu.VMEM((inner, 3 * LANES), BF16),
            pltpu.VMEM((8, LANES), F32),
            pltpu.VMEM((2 * R, model), BF16),
            pltpu.VMEM((5 * STRIP, model), BF16),
            pltpu.VMEM((5 * STRIP, inner), F32),
            pltpu.VMEM((R + 2, 24, inner), F32),
            pltpu.VMEM((count, inner), F32),
            pltpu.VMEM((count, inner), BF16),
            pltpu.VMEM((nc, count, inner), BF16),
            pltpu.VMEM((nr, count, inner), BF16),
            pltpu.VMEM((count, inner), F32),
            pltpu.VMEM((count, inner), F32),
            pltpu.VMEM((2 * count, inner), BF16),
            pltpu.VMEM((count, inner), F32),
            pltpu.VMEM((2, 3 * count, count), BF16),
            pltpu.VMEM(((BATCH + 1) * count, BATCH * count), BF16),
            pltpu.VMEM((stacked, stacked), BF16),
            pltpu.VMEM((2 * count // CHUNKS, stacked), F32),
            pltpu.VMEM((2, count, count), F32),
            pltpu.VMEM((2, count, count), F32),
            pltpu.VMEM((2, LANES, inner), BF16),
            pltpu.VMEM((inner, inner), BF16),
            pltpu.VMEM((top_state.shape[2] // LANES * heads, C * LANES), BF16),
            pltpu.VMEM((count, inner), F32),
            pltpu.VMEM((count, inner), F32),
            pltpu.VMEM((count, inner), F32),
            pltpu.VMEM((count, inner), F32),
            pltpu.VMEM((2 * count, LANES), BF16),
            pltpu.VMEM((count, inner), BF16),
            pltpu.VMEM((count, inner), BF16),
            pltpu.VMEM((CORNERS * STRIP, LANES), BF16),
            pltpu.VMEM((CORNERS * STRIP, LANES), BF16),
            pltpu.SemaphoreType.DMA((5,)),
            pltpu.SemaphoreType.DMA((7,)),
            pltpu.SemaphoreType.DMA((8,)),
            pltpu.SemaphoreType.DMA((8,)),
            pltpu.SemaphoreType.DMA((nc, CHUNKS)),
            pltpu.SemaphoreType.DMA((nc, CHUNKS)),
            pltpu.SemaphoreType.DMA((nr,)),
            pltpu.SemaphoreType.DMA((nr,)),
            pltpu.SemaphoreType.DMA((nr,)),
            pltpu.SemaphoreType.DMA((2,)),
            pltpu.SemaphoreType.DMA((CHUNKS,)),
            pltpu.SemaphoreType.DMA((CHUNKS,)),
            pltpu.SemaphoreType.REGULAR,
        ],
        compiler_params=pltpu.CompilerParams(
            collective_id=0, has_side_effects=True, vmem_limit_bytes=48000 * 1024
        ),
    )(
        *(
            pltpu.with_memory_space_constraint(x, pltpu.HBM)
            for x in (
                tokens.reshape(count, model),
                top_state,
                in_weight,
                bc_weight,
                out_weight,
                conv_weight,
                step_weight.T,
                step_bias[None],
                across_rate[None],
                down_rate[None],
                skip_gain[None],
                norm_gain[None],
            )
        )
    )
    return result.reshape(R, C, model)


def solution(mesh):
    in_specs = (
        P(("groups", "rows"), "cols", None),
        P(("groups", "cols"), None, None),
    ) + (P(),) * 10
    out_specs = P(("groups", "rows"), "cols", None)
    return jax.shard_map(
        functools.partial(shards, mesh.shape["rows"], mesh.shape["cols"]),
        mesh=mesh, in_specs=in_specs, out_specs=out_specs, check_vma=False,
    )
```

```python
import functools

import jax
import jax.numpy as jnp
from jax import lax
from jax.experimental import pallas as pl
from jax.experimental.pallas import tpu as pltpu
from jax.sharding import PartitionSpec as P

F32 = jnp.float32
BF16 = jnp.bfloat16
NEIGHBOURS = ((-1, 0), (1, 0), (0, -1), (0, 1), (-1, -1), (-1, 1), (1, -1), (1, 1))
OPPOSITE = (1, 0, 3, 2, 7, 6, 5, 4)
STRIP = 16
LANES = 128
PIECES = ((0, 2), (2, 2), (4, 2), (6, 2))
CHUNKS = len(PIECES)
ADDED = 3
LENGTHS = sorted({n for _, n in PIECES})
BATCH = 3
CORNERS = 4


def dot(a, b):
    return jnp.dot(a, b, preferred_element_type=F32)


def dot_nt(a, b):
    return lax.dot_general(a, b, (((1,), (1,)), ((), ())), preferred_element_type=F32)


def softplus(x):
    return jnp.maximum(x, 0.0) + jnp.log1p(jnp.exp(-jnp.abs(x)))


def silu(x):
    return x / (1.0 + jnp.exp(-x))


def kernel(
    nr, nc, R, C, heads,
    tok_h, top_h, win_h, wbc_h, wout_h, conv_h, wst_h, bias_h, rate_a_h, rate_d_h, skip_h, gain_h, out,
    conv, wst_t, step_bias, rate_a, rate_d, skip, gain,
    tok, top, win, wbc, wout, wall, param, edge, halo, halo_f, pad, inner_sum, sides, side_sum, gate, vals, rva, rvd, acc_a, acc_d,
    weighted, y_ref, masks, mask_d, mask_a, same_a, same_f, upto_f, spread_r, moves_r, top_r, grow_a, grow_d, exit_y, exit_d,
    cbuf, ysend, yrecv, corner, far_corner,
    ld_sem, sm_sem, hs_sem, hr_sem, as_sem, ar_sem, ds_sem, dr_sem, rl_sem, q_sem, ys_sem, yr_sem, far_sem,
):
    count = R * C
    inner = wout.shape[0]
    state = wbc.shape[1] // 4
    width = inner // heads
    group = 2 * heads
    penult, last = nc - 2, nc - 1
    before = nc - 2
    i = lax.axis_index("rows")
    j = lax.axis_index("cols")
    mesh = pl.DeviceIdType.MESH

    def exists(k):
        di, dj = NEIGHBOURS[k]
        a, b = i + di, j + dj
        return (a >= 0) & (a < nr) & (b >= 0) & (b < nc)

    def target(k):
        di, dj = NEIGHBOURS[k]
        return {"rows": i + di, "cols": j + dj}

    loads = [
        pltpu.make_async_copy(a, b, ld_sem.at[n])
        for n, (a, b) in enumerate(
            ((tok_h, tok), (win_h, win), (wbc_h, wbc), (top_h, top), (wout_h, wout))
        )
    ]
    small = [
        pltpu.make_async_copy(a, b, sm_sem.at[n])
        for n, (a, b) in enumerate(
            (
                (wst_h, wst_t), (bias_h, step_bias), (rate_a_h, rate_a), (rate_d_h, rate_d),
                (skip_h, skip), (conv_h, conv), (gain_h, gain),
            )
        )
    ]
    loads[0].start()
    loads[1].start()
    for load in small:
        load.start()
    for load in loads[2:]:
        load.start()

    barrier = pltpu.get_barrier_semaphore()
    for d in range(1, nr):
        pl.semaphore_signal(
            barrier, inc=1, device_id={"rows": lax.rem(i + d, nr)}, device_id_type=mesh
        )
    for k in range(2, 8):
        @pl.when(exists(k))
        def _(k=k):
            pl.semaphore_signal(barrier, inc=1, device_id=target(k), device_id_type=mesh)

    def as_mask(m):
        return jnp.where(m, 1.0, 0.0).astype(BF16)

    pos = lax.broadcasted_iota(jnp.int32, (2 * R, count), 0)
    src = lax.broadcasted_iota(jnp.int32, (2 * R, count), 1)
    wanted = jnp.where(pos < R, pos * C, (pos - R) * C + C - 1)
    param[...] = jnp.zeros_like(param)
    loads[0].wait()
    edge[...] = dot(as_mask(src == wanted), tok[...]).astype(BF16)
    slot_at = lax.broadcasted_iota(jnp.int32, (CORNERS * STRIP, count), 0)
    token_at = lax.broadcasted_iota(jnp.int32, (CORNERS * STRIP, count), 1)
    which = lax.div(slot_at, STRIP)
    at_corner = token_at == lax.div(which, 2) * (count - C) + lax.rem(which, 2) * (C - 1)
    corner[...] = sum(
        dot(as_mask(at_corner & (lax.rem(slot_at, STRIP) == n)), tok[:, n * LANES : (n + 1) * LANES])
        for n in range(tok.shape[1] // LANES)
    ).astype(BF16)
    around = sum(jnp.where(exists(k), 1, 0) for k in range(2, 8))
    pl.semaphore_wait(barrier, nr - 1 + around)

    def halo_copy(k):
        di, dj = NEIGHBOURS[k]
        if k >= CORNERS:
            piece = corner.at[pl.ds((k - CORNERS) * STRIP, STRIP)]
            place = far_corner.at[pl.ds((OPPOSITE[k] - CORNERS) * STRIP, STRIP)]
        else:
            if di < 0:
                piece = tok.at[pl.ds(0, STRIP)]
            elif di > 0:
                piece = tok.at[pl.ds(count - STRIP, STRIP)]
            else:
                piece = edge.at[pl.ds(0 if dj < 0 else R, STRIP)]
            place = halo.at[pl.ds(OPPOSITE[k] * STRIP, STRIP)]
        return pltpu.make_async_remote_copy(
            src_ref=piece,
            dst_ref=place,
            send_sem=hs_sem.at[k],
            recv_sem=hr_sem.at[OPPOSITE[k]],
            device_id=target(k),
            device_id_type=mesh,
        )

    for k in (4, 5, 6, 7, 2, 3, 0, 1):
        @pl.when(exists(k))
        def _(k=k):
            halo_copy(k).start()

    for k in range(8):
        @pl.when(jnp.logical_not(exists(k)))
        def _(k=k):
            if k >= CORNERS:
                far_corner[pl.ds((k - CORNERS) * STRIP, STRIP)] = jnp.zeros((STRIP, LANES), BF16)
            else:
                halo[pl.ds(k * STRIP, STRIP)] = jnp.zeros((STRIP, halo.shape[1]), BF16)

    def tell_left(amount):
        pl.semaphore_signal(far_sem, inc=amount, device_id={"cols": j - 1}, device_id_type=mesh)

    @pl.when((j >= 1) & (j <= penult))
    def _():
        tell_left(1)

    loads[1].wait()
    projected = dot(tok[...], win[...])
    gate[...] = silu(projected[:, inner:].astype(BF16).astype(F32))
    mixer = projected[:, :inner].astype(BF16).astype(F32)
    pad[...] = jnp.zeros_like(pad)
    sides[...] = jnp.zeros_like(sides)
    side_sum[...] = jnp.zeros_like(side_sum)
    pad[pl.ds(1, R), pl.ds(8, C), :] = mixer.reshape(R, C, inner)
    small[5].wait()

    def tap(a, b):
        return conv[pl.ds(3 * a + b, 1), :]

    own = jnp.zeros((R, C, inner), F32)
    for b in range(3):
        moved = pad[:, pl.ds(7 + b, C), :]
        for a in range(3):
            own = own + tap(a, b).reshape(1, 1, inner) * moved[a : a + R]
    inner_sum[...] = own

    for n in range(1, nc - 1):
        @pl.when(penult - j == n)
        def _(n=n):
            pl.semaphore_wait(far_sem, n)

            @pl.when(j >= 1)
            def _():
                tell_left(n)

    for load in small[:5]:
        load.wait()
    for g in range(LANES // group):
        param[0:1, g * group : (g + 1) * group] = step_bias[...]
        param[1:2, g * group : g * group + heads] = rate_a[...]
        param[1:2, g * group + heads : (g + 1) * group] = rate_d[...]
    param[2:3, 0:heads] = skip[...]
    bias = param[0:1, :]
    rate = param[1:2, :]
    loads[2].wait()
    wall[:, 0:LANES] = wbc[:, 0:LANES]
    wall[:, LANES : 2 * LANES] = jnp.concatenate([wst_t[...]] * (LANES // group), axis=0).astype(F32).T.astype(BF16)
    wall[:, 2 * LANES : 3 * LANES] = wbc[:, LANES : 2 * LANES]

    q = lax.broadcasted_iota(jnp.int32, (count, count), 0)
    k_ = lax.broadcasted_iota(jnp.int32, (count, count), 1)
    same_row = lax.div(q, C) == lax.div(k_, C)
    same_col = lax.rem(q, C) == lax.rem(k_, C)
    for n, same in enumerate((same_row, same_col)):
        masks[n, pl.ds(0, count), :] = as_mask(same & (k_ <= q))
        masks[n, pl.ds(count, count), :] = as_mask(same & (k_ > q))
        masks[n, pl.ds(2 * count, count), :] = as_mask(same)
        same_f[n] = jnp.where(same, 1.0, 0.0)
        upto_f[n] = jnp.where(same & (k_ <= q), 1.0, 0.0)
    p_d = lax.broadcasted_iota(jnp.int32, (BATCH * count, BATCH * count), 0)
    o_d = lax.broadcasted_iota(jnp.int32, (BATCH * count, BATCH * count), 1)
    near_d = lax.rem(p_d, C) == lax.rem(o_d, C)
    mask_d[pl.ds(0, BATCH * count), :] = as_mask(near_d & (o_d > p_d))
    mask_d[pl.ds(BATCH * count, count), :] = as_mask(near_d[:count])
    stacked = last * LENGTHS[-1] * STRIP
    p_a = lax.broadcasted_iota(jnp.int32, (stacked, stacked), 0)
    o_a = lax.broadcasted_iota(jnp.int32, (stacked, stacked), 1)
    p_q = lax.broadcasted_iota(jnp.int32, same_a.shape[1:], 0)
    o_q = lax.broadcasted_iota(jnp.int32, same_a.shape[1:], 1)
    for n, length in enumerate(LENGTHS):
        size = length * STRIP
        near_a = lax.div(lax.rem(p_a, size), C) == lax.div(lax.rem(o_a, size), C)
        mask_a[n] = as_mask(near_a & (o_a > p_a))
        near_q = lax.div(lax.rem(p_q, size), C) == lax.div(lax.rem(o_q, size), C)
        same_a[n] = jnp.where(near_q, 1.0, 0.0)
    spot = lax.broadcasted_iota(jnp.int32, (LANES, inner), 0)
    head = lax.div(lax.broadcasted_iota(jnp.int32, (LANES, inner), 1), width)
    for n in range(2):
        row = head + n * heads
        spread_r[n] = as_mask((spot == row) | (spot == row + group))
    lane_from = lax.broadcasted_iota(jnp.int32, (inner, inner), 0)
    lane_to = lax.broadcasted_iota(jnp.int32, (inner, inner), 1)
    pairs = width * state // LANES
    half_size = pairs * heads
    parity = lax.div(lane_from, half_size)
    pair = lax.div(lax.rem(lane_from, half_size), heads)
    moves_r[...] = as_mask(lax.rem(lane_from, heads) * width + 2 * pair + parity == lane_to)
    loads[3].wait()
    for c in range(C):
        for n in range(pairs):
            top_r[pl.ds(n * heads, heads), c * LANES : (c + 1) * LANES] = top[c, :, n * LANES : (n + 1) * LANES]

    lane = lax.broadcasted_iota(jnp.int32, (count, LANES), 1)
    low_lanes = lax.rem(lax.div(lax.broadcasted_iota(jnp.int32, (1, LANES), 1), group), 2) == 1

    def halves_of(x):
        return jnp.where(low_lanes, x - x.astype(BF16).astype(F32), x).astype(BF16)

    def masked_sum(mask, x):
        r = dot(mask, x)
        return r + pltpu.roll(r, group, 1)

    for k in range(8):
        @pl.when(exists(k))
        def _(k=k):
            if k >= CORNERS:
                piece = corner.at[pl.ds(0, STRIP)]
                place = far_corner.at[pl.ds((k - CORNERS) * STRIP, STRIP)]
            else:
                piece = edge.at[pl.ds(0, STRIP)]
                place = halo.at[pl.ds(k * STRIP, STRIP)]
            pltpu.make_async_remote_copy(
                src_ref=piece,
                dst_ref=place,
                send_sem=hs_sem.at[k],
                recv_sem=hr_sem.at[k],
                device_id=target(k),
                device_id_type=mesh,
            ).wait_recv()

    packed = far_corner[...].astype(F32)
    rows = [
        jnp.concatenate(
            [packed[t * STRIP + n : t * STRIP + n + 1] for n in range(tok.shape[1] // LANES)], axis=1
        )
        for t in range(CORNERS)
    ]
    rows.append(jnp.zeros((STRIP - CORNERS, tok.shape[1]), F32))
    halo[pl.ds(4 * STRIP, STRIP), :] = jnp.concatenate(rows, axis=0).astype(BF16)
    halo_f[...] = dot(halo[...], win[:, :inner]).astype(BF16).astype(F32)

    def halo_rows(k, first, n):
        return halo_f[pl.ds(k * STRIP + first, n), :]

    pad[0, pl.ds(8, C), :] = halo_rows(0, STRIP - C, C)
    pad[R + 1, pl.ds(8, C), :] = halo_rows(1, 0, C)
    pad[0, pl.ds(7, 1), :] = halo_rows(4, 0, 1)
    pad[0, pl.ds(8 + C, 1), :] = halo_rows(4, 1, 1)
    pad[R + 1, pl.ds(7, 1), :] = halo_rows(4, 2, 1)
    pad[R + 1, pl.ds(8 + C, 1), :] = halo_rows(4, 3, 1)
    for n in range(2):
        sides[n, pl.ds(8, R), :] = halo_rows(2 + n, 0, R)
        side = sum(tap(a, 2 * n) * sides[n, pl.ds(7 + a, R), :] for a in range(3))
        for r in range(R):
            side_sum[r, pl.ds(n * (C - 1), 1), :] = side[r : r + 1]
    small[6].wait()
    for a, r in ((0, 0), (2, R - 1)):
        inner_sum[r] += sum(tap(a, b) * pad[r + a, pl.ds(7 + b, C), :] for b in range(3))
    summed = inner_sum[...] + side_sum[...]
    values_f = silu(summed).reshape(count, inner).astype(BF16).astype(F32)
    vals[...] = values_f.astype(BF16)

    def chunk_a(buffer, slot, c):
        rows = pl.ds(PIECES[c][0] * STRIP, PIECES[c][1] * STRIP)
        return buffer.at[rows] if slot is None else buffer.at[slot, rows]

    def send_a(d, c):
        return pltpu.make_async_remote_copy(
            src_ref=chunk_a(vals, None, c), dst_ref=chunk_a(rva, j, c), send_sem=as_sem.at[d, c],
            recv_sem=ar_sem.at[j, c], device_id={"cols": j + d}, device_id_type=mesh,
        )

    def arrival_a(slot, c):
        return pltpu.make_async_remote_copy(
            src_ref=chunk_a(vals, None, c), dst_ref=chunk_a(rva, slot, c), send_sem=as_sem.at[0, c],
            recv_sem=ar_sem.at[slot, c], device_id={"cols": slot}, device_id_type=mesh,
        )

    def send_d(d):
        return pltpu.make_async_remote_copy(
            src_ref=vals, dst_ref=rvd.at[i], send_sem=ds_sem.at[d], recv_sem=dr_sem.at[i],
            device_id={"rows": i + d}, device_id_type=mesh,
        )

    def sends_d(d):
        return (i + d < nr) & (lax.rem(i, 2) == 0) if d == 1 else i + d < nr

    hops_d = [1] + list(range(2, nr, 2))
    sibling = i + 1 - 2 * lax.rem(i, 2)

    def relay_d(slot):
        return pltpu.make_async_remote_copy(
            src_ref=rvd.at[slot], dst_ref=rvd.at[slot], send_sem=rl_sem.at[slot],
            recv_sem=dr_sem.at[slot], device_id={"rows": sibling}, device_id_type=mesh,
        )

    def arrival_d(slot):
        return pltpu.make_async_remote_copy(
            src_ref=vals, dst_ref=rvd.at[slot], send_sem=ds_sem.at[0],
            recv_sem=dr_sem.at[slot], device_id={"rows": slot}, device_id_type=mesh,
        )

    query = pltpu.make_async_remote_copy(
        src_ref=cbuf.at[pl.ds(0, count)], dst_ref=cbuf.at[pl.ds(count, count)], send_sem=q_sem.at[0],
        recv_sem=q_sem.at[1], device_id={"cols": j - 1}, device_id_type=mesh,
    )
    def answer(c):
        return pltpu.make_async_remote_copy(
            src_ref=chunk_a(ysend, None, c), dst_ref=chunk_a(yrecv, None, c), send_sem=ys_sem.at[c],
            recv_sem=yr_sem.at[c], device_id={"cols": j + 1}, device_id_type=mesh,
        )

    def furthest(c):
        return penult if c < ADDED else last

    for c in range(CHUNKS):
        for d in range(1, nc):
            @pl.when(j + d <= furthest(c))
            def _(d=d, c=c):
                send_a(d, c).start()

    for d in hops_d[1:] + hops_d[:1]:
        @pl.when(sends_d(d))
        def _(d=d):
            send_d(d).start()

    full = dot(vals[...], wall[...])
    map_a = full[:, :LANES]
    map_d = full[:, 2 * LANES :]
    c_a = jnp.where(lane < state, pltpu.roll(map_a, state, 1), 0.0).astype(BF16)
    c_d = jnp.where(lane < state, pltpu.roll(map_d, state, 1), 0.0).astype(BF16)
    cbuf[pl.ds(0, count), :] = c_a

    @pl.when(j == last)
    def _():
        query.start()

    steps = softplus(full[:, LANES : 2 * LANES] + bias)
    log_decay = halves_of(-steps * rate)
    cum_a = masked_sum(masks[0, pl.ds(0, count), :], log_decay)
    cum_d = masked_sum(masks[1, pl.ds(0, count), :], log_decay)
    score_a = dot_nt(c_a, map_a.astype(BF16)) * upto_f[0]
    score_d = dot_nt(c_d, map_d.astype(BF16)) * upto_f[1]
    step_halves = halves_of(steps)
    weighted[pl.ds(0, count), :] = (values_f * dot(step_halves, spread_r[0])).astype(BF16)
    weighted[pl.ds(count, count), :] = (values_f * dot(step_halves, spread_r[1])).astype(BF16)
    cum_at = cum_a.T
    cum_dt = cum_d.T
    per_group = LANES // width
    for g in range(inner // LANES):
        total = jnp.zeros((count, LANES), F32)
        for e in range(per_group):
            h = g * per_group + e
            diff_a = cum_a[:, h : h + 1] - cum_at[h : h + 1, :]
            hd = heads + h
            diff_d = cum_d[:, hd : hd + 1] - cum_dt[hd : hd + 1, :]
            mix_a = (jnp.exp(jnp.minimum(diff_a, 0.0)) * score_a).astype(BF16)
            mix_d = (jnp.exp(jnp.minimum(diff_d, 0.0)) * score_d).astype(BF16)
            mix = jnp.concatenate([mix_a, mix_d], axis=1)
            part = dot(mix, weighted[:, g * LANES : (g + 1) * LANES])
            total = jnp.where(lax.div(lane, width) == e, part, total)
        y_ref[:, g * LANES : (g + 1) * LANES] = total

    column = lax.rem(q, C)
    c_low = c_d.astype(F32)
    c_high = pltpu.roll(c_low, state, 1)
    picked = jnp.concatenate(
        [
            jnp.concatenate([jnp.where(column == c, h, 0.0).astype(BF16) for c in range(C)], axis=1)
            for h in (c_low, c_high)
        ],
        axis=0,
    )
    halves = dot_nt(picked, top_r[...])
    acc_d[...] = dot(
        jnp.concatenate([halves[:count], halves[count:]], axis=1).astype(BF16), moves_r[...]
    )
    grow_a[...] = dot(halves_of(jnp.exp(cum_a)), spread_r[0])
    grow_d[...] = dot(halves_of(jnp.exp(cum_d)), spread_r[1])
    skips = dot(halves_of(jnp.broadcast_to(param[2:3, :], (count, LANES))), spread_r[0])
    y_ref[...] += skips * vals[...].astype(F32)

    def leaving(n, steps, log_decay):
        r = masked_sum(masks[n, pl.ds(count, 2 * count), :], log_decay)
        weight = halves_of(steps * jnp.exp(r[:count]))
        whole = halves_of(jnp.exp(r[count:]))
        return dot(jnp.concatenate([weight, whole], axis=0), spread_r[n])

    def across(slot):
        block = rva[slot]
        made = dot(block, wall[:, : 2 * LANES])
        s = softplus(made[:, LANES:] + bias)
        e = leaving(0, s, halves_of(-s * rate))
        entry = (block.astype(F32) * e[:count]).astype(BF16)
        score = dot_nt(cbuf[pl.ds(0, count), :], made[:, :LANES].astype(BF16)) * same_f[0]
        rows = pl.ds(0, count)
        acc_a[rows, :] = acc_a[rows, :] * e[count:] + dot(score.astype(BF16), entry)

    def down(first, m):
        total = m * count
        block = rvd[pl.ds(first, m)].reshape(total, inner)
        made = dot(block, wall[:, LANES:])
        s = softplus(made[:, :LANES] + bias)
        mask = jnp.concatenate(
            [mask_d[pl.ds(0, total), :total], mask_d[pl.ds(BATCH * count, count), :total]], axis=0
        )
        r = masked_sum(mask, halves_of(-s * rate))
        weight = halves_of(s * jnp.exp(r[:total]))
        whole = halves_of(jnp.exp(r[total:]))
        e = dot(jnp.concatenate([weight, whole], axis=0), spread_r[1])
        entry = (block.astype(F32) * e[:total]).astype(BF16)
        score = dot_nt(c_d, made[:, LANES:].astype(BF16))
        near = jnp.concatenate([same_f[1]] * m, axis=1)
        acc_d[...] = acc_d[...] * e[total:] + dot((score * near).astype(BF16), entry)

    def left(c, blocks, added):
        first, size = PIECES[c][0] * STRIP, PIECES[c][1] * STRIP
        kind = LENGTHS.index(PIECES[c][1])
        rows = pl.ds(first, size)
        total = blocks * size
        block = rva[pl.ds(0, blocks), rows, :].reshape(total, inner)
        made = dot(block, wall[:, : 2 * LANES])
        s = softplus(made[:, LANES:] + bias)
        r = masked_sum(mask_a[kind, pl.ds(0, total), :total], halves_of(-s * rate))
        e = dot(halves_of(s * jnp.exp(r)), spread_r[0])
        entry = (block.astype(F32) * e).astype(BF16)
        queries = cbuf[rows, :]
        if added:
            queries = jnp.concatenate([queries, cbuf[pl.ds(count + first, size), :]], axis=0)
        near = same_a[kind, pl.ds(0, queries.shape[0]), :total]
        score = dot_nt(queries, made[:, :LANES].astype(BF16)) * near
        part = dot(score.astype(BF16), entry)
        if added:
            ysend[rows, :] = (part[size:] * exit_d[rows, :] + exit_y[rows, :]).astype(BF16)
            answer(c).start()
        acc_a[rows, :] = part[:size]

    acc_a[...] = jnp.zeros_like(acc_a)
    loads[4].wait()

    @pl.when(j == penult)
    def _():
        e = leaving(0, steps, log_decay)
        entry = (vals[...].astype(F32) * e[:count]).astype(BF16)
        exit_d[...] = e[count:]
        query.wait_recv()
        score = dot_nt(cbuf[pl.ds(count, count), :], map_a.astype(BF16)) * same_f[0]
        exit_y[...] = dot(score.astype(BF16), entry)

    def pass_on(t, carry):
        slot = lax.rem(i, 2) + 2 * t
        arrival_d(slot).wait_recv()
        relay_d(slot).start()
        return carry

    straight = lax.div(i, 2)
    lax.fori_loop(0, straight, pass_on, 0)

    @pl.when(j == penult)
    def _():
        for c in range(ADDED):
            for slot in range(before):
                arrival_a(slot, c).wait_recv()
            left(c, before, True)

    def batch(b, carry):
        first = b * BATCH
        for m in range(BATCH):
            @pl.when((first + m < i) & (lax.rem(first + m + i, 2) == 1))
            def _(m=m):
                arrival_d(first + m).wait_recv()
        for m in range(1, BATCH + 1):
            @pl.when(i - first == m if m < BATCH else i - first >= m)
            def _(m=m):
                down(first, m)
        return carry

    lax.fori_loop(0, lax.div(i + BATCH - 1, BATCH), batch, 0)

    @pl.when(j == penult)
    def _():
        for c in range(ADDED, CHUNKS):
            for slot in range(before):
                arrival_a(slot, c).wait_recv()
            left(c, before, False)

    @pl.when(j < penult)
    def _():
        def hop(slot, carry):
            for c in range(CHUNKS):
                arrival_a(slot, c).wait_recv()
            across(slot)
            return carry

        lax.fori_loop(0, j, hop, 0)

    @pl.when(j == last)
    def _():
        for c in range(ADDED, CHUNKS):
            for slot in range(last):
                arrival_a(slot, c).wait_recv()
            left(c, last, False)
        for c in range(ADDED):
            answer(c).wait_recv()
        rows = pl.ds(0, PIECES[ADDED][0] * STRIP)
        acc_a[rows, :] = yrecv[rows, :].astype(F32)

    y = y_ref[...] + grow_a[...] * acc_a[...] + grow_d[...] * acc_d[...]
    gated = y * gate[...]
    scale = lax.rsqrt(jnp.mean(gated * gated, axis=-1, keepdims=True) + 1e-05)
    out[...] = (dot((gated * gain[...]).astype(BF16), wout[...]) * scale).astype(BF16)

    for k in range(8):
        @pl.when(exists(k))
        def _(k=k):
            halo_copy(k).wait_send()
    for c in range(CHUNKS):
        for d in range(1, nc):
            @pl.when(j + d <= furthest(c))
            def _(d=d, c=c):
                send_a(d, c).wait_send()

    for d in hops_d:
        @pl.when(sends_d(d))
        def _(d=d):
            send_d(d).wait_send()

    def passed_on(t, carry):
        relay_d(lax.rem(i, 2) + 2 * t).wait_send()
        return carry

    lax.fori_loop(0, straight, passed_on, 0)

    @pl.when(j == last)
    def _():
        query.wait_send()

    @pl.when(j == penult)
    def _():
        for c in range(ADDED):
            answer(c).wait_send()


def shards(
    nr, nc,
    tokens, top_state, in_weight, conv_weight, bc_weight, step_weight, step_bias,
    across_rate, down_rate, skip_gain, norm_gain, out_weight,
):
    R, C, model = tokens.shape
    inner = out_weight.shape[0]
    heads = across_rate.shape[0]
    count = R * C
    vmem = pl.BlockSpec(memory_space=pltpu.VMEM)
    stacked = (nc - 1) * LENGTHS[-1] * STRIP
    result = pl.pallas_call(
        functools.partial(kernel, nr, nc, R, C, heads),
        out_shape=jax.ShapeDtypeStruct((count, model), BF16),
        in_specs=[pl.BlockSpec(memory_space=pltpu.HBM)] * 12,
        out_specs=vmem,
        scratch_shapes=[
            pltpu.VMEM(conv_weight.shape, F32),
            pltpu.VMEM((2 * heads, inner), BF16),
            pltpu.VMEM((1, 2 * heads), F32),
            pltpu.VMEM((1, heads), F32),
            pltpu.VMEM((1, heads), F32),
            pltpu.VMEM((1, heads), F32),
            pltpu.VMEM((1, inner), F32),
            pltpu.VMEM((count, model), BF16),
            pltpu.VMEM(top_state.shape, BF16),
            pltpu.VMEM(in_weight.shape, BF16),
            pltpu.VMEM(bc_weight.shape, BF16),
            pltpu.VMEM(out_weight.shape, BF16),
            pltpu.VMEM((inner, 3 * LANES), BF16),
            pltpu.VMEM((8, LANES), F32),
            pltpu.VMEM((2 * R, model), BF16),
            pltpu.VMEM((5 * STRIP, model), BF16),
            pltpu.VMEM((5 * STRIP, inner), F32),
            pltpu.VMEM((R + 2, 24, inner), F32),
            pltpu.VMEM((R, C, inner), F32),
            pltpu.VMEM((2, R + 16, inner), F32),
            pltpu.VMEM((R, C, inner), F32),
            pltpu.VMEM((count, inner), F32),
            pltpu.VMEM((count, inner), BF16),
            pltpu.VMEM((nc, count, inner), BF16),
            pltpu.VMEM((nr, count, inner), BF16),
            pltpu.VMEM((count, inner), F32),
            pltpu.VMEM((count, inner), F32),
            pltpu.VMEM((2 * count, inner), BF16),
            pltpu.VMEM((count, inner), F32),
            pltpu.VMEM((2, 3 * count, count), BF16),
            pltpu.VMEM(((BATCH + 1) * count, BATCH * count), BF16),
            pltpu.VMEM((len(LENGTHS), stacked, stacked), BF16),
            pltpu.VMEM((len(LENGTHS), 2 * LENGTHS[-1] * STRIP, stacked), F32),
            pltpu.VMEM((2, count, count), F32),
            pltpu.VMEM((2, count, count), F32),
            pltpu.VMEM((2, LANES, inner), BF16),
            pltpu.VMEM((inner, inner), BF16),
            pltpu.VMEM((top_state.shape[2] // LANES * heads, C * LANES), BF16),
            pltpu.VMEM((count, inner), F32),
            pltpu.VMEM((count, inner), F32),
            pltpu.VMEM((count, inner), F32),
            pltpu.VMEM((count, inner), F32),
            pltpu.VMEM((2 * count, LANES), BF16),
            pltpu.VMEM((count, inner), BF16),
            pltpu.VMEM((count, inner), BF16),
            pltpu.VMEM((CORNERS * STRIP, LANES), BF16),
            pltpu.VMEM((CORNERS * STRIP, LANES), BF16),
            pltpu.SemaphoreType.DMA((5,)),
            pltpu.SemaphoreType.DMA((7,)),
            pltpu.SemaphoreType.DMA((8,)),
            pltpu.SemaphoreType.DMA((8,)),
            pltpu.SemaphoreType.DMA((nc, CHUNKS)),
            pltpu.SemaphoreType.DMA((nc, CHUNKS)),
            pltpu.SemaphoreType.DMA((nr,)),
            pltpu.SemaphoreType.DMA((nr,)),
            pltpu.SemaphoreType.DMA((nr,)),
            pltpu.SemaphoreType.DMA((2,)),
            pltpu.SemaphoreType.DMA((CHUNKS,)),
            pltpu.SemaphoreType.DMA((CHUNKS,)),
            pltpu.SemaphoreType.REGULAR,
        ],
        compiler_params=pltpu.CompilerParams(
            collective_id=0, has_side_effects=True, vmem_limit_bytes=48000 * 1024
        ),
    )(
        *(
            pltpu.with_memory_space_constraint(x, pltpu.HBM)
            for x in (
                tokens.reshape(count, model),
                top_state,
                in_weight,
                bc_weight,
                out_weight,
                conv_weight,
                step_weight.T,
                step_bias[None],
                across_rate[None],
                down_rate[None],
                skip_gain[None],
                norm_gain[None],
            )
        )
    )
    return result.reshape(R, C, model)


def solution(mesh):
    in_specs = (
        P(("groups", "rows"), "cols", None),
        P(("groups", "cols"), None, None),
    ) + (P(),) * 10
    out_specs = P(("groups", "rows"), "cols", None)
    return jax.shard_map(
        functools.partial(shards, mesh.shape["rows"], mesh.shape["cols"]),
        mesh=mesh, in_specs=in_specs, out_specs=out_specs, check_vma=False,
    )
```

```python
import functools

import jax
import jax.numpy as jnp
from jax import lax
from jax.experimental import pallas as pl
from jax.experimental.pallas import tpu as pltpu
from jax.sharding import PartitionSpec as P

F32 = jnp.float32
BF16 = jnp.bfloat16
NEIGHBOURS = ((-1, 0), (1, 0), (0, -1), (0, 1), (-1, -1), (-1, 1), (1, -1), (1, 1))
OPPOSITE = (1, 0, 3, 2, 7, 6, 5, 4)
STRIP = 16
LANES = 128
PIECES = ((0, 2), (2, 2), (4, 2), (6, 2))
CHUNKS = len(PIECES)
ADDED = 3
LENGTHS = sorted({n for _, n in PIECES})
BATCH = 3
CORNERS = 4


def dot(a, b):
    return jnp.dot(a, b, preferred_element_type=F32)


def dot_nt(a, b):
    return lax.dot_general(a, b, (((1,), (1,)), ((), ())), preferred_element_type=F32)


def softplus(x):
    return jnp.maximum(x, 0.0) + jnp.log1p(jnp.exp(-jnp.abs(x)))


def silu(x):
    return x / (1.0 + jnp.exp(-x))


def kernel(
    nr, nc, R, C, heads,
    tok_h, top_h, win_h, wbc_h, wout_h, conv_h, wst_h, bias_h, rate_a_h, rate_d_h, skip_h, gain_h, out,
    conv, wst_t, step_bias, rate_a, rate_d, skip, gain,
    tok, top, win, wbc, wout, wall, param, edge, halo, halo_f, pad, inner_sum, sides, side_sum, gate, vals, rva, rvd, acc_a, acc_d,
    weighted, y_ref, masks, mask_d, mask_a, same_a, same_f, upto_f, spread_r, moves_r, top_r, grow_a, grow_d, exit_y, exit_d,
    cbuf, ysend, yrecv, corner, far_corner,
    ld_sem, sm_sem, hs_sem, hr_sem, as_sem, ar_sem, ds_sem, dr_sem, rl_sem, q_sem, ys_sem, yr_sem, far_sem,
):
    count = R * C
    inner = wout.shape[0]
    state = wbc.shape[1] // 4
    width = inner // heads
    group = 2 * heads
    penult, last = nc - 2, nc - 1
    before = nc - 2
    i = lax.axis_index("rows")
    j = lax.axis_index("cols")
    mesh = pl.DeviceIdType.MESH

    def exists(k):
        di, dj = NEIGHBOURS[k]
        a, b = i + di, j + dj
        return (a >= 0) & (a < nr) & (b >= 0) & (b < nc)

    def target(k):
        di, dj = NEIGHBOURS[k]
        return {"rows": i + di, "cols": j + dj}

    loads = [
        pltpu.make_async_copy(a, b, ld_sem.at[n])
        for n, (a, b) in enumerate(
            ((tok_h, tok), (win_h, win), (wbc_h, wbc), (top_h, top), (wout_h, wout))
        )
    ]
    small = [
        pltpu.make_async_copy(a, b, sm_sem.at[n])
        for n, (a, b) in enumerate(
            (
                (wst_h, wst_t), (bias_h, step_bias), (rate_a_h, rate_a), (rate_d_h, rate_d),
                (skip_h, skip), (conv_h, conv), (gain_h, gain),
            )
        )
    ]
    loads[0].start()
    loads[1].start()
    for load in small:
        load.start()
    for load in loads[2:]:
        load.start()

    barrier = pltpu.get_barrier_semaphore()
    for d in range(1, nr):
        pl.semaphore_signal(
            barrier, inc=1, device_id={"rows": lax.rem(i + d, nr)}, device_id_type=mesh
        )
    for k in range(2, 8):
        @pl.when(exists(k))
        def _(k=k):
            pl.semaphore_signal(barrier, inc=1, device_id=target(k), device_id_type=mesh)

    def as_mask(m):
        return jnp.where(m, 1.0, 0.0).astype(BF16)

    pos = lax.broadcasted_iota(jnp.int32, (2 * R, count), 0)
    src = lax.broadcasted_iota(jnp.int32, (2 * R, count), 1)
    wanted = jnp.where(pos < R, pos * C, (pos - R) * C + C - 1)
    param[...] = jnp.zeros_like(param)
    loads[0].wait()
    edge[...] = dot(as_mask(src == wanted), tok[...]).astype(BF16)
    slot_at = lax.broadcasted_iota(jnp.int32, (CORNERS * STRIP, count), 0)
    token_at = lax.broadcasted_iota(jnp.int32, (CORNERS * STRIP, count), 1)
    which = lax.div(slot_at, STRIP)
    at_corner = token_at == lax.div(which, 2) * (count - C) + lax.rem(which, 2) * (C - 1)
    corner[...] = sum(
        dot(as_mask(at_corner & (lax.rem(slot_at, STRIP) == n)), tok[:, n * LANES : (n + 1) * LANES])
        for n in range(tok.shape[1] // LANES)
    ).astype(BF16)
    around = sum(jnp.where(exists(k), 1, 0) for k in range(2, 8))
    pl.semaphore_wait(barrier, nr - 1 + around)

    def halo_copy(k):
        di, dj = NEIGHBOURS[k]
        if k >= CORNERS:
            piece = corner.at[pl.ds((k - CORNERS) * STRIP, STRIP)]
            place = far_corner.at[pl.ds((OPPOSITE[k] - CORNERS) * STRIP, STRIP)]
        else:
            if di < 0:
                piece = tok.at[pl.ds(0, STRIP)]
            elif di > 0:
                piece = tok.at[pl.ds(count - STRIP, STRIP)]
            else:
                piece = edge.at[pl.ds(0 if dj < 0 else R, STRIP)]
            place = halo.at[pl.ds(OPPOSITE[k] * STRIP, STRIP)]
        return pltpu.make_async_remote_copy(
            src_ref=piece,
            dst_ref=place,
            send_sem=hs_sem.at[k],
            recv_sem=hr_sem.at[OPPOSITE[k]],
            device_id=target(k),
            device_id_type=mesh,
        )

    for k in (4, 5, 6, 7, 2, 3, 0, 1):
        @pl.when(exists(k))
        def _(k=k):
            halo_copy(k).start()

    for k in range(8):
        @pl.when(jnp.logical_not(exists(k)))
        def _(k=k):
            if k >= CORNERS:
                far_corner[pl.ds((k - CORNERS) * STRIP, STRIP)] = jnp.zeros((STRIP, LANES), BF16)
            else:
                halo[pl.ds(k * STRIP, STRIP)] = jnp.zeros((STRIP, halo.shape[1]), BF16)

    def tell_left(amount):
        pl.semaphore_signal(far_sem, inc=amount, device_id={"cols": j - 1}, device_id_type=mesh)

    @pl.when((j >= 1) & (j <= penult))
    def _():
        tell_left(1)

    loads[1].wait()
    projected = dot(tok[...], win[...])
    gate[...] = silu(projected[:, inner:].astype(BF16).astype(F32))
    mixer = projected[:, :inner].astype(BF16).astype(F32)
    pad[...] = jnp.zeros_like(pad)
    sides[...] = jnp.zeros_like(sides)
    side_sum[...] = jnp.zeros_like(side_sum)
    pad[pl.ds(1, R), pl.ds(8, C), :] = mixer.reshape(R, C, inner)
    small[5].wait()

    def tap(a, b):
        return conv[pl.ds(3 * a + b, 1), :]

    own = jnp.zeros((R, C, inner), F32)
    for b in range(3):
        moved = pad[:, pl.ds(7 + b, C), :]
        for a in range(3):
            own = own + tap(a, b).reshape(1, 1, inner) * moved[a : a + R]
    inner_sum[...] = own

    for n in range(1, nc - 1):
        @pl.when(penult - j == n)
        def _(n=n):
            pl.semaphore_wait(far_sem, n)

            @pl.when(j >= 1)
            def _():
                tell_left(n)

    for load in small[:5]:
        load.wait()
    for g in range(LANES // group):
        param[0:1, g * group : (g + 1) * group] = step_bias[...]
        param[1:2, g * group : g * group + heads] = rate_a[...]
        param[1:2, g * group + heads : (g + 1) * group] = rate_d[...]
    param[2:3, 0:heads] = skip[...]
    bias = param[0:1, :]
    rate = param[1:2, :]
    loads[2].wait()
    wall[:, 0:LANES] = wbc[:, 0:LANES]
    wall[:, LANES : 2 * LANES] = jnp.concatenate([wst_t[...]] * (LANES // group), axis=0).astype(F32).T.astype(BF16)
    wall[:, 2 * LANES : 3 * LANES] = wbc[:, LANES : 2 * LANES]

    q = lax.broadcasted_iota(jnp.int32, (count, count), 0)
    k_ = lax.broadcasted_iota(jnp.int32, (count, count), 1)
    same_row = lax.div(q, C) == lax.div(k_, C)
    same_col = lax.rem(q, C) == lax.rem(k_, C)
    for n, same in enumerate((same_row, same_col)):
        masks[n, pl.ds(0, count), :] = as_mask(same & (k_ <= q))
        masks[n, pl.ds(count, count), :] = as_mask(same & (k_ > q))
        masks[n, pl.ds(2 * count, count), :] = as_mask(same)
        same_f[n] = jnp.where(same, 1.0, 0.0)
        upto_f[n] = jnp.where(same & (k_ <= q), 1.0, 0.0)
    p_d = lax.broadcasted_iota(jnp.int32, (BATCH * count, BATCH * count), 0)
    o_d = lax.broadcasted_iota(jnp.int32, (BATCH * count, BATCH * count), 1)
    near_d = lax.rem(p_d, C) == lax.rem(o_d, C)
    mask_d[pl.ds(0, BATCH * count), :] = as_mask(near_d & (o_d > p_d))
    mask_d[pl.ds(BATCH * count, count), :] = as_mask(near_d[:count])
    stacked = last * LENGTHS[-1] * STRIP
    p_a = lax.broadcasted_iota(jnp.int32, (stacked, stacked), 0)
    o_a = lax.broadcasted_iota(jnp.int32, (stacked, stacked), 1)
    p_q = lax.broadcasted_iota(jnp.int32, same_a.shape[1:], 0)
    o_q = lax.broadcasted_iota(jnp.int32, same_a.shape[1:], 1)
    for n, length in enumerate(LENGTHS):
        size = length * STRIP
        near_a = lax.div(lax.rem(p_a, size), C) == lax.div(lax.rem(o_a, size), C)
        mask_a[n] = as_mask(near_a & (o_a > p_a))
        near_q = lax.div(lax.rem(p_q, size), C) == lax.div(lax.rem(o_q, size), C)
        same_a[n] = jnp.where(near_q, 1.0, 0.0)
    spot = lax.broadcasted_iota(jnp.int32, (LANES, inner), 0)
    head = lax.div(lax.broadcasted_iota(jnp.int32, (LANES, inner), 1), width)
    for n in range(2):
        row = head + n * heads
        spread_r[n] = as_mask((spot == row) | (spot == row + group))
    lane_from = lax.broadcasted_iota(jnp.int32, (inner, inner), 0)
    lane_to = lax.broadcasted_iota(jnp.int32, (inner, inner), 1)
    pairs = width * state // LANES
    half_size = pairs * heads
    parity = lax.div(lane_from, half_size)
    pair = lax.div(lax.rem(lane_from, half_size), heads)
    moves_r[...] = as_mask(lax.rem(lane_from, heads) * width + 2 * pair + parity == lane_to)
    loads[3].wait()
    for c in range(C):
        for n in range(pairs):
            top_r[pl.ds(n * heads, heads), c * LANES : (c + 1) * LANES] = top[c, :, n * LANES : (n + 1) * LANES]

    lane = lax.broadcasted_iota(jnp.int32, (count, LANES), 1)
    low_lanes = lax.rem(lax.div(lax.broadcasted_iota(jnp.int32, (1, LANES), 1), group), 2) == 1

    def halves_of(x):
        return jnp.where(low_lanes, x - x.astype(BF16).astype(F32), x).astype(BF16)

    def masked_sum(mask, x):
        r = dot(mask, x)
        return r + pltpu.roll(r, group, 1)

    for k in range(8):
        @pl.when(exists(k))
        def _(k=k):
            if k >= CORNERS:
                piece = corner.at[pl.ds(0, STRIP)]
                place = far_corner.at[pl.ds((k - CORNERS) * STRIP, STRIP)]
            else:
                piece = edge.at[pl.ds(0, STRIP)]
                place = halo.at[pl.ds(k * STRIP, STRIP)]
            pltpu.make_async_remote_copy(
                src_ref=piece,
                dst_ref=place,
                send_sem=hs_sem.at[k],
                recv_sem=hr_sem.at[k],
                device_id=target(k),
                device_id_type=mesh,
            ).wait_recv()

    packed = far_corner[...].astype(F32)
    rows = [
        jnp.concatenate(
            [packed[t * STRIP + n : t * STRIP + n + 1] for n in range(tok.shape[1] // LANES)], axis=1
        )
        for t in range(CORNERS)
    ]
    rows.append(jnp.zeros((STRIP - CORNERS, tok.shape[1]), F32))
    halo[pl.ds(4 * STRIP, STRIP), :] = jnp.concatenate(rows, axis=0).astype(BF16)
    halo_f[...] = dot(halo[...], win[:, :inner]).astype(BF16).astype(F32)

    def halo_rows(k, first, n):
        return halo_f[pl.ds(k * STRIP + first, n), :]

    pad[0, pl.ds(8, C), :] = halo_rows(0, STRIP - C, C)
    pad[R + 1, pl.ds(8, C), :] = halo_rows(1, 0, C)
    pad[0, pl.ds(7, 1), :] = halo_rows(4, 0, 1)
    pad[0, pl.ds(8 + C, 1), :] = halo_rows(4, 1, 1)
    pad[R + 1, pl.ds(7, 1), :] = halo_rows(4, 2, 1)
    pad[R + 1, pl.ds(8 + C, 1), :] = halo_rows(4, 3, 1)
    for n in range(2):
        sides[n, pl.ds(8, R), :] = halo_rows(2 + n, 0, R)
        side = sum(tap(a, 2 * n) * sides[n, pl.ds(7 + a, R), :] for a in range(3))
        for r in range(R):
            side_sum[r, pl.ds(n * (C - 1), 1), :] = side[r : r + 1]
    small[6].wait()
    for a, r in ((0, 0), (2, R - 1)):
        inner_sum[r] += sum(tap(a, b) * pad[r + a, pl.ds(7 + b, C), :] for b in range(3))
    def chunk_a(buffer, slot, c):
        rows = pl.ds(PIECES[c][0] * STRIP, PIECES[c][1] * STRIP)
        return buffer.at[rows] if slot is None else buffer.at[slot, rows]

    def send_a(d, c):
        return pltpu.make_async_remote_copy(
            src_ref=chunk_a(vals, None, c), dst_ref=chunk_a(rva, j, c), send_sem=as_sem.at[d, c],
            recv_sem=ar_sem.at[j, c], device_id={"cols": j + d}, device_id_type=mesh,
        )

    def arrival_a(slot, c):
        return pltpu.make_async_remote_copy(
            src_ref=chunk_a(vals, None, c), dst_ref=chunk_a(rva, slot, c), send_sem=as_sem.at[0, c],
            recv_sem=ar_sem.at[slot, c], device_id={"cols": slot}, device_id_type=mesh,
        )

    def send_d(d):
        return pltpu.make_async_remote_copy(
            src_ref=vals, dst_ref=rvd.at[i], send_sem=ds_sem.at[d], recv_sem=dr_sem.at[i],
            device_id={"rows": i + d}, device_id_type=mesh,
        )

    def sends_d(d):
        return (i + d < nr) & (lax.rem(i, 2) == 0) if d == 1 else i + d < nr

    hops_d = [1] + list(range(2, nr, 2))
    sibling = i + 1 - 2 * lax.rem(i, 2)

    def relay_d(slot):
        return pltpu.make_async_remote_copy(
            src_ref=rvd.at[slot], dst_ref=rvd.at[slot], send_sem=rl_sem.at[slot],
            recv_sem=dr_sem.at[slot], device_id={"rows": sibling}, device_id_type=mesh,
        )

    def arrival_d(slot):
        return pltpu.make_async_remote_copy(
            src_ref=vals, dst_ref=rvd.at[slot], send_sem=ds_sem.at[0],
            recv_sem=dr_sem.at[slot], device_id={"rows": slot}, device_id_type=mesh,
        )

    query = pltpu.make_async_remote_copy(
        src_ref=cbuf.at[pl.ds(0, count)], dst_ref=cbuf.at[pl.ds(count, count)], send_sem=q_sem.at[0],
        recv_sem=q_sem.at[1], device_id={"cols": j - 1}, device_id_type=mesh,
    )
    def answer(c):
        return pltpu.make_async_remote_copy(
            src_ref=chunk_a(ysend, None, c), dst_ref=chunk_a(yrecv, None, c), send_sem=ys_sem.at[c],
            recv_sem=yr_sem.at[c], device_id={"cols": j + 1}, device_id_type=mesh,
        )

    def furthest(c):
        return penult if c < ADDED else last

    for c, (first, length) in enumerate(PIECES):
        grid_rows = pl.ds(first * STRIP // C, length * STRIP // C)
        summed = inner_sum[grid_rows] + side_sum[grid_rows]
        vals[pl.ds(first * STRIP, length * STRIP), :] = silu(summed).reshape(length * STRIP, inner).astype(BF16)
        for d in range(1, nc) if c > 1 else range(nc - 1, 0, -1):
            @pl.when(j + d <= furthest(c))
            def _(d=d, c=c):
                send_a(d, c).start()

    for d in hops_d[1:] + hops_d[:1]:
        @pl.when(sends_d(d))
        def _(d=d):
            send_d(d).start()

    full = dot(vals[...], wall[...])
    values_f = vals[...].astype(F32)
    map_a = full[:, :LANES]
    map_d = full[:, 2 * LANES :]
    c_a = jnp.where(lane < state, pltpu.roll(map_a, state, 1), 0.0).astype(BF16)
    c_d = jnp.where(lane < state, pltpu.roll(map_d, state, 1), 0.0).astype(BF16)
    cbuf[pl.ds(0, count), :] = c_a

    @pl.when(j == last)
    def _():
        query.start()

    steps = softplus(full[:, LANES : 2 * LANES] + bias)
    log_decay = halves_of(-steps * rate)
    cum_a = masked_sum(masks[0, pl.ds(0, count), :], log_decay)
    cum_d = masked_sum(masks[1, pl.ds(0, count), :], log_decay)
    score_a = dot_nt(c_a, map_a.astype(BF16)) * upto_f[0]
    score_d = dot_nt(c_d, map_d.astype(BF16)) * upto_f[1]
    step_halves = halves_of(steps)
    weighted[pl.ds(0, count), :] = (values_f * dot(step_halves, spread_r[0])).astype(BF16)
    weighted[pl.ds(count, count), :] = (values_f * dot(step_halves, spread_r[1])).astype(BF16)
    cum_at = cum_a.T
    cum_dt = cum_d.T
    per_group = LANES // width
    for g in range(inner // LANES):
        total = jnp.zeros((count, LANES), F32)
        for e in range(per_group):
            h = g * per_group + e
            diff_a = cum_a[:, h : h + 1] - cum_at[h : h + 1, :]
            hd = heads + h
            diff_d = cum_d[:, hd : hd + 1] - cum_dt[hd : hd + 1, :]
            mix_a = (jnp.exp(jnp.minimum(diff_a, 0.0)) * score_a).astype(BF16)
            mix_d = (jnp.exp(jnp.minimum(diff_d, 0.0)) * score_d).astype(BF16)
            mix = jnp.concatenate([mix_a, mix_d], axis=1)
            part = dot(mix, weighted[:, g * LANES : (g + 1) * LANES])
            total = jnp.where(lax.div(lane, width) == e, part, total)
        y_ref[:, g * LANES : (g + 1) * LANES] = total

    column = lax.rem(q, C)
    c_low = c_d.astype(F32)
    c_high = pltpu.roll(c_low, state, 1)
    picked = jnp.concatenate(
        [
            jnp.concatenate([jnp.where(column == c, h, 0.0).astype(BF16) for c in range(C)], axis=1)
            for h in (c_low, c_high)
        ],
        axis=0,
    )
    halves = dot_nt(picked, top_r[...])
    acc_d[...] = dot(
        jnp.concatenate([halves[:count], halves[count:]], axis=1).astype(BF16), moves_r[...]
    )
    grow_a[...] = dot(halves_of(jnp.exp(cum_a)), spread_r[0])
    grow_d[...] = dot(halves_of(jnp.exp(cum_d)), spread_r[1])
    skips = dot(halves_of(jnp.broadcast_to(param[2:3, :], (count, LANES))), spread_r[0])
    y_ref[...] += skips * vals[...].astype(F32)

    def leaving(n, steps, log_decay):
        r = masked_sum(masks[n, pl.ds(count, 2 * count), :], log_decay)
        weight = halves_of(steps * jnp.exp(r[:count]))
        whole = halves_of(jnp.exp(r[count:]))
        return dot(jnp.concatenate([weight, whole], axis=0), spread_r[n])

    def across(slot):
        block = rva[slot]
        made = dot(block, wall[:, : 2 * LANES])
        s = softplus(made[:, LANES:] + bias)
        e = leaving(0, s, halves_of(-s * rate))
        entry = (block.astype(F32) * e[:count]).astype(BF16)
        score = dot_nt(cbuf[pl.ds(0, count), :], made[:, :LANES].astype(BF16)) * same_f[0]
        rows = pl.ds(0, count)
        acc_a[rows, :] = acc_a[rows, :] * e[count:] + dot(score.astype(BF16), entry)

    def down(first, m):
        total = m * count
        block = rvd[pl.ds(first, m)].reshape(total, inner)
        made = dot(block, wall[:, LANES:])
        s = softplus(made[:, :LANES] + bias)
        mask = jnp.concatenate(
            [mask_d[pl.ds(0, total), :total], mask_d[pl.ds(BATCH * count, count), :total]], axis=0
        )
        r = masked_sum(mask, halves_of(-s * rate))
        weight = halves_of(s * jnp.exp(r[:total]))
        whole = halves_of(jnp.exp(r[total:]))
        e = dot(jnp.concatenate([weight, whole], axis=0), spread_r[1])
        entry = (block.astype(F32) * e[:total]).astype(BF16)
        score = dot_nt(c_d, made[:, LANES:].astype(BF16))
        near = jnp.concatenate([same_f[1]] * m, axis=1)
        acc_d[...] = acc_d[...] * e[total:] + dot((score * near).astype(BF16), entry)

    def left(c, blocks, added):
        first, size = PIECES[c][0] * STRIP, PIECES[c][1] * STRIP
        kind = LENGTHS.index(PIECES[c][1])
        rows = pl.ds(first, size)
        total = blocks * size
        block = rva[pl.ds(0, blocks), rows, :].reshape(total, inner)
        made = dot(block, wall[:, : 2 * LANES])
        s = softplus(made[:, LANES:] + bias)
        r = masked_sum(mask_a[kind, pl.ds(0, total), :total], halves_of(-s * rate))
        e = dot(halves_of(s * jnp.exp(r)), spread_r[0])
        entry = (block.astype(F32) * e).astype(BF16)
        queries = cbuf[rows, :]
        if added:
            queries = jnp.concatenate([queries, cbuf[pl.ds(count + first, size), :]], axis=0)
        near = same_a[kind, pl.ds(0, queries.shape[0]), :total]
        score = dot_nt(queries, made[:, :LANES].astype(BF16)) * near
        part = dot(score.astype(BF16), entry)
        if added:
            ysend[rows, :] = (part[size:] * exit_d[rows, :] + exit_y[rows, :]).astype(BF16)
            answer(c).start()
        acc_a[rows, :] = part[:size]

    acc_a[...] = jnp.zeros_like(acc_a)
    loads[4].wait()

    @pl.when(j == penult)
    def _():
        e = leaving(0, steps, log_decay)
        entry = (vals[...].astype(F32) * e[:count]).astype(BF16)
        exit_d[...] = e[count:]
        query.wait_recv()
        score = dot_nt(cbuf[pl.ds(count, count), :], map_a.astype(BF16)) * same_f[0]
        exit_y[...] = dot(score.astype(BF16), entry)

    def pass_on(t, carry):
        slot = lax.rem(i, 2) + 2 * t
        arrival_d(slot).wait_recv()
        relay_d(slot).start()
        return carry

    straight = lax.div(i, 2)

    @pl.when(j != penult)
    def _():
        lax.fori_loop(0, straight, pass_on, 0)

    @pl.when(j == penult)
    def _():
        for c in range(ADDED):
            if c == ADDED - 1:
                lax.fori_loop(0, straight, pass_on, 0)
            for slot in range(before):
                arrival_a(slot, c).wait_recv()
            left(c, before, True)

    def batch(b, carry):
        first = b * BATCH
        for m in range(BATCH):
            @pl.when((first + m < i) & (lax.rem(first + m + i, 2) == 1))
            def _(m=m):
                arrival_d(first + m).wait_recv()
        for m in range(1, BATCH + 1):
            @pl.when(i - first == m if m < BATCH else i - first >= m)
            def _(m=m):
                down(first, m)
        return carry

    lax.fori_loop(0, lax.div(i + BATCH - 1, BATCH), batch, 0)

    @pl.when(j == penult)
    def _():
        for c in range(ADDED, CHUNKS):
            for slot in range(before):
                arrival_a(slot, c).wait_recv()
            left(c, before, False)

    @pl.when(j < penult)
    def _():
        def hop(slot, carry):
            for c in range(CHUNKS):
                arrival_a(slot, c).wait_recv()
            across(slot)
            return carry

        lax.fori_loop(0, j, hop, 0)

    y_ref[...] = (y_ref[...] + grow_d[...] * acc_d[...]) * gate[...]
    grow_a[...] = grow_a[...] * gate[...]

    @pl.when(j == last)
    def _():
        for c in range(ADDED, CHUNKS):
            for slot in range(last):
                arrival_a(slot, c).wait_recv()
            left(c, last, False)
        for c in range(ADDED):
            answer(c).wait_recv()
        rows = pl.ds(0, PIECES[ADDED][0] * STRIP)
        acc_a[rows, :] = yrecv[rows, :].astype(F32)

    gated = y_ref[...] + grow_a[...] * acc_a[...]
    scale = lax.rsqrt(jnp.mean(gated * gated, axis=-1, keepdims=True) + 1e-05)
    out[...] = (dot((gated * gain[...]).astype(BF16), wout[...]) * scale).astype(BF16)

    for k in range(8):
        @pl.when(exists(k))
        def _(k=k):
            halo_copy(k).wait_send()
    for c in range(CHUNKS):
        for d in range(1, nc):
            @pl.when(j + d <= furthest(c))
            def _(d=d, c=c):
                send_a(d, c).wait_send()

    for d in hops_d:
        @pl.when(sends_d(d))
        def _(d=d):
            send_d(d).wait_send()

    def passed_on(t, carry):
        relay_d(lax.rem(i, 2) + 2 * t).wait_send()
        return carry

    lax.fori_loop(0, straight, passed_on, 0)

    @pl.when(j == last)
    def _():
        query.wait_send()

    @pl.when(j == penult)
    def _():
        for c in range(ADDED):
            answer(c).wait_send()


def shards(
    nr, nc,
    tokens, top_state, in_weight, conv_weight, bc_weight, step_weight, step_bias,
    across_rate, down_rate, skip_gain, norm_gain, out_weight,
):
    R, C, model = tokens.shape
    inner = out_weight.shape[0]
    heads = across_rate.shape[0]
    count = R * C
    vmem = pl.BlockSpec(memory_space=pltpu.VMEM)
    stacked = (nc - 1) * LENGTHS[-1] * STRIP
    result = pl.pallas_call(
        functools.partial(kernel, nr, nc, R, C, heads),
        out_shape=jax.ShapeDtypeStruct((count, model), BF16),
        in_specs=[pl.BlockSpec(memory_space=pltpu.HBM)] * 12,
        out_specs=vmem,
        scratch_shapes=[
            pltpu.VMEM(conv_weight.shape, F32),
            pltpu.VMEM((2 * heads, inner), BF16),
            pltpu.VMEM((1, 2 * heads), F32),
            pltpu.VMEM((1, heads), F32),
            pltpu.VMEM((1, heads), F32),
            pltpu.VMEM((1, heads), F32),
            pltpu.VMEM((1, inner), F32),
            pltpu.VMEM((count, model), BF16),
            pltpu.VMEM(top_state.shape, BF16),
            pltpu.VMEM(in_weight.shape, BF16),
            pltpu.VMEM(bc_weight.shape, BF16),
            pltpu.VMEM(out_weight.shape, BF16),
            pltpu.VMEM((inner, 3 * LANES), BF16),
            pltpu.VMEM((8, LANES), F32),
            pltpu.VMEM((2 * R, model), BF16),
            pltpu.VMEM((5 * STRIP, model), BF16),
            pltpu.VMEM((5 * STRIP, inner), F32),
            pltpu.VMEM((R + 2, 24, inner), F32),
            pltpu.VMEM((R, C, inner), F32),
            pltpu.VMEM((2, R + 16, inner), F32),
            pltpu.VMEM((R, C, inner), F32),
            pltpu.VMEM((count, inner), F32),
            pltpu.VMEM((count, inner), BF16),
            pltpu.VMEM((nc, count, inner), BF16),
            pltpu.VMEM((nr, count, inner), BF16),
            pltpu.VMEM((count, inner), F32),
            pltpu.VMEM((count, inner), F32),
            pltpu.VMEM((2 * count, inner), BF16),
            pltpu.VMEM((count, inner), F32),
            pltpu.VMEM((2, 3 * count, count), BF16),
            pltpu.VMEM(((BATCH + 1) * count, BATCH * count), BF16),
            pltpu.VMEM((len(LENGTHS), stacked, stacked), BF16),
            pltpu.VMEM((len(LENGTHS), 2 * LENGTHS[-1] * STRIP, stacked), F32),
            pltpu.VMEM((2, count, count), F32),
            pltpu.VMEM((2, count, count), F32),
            pltpu.VMEM((2, LANES, inner), BF16),
            pltpu.VMEM((inner, inner), BF16),
            pltpu.VMEM((top_state.shape[2] // LANES * heads, C * LANES), BF16),
            pltpu.VMEM((count, inner), F32),
            pltpu.VMEM((count, inner), F32),
            pltpu.VMEM((count, inner), F32),
            pltpu.VMEM((count, inner), F32),
            pltpu.VMEM((2 * count, LANES), BF16),
            pltpu.VMEM((count, inner), BF16),
            pltpu.VMEM((count, inner), BF16),
            pltpu.VMEM((CORNERS * STRIP, LANES), BF16),
            pltpu.VMEM((CORNERS * STRIP, LANES), BF16),
            pltpu.SemaphoreType.DMA((5,)),
            pltpu.SemaphoreType.DMA((7,)),
            pltpu.SemaphoreType.DMA((8,)),
            pltpu.SemaphoreType.DMA((8,)),
            pltpu.SemaphoreType.DMA((nc, CHUNKS)),
            pltpu.SemaphoreType.DMA((nc, CHUNKS)),
            pltpu.SemaphoreType.DMA((nr,)),
            pltpu.SemaphoreType.DMA((nr,)),
            pltpu.SemaphoreType.DMA((nr,)),
            pltpu.SemaphoreType.DMA((2,)),
            pltpu.SemaphoreType.DMA((CHUNKS,)),
            pltpu.SemaphoreType.DMA((CHUNKS,)),
            pltpu.SemaphoreType.REGULAR,
        ],
        compiler_params=pltpu.CompilerParams(
            collective_id=0, has_side_effects=True, vmem_limit_bytes=48000 * 1024
        ),
    )(
        *(
            pltpu.with_memory_space_constraint(x, pltpu.HBM)
            for x in (
                tokens.reshape(count, model),
                top_state,
                in_weight,
                bc_weight,
                out_weight,
                conv_weight,
                step_weight.T,
                step_bias[None],
                across_rate[None],
                down_rate[None],
                skip_gain[None],
                norm_gain[None],
            )
        )
    )
    return result.reshape(R, C, model)


def solution(mesh):
    in_specs = (
        P(("groups", "rows"), "cols", None),
        P(("groups", "cols"), None, None),
    ) + (P(),) * 10
    out_specs = P(("groups", "rows"), "cols", None)
    return jax.shard_map(
        functools.partial(shards, mesh.shape["rows"], mesh.shape["cols"]),
        mesh=mesh, in_specs=in_specs, out_specs=out_specs, check_vma=False,
    )
```

```python
import functools

import jax
import jax.numpy as jnp
from jax import lax
from jax.experimental import pallas as pl
from jax.experimental.pallas import tpu as pltpu
from jax.sharding import PartitionSpec as P

F32 = jnp.float32
BF16 = jnp.bfloat16
NEIGHBOURS = ((-1, 0), (1, 0), (0, -1), (0, 1), (-1, -1), (-1, 1), (1, -1), (1, 1))
OPPOSITE = (1, 0, 3, 2, 7, 6, 5, 4)
STRIP = 16
LANES = 128
PIECES = ((0, 2), (2, 2), (4, 2), (6, 2))
CHUNKS = len(PIECES)
ADDED = 3
LENGTHS = sorted({n for _, n in PIECES})
BATCH = 3
CORNERS = 4


def dot(a, b):
    return jnp.dot(a, b, preferred_element_type=F32)


def dot_nt(a, b):
    return lax.dot_general(a, b, (((1,), (1,)), ((), ())), preferred_element_type=F32)


def softplus(x):
    return jnp.maximum(x, 0.0) + jnp.log1p(jnp.exp(-jnp.abs(x)))


def silu(x):
    return x / (1.0 + jnp.exp(-x))


def kernel(
    nr, nc, R, C, heads,
    tok_h, top_h, win_h, wbc_h, wout_h, conv_h, wst_h, bias_h, rate_a_h, rate_d_h, skip_h, gain_h, out,
    conv, wst_t, step_bias, rate_a, rate_d, skip, gain,
    tok, top, win, wbc, wout, wall, param, edge, halo, halo_f, pad, inner_sum, sides, side_sum, gate, vals, rva, rvd, acc_a, acc_d,
    weighted, y_ref, masks, mask_d, mask_a, same_a, same_f, upto_f, spread_r, moves_r, top_r, grow_a, grow_d, exit_y, exit_d,
    cbuf, ysend, yrecv, corner, far_corner,
    ld_sem, sm_sem, hs_sem, hr_sem, as_sem, ar_sem, ds_sem, dr_sem, rl_sem, q_sem, ys_sem, yr_sem, far_sem,
):
    count = R * C
    inner = wout.shape[0]
    state = wbc.shape[1] // 4
    width = inner // heads
    group = 2 * heads
    penult, last = nc - 2, nc - 1
    before = nc - 2
    i = lax.axis_index("rows")
    j = lax.axis_index("cols")
    mesh = pl.DeviceIdType.MESH

    def exists(k):
        di, dj = NEIGHBOURS[k]
        a, b = i + di, j + dj
        return (a >= 0) & (a < nr) & (b >= 0) & (b < nc)

    def target(k):
        di, dj = NEIGHBOURS[k]
        return {"rows": i + di, "cols": j + dj}

    loads = [
        pltpu.make_async_copy(a, b, ld_sem.at[n])
        for n, (a, b) in enumerate(
            ((tok_h, tok), (win_h, win), (wbc_h, wbc), (top_h, top), (wout_h, wout))
        )
    ]
    small = [
        pltpu.make_async_copy(a, b, sm_sem.at[n])
        for n, (a, b) in enumerate(
            (
                (wst_h, wst_t), (bias_h, step_bias), (rate_a_h, rate_a), (rate_d_h, rate_d),
                (skip_h, skip), (conv_h, conv), (gain_h, gain),
            )
        )
    ]
    loads[0].start()
    loads[1].start()
    for load in small:
        load.start()
    for load in loads[2:]:
        load.start()

    barrier = pltpu.get_barrier_semaphore()
    for d in range(1, nr):
        pl.semaphore_signal(
            barrier, inc=1, device_id={"rows": lax.rem(i + d, nr)}, device_id_type=mesh
        )
    for k in range(2, 8):
        @pl.when(exists(k))
        def _(k=k):
            pl.semaphore_signal(barrier, inc=1, device_id=target(k), device_id_type=mesh)

    def as_mask(m):
        return jnp.where(m, 1.0, 0.0).astype(BF16)

    pos = lax.broadcasted_iota(jnp.int32, (2 * R, count), 0)
    src = lax.broadcasted_iota(jnp.int32, (2 * R, count), 1)
    wanted = jnp.where(pos < R, pos * C, (pos - R) * C + C - 1)
    param[...] = jnp.zeros_like(param)
    loads[0].wait()
    edge[...] = dot(as_mask(src == wanted), tok[...]).astype(BF16)
    slot_at = lax.broadcasted_iota(jnp.int32, (CORNERS * STRIP, count), 0)
    token_at = lax.broadcasted_iota(jnp.int32, (CORNERS * STRIP, count), 1)
    which = lax.div(slot_at, STRIP)
    at_corner = token_at == lax.div(which, 2) * (count - C) + lax.rem(which, 2) * (C - 1)
    corner[...] = sum(
        dot(as_mask(at_corner & (lax.rem(slot_at, STRIP) == n)), tok[:, n * LANES : (n + 1) * LANES])
        for n in range(tok.shape[1] // LANES)
    ).astype(BF16)
    around = sum(jnp.where(exists(k), 1, 0) for k in range(2, 8))
    pl.semaphore_wait(barrier, nr - 1 + around)

    def halo_copy(k):
        di, dj = NEIGHBOURS[k]
        if k >= CORNERS:
            piece = corner.at[pl.ds((k - CORNERS) * STRIP, STRIP)]
            place = far_corner.at[pl.ds((OPPOSITE[k] - CORNERS) * STRIP, STRIP)]
        else:
            if di < 0:
                piece = tok.at[pl.ds(0, STRIP)]
            elif di > 0:
                piece = tok.at[pl.ds(count - STRIP, STRIP)]
            else:
                piece = edge.at[pl.ds(0 if dj < 0 else R, STRIP)]
            place = halo.at[pl.ds(OPPOSITE[k] * STRIP, STRIP)]
        return pltpu.make_async_remote_copy(
            src_ref=piece,
            dst_ref=place,
            send_sem=hs_sem.at[k],
            recv_sem=hr_sem.at[OPPOSITE[k]],
            device_id=target(k),
            device_id_type=mesh,
        )

    for k in (4, 5, 6, 7, 2, 3, 0, 1):
        @pl.when(exists(k))
        def _(k=k):
            halo_copy(k).start()

    for k in range(8):
        @pl.when(jnp.logical_not(exists(k)))
        def _(k=k):
            if k >= CORNERS:
                far_corner[pl.ds((k - CORNERS) * STRIP, STRIP)] = jnp.zeros((STRIP, LANES), BF16)
            else:
                halo[pl.ds(k * STRIP, STRIP)] = jnp.zeros((STRIP, halo.shape[1]), BF16)

    def tell_left(amount):
        pl.semaphore_signal(far_sem, inc=amount, device_id={"cols": j - 1}, device_id_type=mesh)

    @pl.when((j >= 1) & (j <= penult))
    def _():
        tell_left(1)

    loads[1].wait()
    projected = dot(tok[...], win[...])
    gate[...] = silu(projected[:, inner:].astype(BF16).astype(F32))
    mixer = projected[:, :inner].astype(BF16).astype(F32)
    pad[...] = jnp.zeros_like(pad)
    sides[...] = jnp.zeros_like(sides)
    side_sum[...] = jnp.zeros_like(side_sum)
    pad[pl.ds(1, R), pl.ds(8, C), :] = mixer.reshape(R, C, inner)
    small[5].wait()

    def tap(a, b):
        return conv[pl.ds(3 * a + b, 1), :]

    own = jnp.zeros((R, C, inner), F32)
    for b in range(3):
        moved = pad[:, pl.ds(7 + b, C), :]
        for a in range(3):
            own = own + tap(a, b).reshape(1, 1, inner) * moved[a : a + R]
    inner_sum[...] = own

    for n in range(1, nc - 1):
        @pl.when(penult - j == n)
        def _(n=n):
            pl.semaphore_wait(far_sem, n)

            @pl.when(j >= 1)
            def _():
                tell_left(n)

    for load in small[:5]:
        load.wait()
    for g in range(LANES // group):
        param[0:1, g * group : (g + 1) * group] = step_bias[...]
        param[1:2, g * group : g * group + heads] = rate_a[...]
        param[1:2, g * group + heads : (g + 1) * group] = rate_d[...]
    param[2:3, 0:heads] = skip[...]
    bias = param[0:1, :]
    rate = param[1:2, :]
    loads[2].wait()
    wall[:, 0:LANES] = wbc[:, 0:LANES]
    wall[:, LANES : 2 * LANES] = jnp.concatenate([wst_t[...]] * (LANES // group), axis=0).astype(F32).T.astype(BF16)
    wall[:, 2 * LANES : 3 * LANES] = wbc[:, LANES : 2 * LANES]

    q = lax.broadcasted_iota(jnp.int32, (count, count), 0)
    k_ = lax.broadcasted_iota(jnp.int32, (count, count), 1)
    same_row = lax.div(q, C) == lax.div(k_, C)
    same_col = lax.rem(q, C) == lax.rem(k_, C)
    for n, same in enumerate((same_row, same_col)):
        masks[n, pl.ds(0, count), :] = as_mask(same & (k_ <= q))
        masks[n, pl.ds(count, count), :] = as_mask(same & (k_ > q))
        masks[n, pl.ds(2 * count, count), :] = as_mask(same)
        same_f[n] = jnp.where(same, 1.0, 0.0)
        upto_f[n] = jnp.where(same & (k_ <= q), 1.0, 0.0)
    p_d = lax.broadcasted_iota(jnp.int32, (BATCH * count, BATCH * count), 0)
    o_d = lax.broadcasted_iota(jnp.int32, (BATCH * count, BATCH * count), 1)
    near_d = lax.rem(p_d, C) == lax.rem(o_d, C)
    mask_d[pl.ds(0, BATCH * count), :] = as_mask(near_d & (o_d > p_d))
    mask_d[pl.ds(BATCH * count, count), :] = as_mask(near_d[:count])
    stacked = last * LENGTHS[-1] * STRIP
    p_a = lax.broadcasted_iota(jnp.int32, (stacked, stacked), 0)
    o_a = lax.broadcasted_iota(jnp.int32, (stacked, stacked), 1)
    p_q = lax.broadcasted_iota(jnp.int32, same_a.shape[1:], 0)
    o_q = lax.broadcasted_iota(jnp.int32, same_a.shape[1:], 1)
    for n, length in enumerate(LENGTHS):
        size = length * STRIP
        near_a = lax.div(lax.rem(p_a, size), C) == lax.div(lax.rem(o_a, size), C)
        mask_a[n] = as_mask(near_a & (o_a > p_a))
        near_q = lax.div(lax.rem(p_q, size), C) == lax.div(lax.rem(o_q, size), C)
        same_a[n] = jnp.where(near_q, 1.0, 0.0)
    spot = lax.broadcasted_iota(jnp.int32, (LANES, inner), 0)
    head = lax.div(lax.broadcasted_iota(jnp.int32, (LANES, inner), 1), width)
    for n in range(2):
        row = head + n * heads
        spread_r[n] = as_mask((spot == row) | (spot == row + group))
    lane_from = lax.broadcasted_iota(jnp.int32, (inner, inner), 0)
    lane_to = lax.broadcasted_iota(jnp.int32, (inner, inner), 1)
    pairs = width * state // LANES
    half_size = pairs * heads
    parity = lax.div(lane_from, half_size)
    pair = lax.div(lax.rem(lane_from, half_size), heads)
    moves_r[...] = as_mask(lax.rem(lane_from, heads) * width + 2 * pair + parity == lane_to)
    loads[3].wait()
    for c in range(C):
        for n in range(pairs):
            top_r[pl.ds(n * heads, heads), c * LANES : (c + 1) * LANES] = top[c, :, n * LANES : (n + 1) * LANES]

    lane = lax.broadcasted_iota(jnp.int32, (count, LANES), 1)
    low_lanes = lax.rem(lax.div(lax.broadcasted_iota(jnp.int32, (1, LANES), 1), group), 2) == 1

    def halves_of(x):
        return jnp.where(low_lanes, x - x.astype(BF16).astype(F32), x).astype(BF16)

    def masked_sum(mask, x):
        r = dot(mask, x)
        return r + pltpu.roll(r, group, 1)

    for k in range(8):
        @pl.when(exists(k))
        def _(k=k):
            if k >= CORNERS:
                piece = corner.at[pl.ds(0, STRIP)]
                place = far_corner.at[pl.ds((k - CORNERS) * STRIP, STRIP)]
            else:
                piece = edge.at[pl.ds(0, STRIP)]
                place = halo.at[pl.ds(k * STRIP, STRIP)]
            pltpu.make_async_remote_copy(
                src_ref=piece,
                dst_ref=place,
                send_sem=hs_sem.at[k],
                recv_sem=hr_sem.at[k],
                device_id=target(k),
                device_id_type=mesh,
            ).wait_recv()

    packed = far_corner[...].astype(F32)
    rows = [
        jnp.concatenate(
            [packed[t * STRIP + n : t * STRIP + n + 1] for n in range(tok.shape[1] // LANES)], axis=1
        )
        for t in range(CORNERS)
    ]
    rows.append(jnp.zeros((STRIP - CORNERS, tok.shape[1]), F32))
    halo[pl.ds(4 * STRIP, STRIP), :] = jnp.concatenate(rows, axis=0).astype(BF16)
    halo_f[...] = dot(halo[...], win[:, :inner]).astype(BF16).astype(F32)

    def halo_rows(k, first, n):
        return halo_f[pl.ds(k * STRIP + first, n), :]

    pad[0, pl.ds(8, C), :] = halo_rows(0, STRIP - C, C)
    pad[R + 1, pl.ds(8, C), :] = halo_rows(1, 0, C)
    pad[0, pl.ds(7, 1), :] = halo_rows(4, 0, 1)
    pad[0, pl.ds(8 + C, 1), :] = halo_rows(4, 1, 1)
    pad[R + 1, pl.ds(7, 1), :] = halo_rows(4, 2, 1)
    pad[R + 1, pl.ds(8 + C, 1), :] = halo_rows(4, 3, 1)
    for n in range(2):
        sides[n, pl.ds(8, R), :] = halo_rows(2 + n, 0, R)
        side = sum(tap(a, 2 * n) * sides[n, pl.ds(7 + a, R), :] for a in range(3))
        for r in range(R):
            side_sum[r, pl.ds(n * (C - 1), 1), :] = side[r : r + 1]
    small[6].wait()
    for a, r in ((0, 0), (2, R - 1)):
        inner_sum[r] += sum(tap(a, b) * pad[r + a, pl.ds(7 + b, C), :] for b in range(3))
    def chunk_a(buffer, slot, c):
        rows = pl.ds(PIECES[c][0] * STRIP, PIECES[c][1] * STRIP)
        return buffer.at[rows] if slot is None else buffer.at[slot, rows]

    def send_a(d, c):
        return pltpu.make_async_remote_copy(
            src_ref=chunk_a(vals, None, c), dst_ref=chunk_a(rva, j, c), send_sem=as_sem.at[d, c],
            recv_sem=ar_sem.at[j, c], device_id={"cols": j + d}, device_id_type=mesh,
        )

    def arrival_a(slot, c):
        return pltpu.make_async_remote_copy(
            src_ref=chunk_a(vals, None, c), dst_ref=chunk_a(rva, slot, c), send_sem=as_sem.at[0, c],
            recv_sem=ar_sem.at[slot, c], device_id={"cols": slot}, device_id_type=mesh,
        )

    def send_d(d):
        return pltpu.make_async_remote_copy(
            src_ref=vals, dst_ref=rvd.at[i], send_sem=ds_sem.at[d], recv_sem=dr_sem.at[i],
            device_id={"rows": i + d}, device_id_type=mesh,
        )

    def sends_d(d):
        return (i + d < nr) & (lax.rem(i, 2) == 0) if d == 1 else i + d < nr

    hops_d = [1] + list(range(2, nr, 2))
    sibling = i + 1 - 2 * lax.rem(i, 2)

    def relay_d(slot):
        return pltpu.make_async_remote_copy(
            src_ref=rvd.at[slot], dst_ref=rvd.at[slot], send_sem=rl_sem.at[slot],
            recv_sem=dr_sem.at[slot], device_id={"rows": sibling}, device_id_type=mesh,
        )

    def arrival_d(slot):
        return pltpu.make_async_remote_copy(
            src_ref=vals, dst_ref=rvd.at[slot], send_sem=ds_sem.at[0],
            recv_sem=dr_sem.at[slot], device_id={"rows": slot}, device_id_type=mesh,
        )

    query = pltpu.make_async_remote_copy(
        src_ref=cbuf.at[pl.ds(0, count)], dst_ref=cbuf.at[pl.ds(count, count)], send_sem=q_sem.at[0],
        recv_sem=q_sem.at[1], device_id={"cols": j - 1}, device_id_type=mesh,
    )
    def answer(c):
        return pltpu.make_async_remote_copy(
            src_ref=chunk_a(ysend, None, c), dst_ref=chunk_a(yrecv, None, c), send_sem=ys_sem.at[c],
            recv_sem=yr_sem.at[c], device_id={"cols": j + 1}, device_id_type=mesh,
        )

    def furthest(c):
        return penult if c < ADDED else last

    for c, (first, length) in enumerate(PIECES):
        grid_rows = pl.ds(first * STRIP // C, length * STRIP // C)
        summed = inner_sum[grid_rows] + side_sum[grid_rows]
        vals[pl.ds(first * STRIP, length * STRIP), :] = silu(summed).reshape(length * STRIP, inner).astype(BF16)
        for d in range(1, nc) if c > 1 else range(nc - 1, 0, -1):
            @pl.when(j + d <= furthest(c))
            def _(d=d, c=c):
                send_a(d, c).start()

    for d in hops_d[1:] + hops_d[:1]:
        @pl.when(sends_d(d))
        def _(d=d):
            send_d(d).start()

    full = dot(vals[...], wall[...])
    values_f = vals[...].astype(F32)
    map_a = full[:, :LANES]
    map_d = full[:, 2 * LANES :]
    c_a = jnp.where(lane < state, pltpu.roll(map_a, state, 1), 0.0).astype(BF16)
    c_d = jnp.where(lane < state, pltpu.roll(map_d, state, 1), 0.0).astype(BF16)
    cbuf[pl.ds(0, count), :] = c_a

    @pl.when(j == last)
    def _():
        query.start()

    steps = softplus(full[:, LANES : 2 * LANES] + bias)
    log_decay = halves_of(-steps * rate)
    cum_a = masked_sum(masks[0, pl.ds(0, count), :], log_decay)
    cum_d = masked_sum(masks[1, pl.ds(0, count), :], log_decay)
    score_a = dot_nt(c_a, map_a.astype(BF16)) * upto_f[0]
    score_d = dot_nt(c_d, map_d.astype(BF16)) * upto_f[1]
    step_halves = halves_of(steps)
    weighted[pl.ds(0, count), :] = (values_f * dot(step_halves, spread_r[0])).astype(BF16)
    weighted[pl.ds(count, count), :] = (values_f * dot(step_halves, spread_r[1])).astype(BF16)
    cum_at = cum_a.T
    cum_dt = cum_d.T
    per_group = LANES // width
    for g in range(inner // LANES):
        total = jnp.zeros((count, LANES), F32)
        for e in range(per_group):
            h = g * per_group + e
            diff_a = cum_a[:, h : h + 1] - cum_at[h : h + 1, :]
            hd = heads + h
            diff_d = cum_d[:, hd : hd + 1] - cum_dt[hd : hd + 1, :]
            mix_a = (jnp.exp(jnp.minimum(diff_a, 0.0)) * score_a).astype(BF16)
            mix_d = (jnp.exp(jnp.minimum(diff_d, 0.0)) * score_d).astype(BF16)
            mix = jnp.concatenate([mix_a, mix_d], axis=1)
            part = dot(mix, weighted[:, g * LANES : (g + 1) * LANES])
            total = jnp.where(lax.div(lane, width) == e, part, total)
        y_ref[:, g * LANES : (g + 1) * LANES] = total

    column = lax.rem(q, C)
    c_low = c_d.astype(F32)
    c_high = pltpu.roll(c_low, state, 1)
    picked = jnp.concatenate(
        [
            jnp.concatenate([jnp.where(column == c, h, 0.0).astype(BF16) for c in range(C)], axis=1)
            for h in (c_low, c_high)
        ],
        axis=0,
    )
    halves = dot_nt(picked, top_r[...])
    acc_d[...] = dot(
        jnp.concatenate([halves[:count], halves[count:]], axis=1).astype(BF16), moves_r[...]
    )
    grow_a[...] = dot(halves_of(jnp.exp(cum_a)), spread_r[0])
    grow_d[...] = dot(halves_of(jnp.exp(cum_d)), spread_r[1])
    skips = dot(halves_of(jnp.broadcast_to(param[2:3, :], (count, LANES))), spread_r[0])
    y_ref[...] += skips * vals[...].astype(F32)

    def leaving(n, steps, log_decay):
        r = masked_sum(masks[n, pl.ds(count, 2 * count), :], log_decay)
        weight = halves_of(steps * jnp.exp(r[:count]))
        whole = halves_of(jnp.exp(r[count:]))
        return dot(jnp.concatenate([weight, whole], axis=0), spread_r[n])

    def across(slot):
        block = rva[slot]
        made = dot(block, wall[:, : 2 * LANES])
        s = softplus(made[:, LANES:] + bias)
        e = leaving(0, s, halves_of(-s * rate))
        entry = (block.astype(F32) * e[:count]).astype(BF16)
        score = dot_nt(cbuf[pl.ds(0, count), :], made[:, :LANES].astype(BF16)) * same_f[0]
        rows = pl.ds(0, count)
        acc_a[rows, :] = acc_a[rows, :] * e[count:] + dot(score.astype(BF16), entry)

    def down(first, m):
        total = m * count
        block = rvd[pl.ds(first, m)].reshape(total, inner)
        made = dot(block, wall[:, LANES:])
        s = softplus(made[:, :LANES] + bias)
        mask = jnp.concatenate(
            [mask_d[pl.ds(0, total), :total], mask_d[pl.ds(BATCH * count, count), :total]], axis=0
        )
        r = masked_sum(mask, halves_of(-s * rate))
        weight = halves_of(s * jnp.exp(r[:total]))
        whole = halves_of(jnp.exp(r[total:]))
        e = dot(jnp.concatenate([weight, whole], axis=0), spread_r[1])
        entry = (block.astype(F32) * e[:total]).astype(BF16)
        score = dot_nt(c_d, made[:, LANES:].astype(BF16))
        near = jnp.concatenate([same_f[1]] * m, axis=1)
        acc_d[...] = acc_d[...] * e[total:] + dot((score * near).astype(BF16), entry)

    def left(c, blocks, added):
        first, size = PIECES[c][0] * STRIP, PIECES[c][1] * STRIP
        kind = LENGTHS.index(PIECES[c][1])
        rows = pl.ds(first, size)
        total = blocks * size
        block = rva[pl.ds(0, blocks), rows, :].reshape(total, inner)
        made = dot(block, wall[:, : 2 * LANES])
        s = softplus(made[:, LANES:] + bias)
        r = masked_sum(mask_a[kind, pl.ds(0, total), :total], halves_of(-s * rate))
        e = dot(halves_of(s * jnp.exp(r)), spread_r[0])
        entry = (block.astype(F32) * e).astype(BF16)
        queries = cbuf[rows, :]
        if added:
            queries = jnp.concatenate([queries, cbuf[pl.ds(count + first, size), :]], axis=0)
        near = same_a[kind, pl.ds(0, queries.shape[0]), :total]
        score = dot_nt(queries, made[:, :LANES].astype(BF16)) * near
        part = dot(score.astype(BF16), entry)
        if added:
            ysend[rows, :] = (part[size:] * exit_d[rows, :] + exit_y[rows, :]).astype(BF16)
            answer(c).start()
        acc_a[rows, :] = part[:size]

    acc_a[...] = jnp.zeros_like(acc_a)
    loads[4].wait()

    @pl.when(j == penult)
    def _():
        e = leaving(0, steps, log_decay)
        entry = (vals[...].astype(F32) * e[:count]).astype(BF16)
        exit_d[...] = e[count:]
        query.wait_recv()
        score = dot_nt(cbuf[pl.ds(count, count), :], map_a.astype(BF16)) * same_f[0]
        exit_y[...] = dot(score.astype(BF16), entry)

    def pass_on(t, carry):
        slot = lax.rem(i, 2) + 2 * t
        arrival_d(slot).wait_recv()
        relay_d(slot).start()
        return carry

    straight = lax.div(i, 2)

    @pl.when(j != penult)
    def _():
        lax.fori_loop(0, straight, pass_on, 0)

    @pl.when(j == penult)
    def _():
        for c in range(ADDED):
            if c == ADDED - 1:
                lax.fori_loop(0, straight, pass_on, 0)
            for slot in range(before):
                arrival_a(slot, c).wait_recv()
            left(c, before, True)

    def batch(b, carry):
        first = b * BATCH
        for m in range(BATCH):
            @pl.when((first + m < i) & (lax.rem(first + m + i, 2) == 1))
            def _(m=m):
                arrival_d(first + m).wait_recv()
        for m in range(1, BATCH + 1):
            @pl.when(i - first == m if m < BATCH else i - first >= m)
            def _(m=m):
                down(first, m)
        return carry

    lax.fori_loop(0, lax.div(i + BATCH - 1, BATCH), batch, 0)

    @pl.when(j == penult)
    def _():
        for c in range(ADDED, CHUNKS):
            for slot in range(before):
                arrival_a(slot, c).wait_recv()
            left(c, before, False)

    @pl.when(j < penult)
    def _():
        def hop(slot, carry):
            for c in range(CHUNKS):
                arrival_a(slot, c).wait_recv()
            across(slot)
            return carry

        lax.fori_loop(0, j, hop, 0)

    y_ref[...] = (y_ref[...] + grow_d[...] * acc_d[...]) * gate[...]
    grow_a[...] = grow_a[...] * gate[...]

    def finish(first, size, across_sum):
        rows = pl.ds(first, size)
        gated = y_ref[rows, :] + grow_a[rows, :] * across_sum[rows, :].astype(F32)
        scale = lax.rsqrt(jnp.mean(gated * gated, axis=-1, keepdims=True) + 1e-05)
        out[rows, :] = (dot((gated * gain[...]).astype(BF16), wout[...]) * scale).astype(BF16)

    @pl.when(j != last)
    def _():
        finish(0, count, acc_a)

    @pl.when(j == last)
    def _():
        for c in range(ADDED, CHUNKS):
            for slot in range(last):
                arrival_a(slot, c).wait_recv()
            left(c, last, False)
        for c in range(ADDED - 1):
            answer(c).wait_recv()
        final, after = PIECES[ADDED - 1][0] * STRIP, PIECES[ADDED][0] * STRIP
        finish(0, final, yrecv)
        finish(after, count - after, acc_a)
        answer(ADDED - 1).wait_recv()
        finish(final, after - final, yrecv)

    for k in range(8):
        @pl.when(exists(k))
        def _(k=k):
            halo_copy(k).wait_send()
    for c in range(CHUNKS):
        for d in range(1, nc):
            @pl.when(j + d <= furthest(c))
            def _(d=d, c=c):
                send_a(d, c).wait_send()

    for d in hops_d:
        @pl.when(sends_d(d))
        def _(d=d):
            send_d(d).wait_send()

    def passed_on(t, carry):
        relay_d(lax.rem(i, 2) + 2 * t).wait_send()
        return carry

    lax.fori_loop(0, straight, passed_on, 0)

    @pl.when(j == last)
    def _():
        query.wait_send()

    @pl.when(j == penult)
    def _():
        for c in range(ADDED):
            answer(c).wait_send()


def shards(
    nr, nc,
    tokens, top_state, in_weight, conv_weight, bc_weight, step_weight, step_bias,
    across_rate, down_rate, skip_gain, norm_gain, out_weight,
):
    R, C, model = tokens.shape
    inner = out_weight.shape[0]
    heads = across_rate.shape[0]
    count = R * C
    vmem = pl.BlockSpec(memory_space=pltpu.VMEM)
    stacked = (nc - 1) * LENGTHS[-1] * STRIP
    result = pl.pallas_call(
        functools.partial(kernel, nr, nc, R, C, heads),
        out_shape=jax.ShapeDtypeStruct((count, model), BF16),
        in_specs=[pl.BlockSpec(memory_space=pltpu.HBM)] * 12,
        out_specs=vmem,
        scratch_shapes=[
            pltpu.VMEM(conv_weight.shape, F32),
            pltpu.VMEM((2 * heads, inner), BF16),
            pltpu.VMEM((1, 2 * heads), F32),
            pltpu.VMEM((1, heads), F32),
            pltpu.VMEM((1, heads), F32),
            pltpu.VMEM((1, heads), F32),
            pltpu.VMEM((1, inner), F32),
            pltpu.VMEM((count, model), BF16),
            pltpu.VMEM(top_state.shape, BF16),
            pltpu.VMEM(in_weight.shape, BF16),
            pltpu.VMEM(bc_weight.shape, BF16),
            pltpu.VMEM(out_weight.shape, BF16),
            pltpu.VMEM((inner, 3 * LANES), BF16),
            pltpu.VMEM((8, LANES), F32),
            pltpu.VMEM((2 * R, model), BF16),
            pltpu.VMEM((5 * STRIP, model), BF16),
            pltpu.VMEM((5 * STRIP, inner), F32),
            pltpu.VMEM((R + 2, 24, inner), F32),
            pltpu.VMEM((R, C, inner), F32),
            pltpu.VMEM((2, R + 16, inner), F32),
            pltpu.VMEM((R, C, inner), F32),
            pltpu.VMEM((count, inner), F32),
            pltpu.VMEM((count, inner), BF16),
            pltpu.VMEM((nc, count, inner), BF16),
            pltpu.VMEM((nr, count, inner), BF16),
            pltpu.VMEM((count, inner), F32),
            pltpu.VMEM((count, inner), F32),
            pltpu.VMEM((2 * count, inner), BF16),
            pltpu.VMEM((count, inner), F32),
            pltpu.VMEM((2, 3 * count, count), BF16),
            pltpu.VMEM(((BATCH + 1) * count, BATCH * count), BF16),
            pltpu.VMEM((len(LENGTHS), stacked, stacked), BF16),
            pltpu.VMEM((len(LENGTHS), 2 * LENGTHS[-1] * STRIP, stacked), F32),
            pltpu.VMEM((2, count, count), F32),
            pltpu.VMEM((2, count, count), F32),
            pltpu.VMEM((2, LANES, inner), BF16),
            pltpu.VMEM((inner, inner), BF16),
            pltpu.VMEM((top_state.shape[2] // LANES * heads, C * LANES), BF16),
            pltpu.VMEM((count, inner), F32),
            pltpu.VMEM((count, inner), F32),
            pltpu.VMEM((count, inner), F32),
            pltpu.VMEM((count, inner), F32),
            pltpu.VMEM((2 * count, LANES), BF16),
            pltpu.VMEM((count, inner), BF16),
            pltpu.VMEM((count, inner), BF16),
            pltpu.VMEM((CORNERS * STRIP, LANES), BF16),
            pltpu.VMEM((CORNERS * STRIP, LANES), BF16),
            pltpu.SemaphoreType.DMA((5,)),
            pltpu.SemaphoreType.DMA((7,)),
            pltpu.SemaphoreType.DMA((8,)),
            pltpu.SemaphoreType.DMA((8,)),
            pltpu.SemaphoreType.DMA((nc, CHUNKS)),
            pltpu.SemaphoreType.DMA((nc, CHUNKS)),
            pltpu.SemaphoreType.DMA((nr,)),
            pltpu.SemaphoreType.DMA((nr,)),
            pltpu.SemaphoreType.DMA((nr,)),
            pltpu.SemaphoreType.DMA((2,)),
            pltpu.SemaphoreType.DMA((CHUNKS,)),
            pltpu.SemaphoreType.DMA((CHUNKS,)),
            pltpu.SemaphoreType.REGULAR,
        ],
        compiler_params=pltpu.CompilerParams(
            collective_id=0, has_side_effects=True, vmem_limit_bytes=48000 * 1024
        ),
    )(
        *(
            pltpu.with_memory_space_constraint(x, pltpu.HBM)
            for x in (
                tokens.reshape(count, model),
                top_state,
                in_weight,
                bc_weight,
                out_weight,
                conv_weight,
                step_weight.T,
                step_bias[None],
                across_rate[None],
                down_rate[None],
                skip_gain[None],
                norm_gain[None],
            )
        )
    )
    return result.reshape(R, C, model)


def solution(mesh):
    in_specs = (
        P(("groups", "rows"), "cols", None),
        P(("groups", "cols"), None, None),
    ) + (P(),) * 10
    out_specs = P(("groups", "rows"), "cols", None)
    return jax.shard_map(
        functools.partial(shards, mesh.shape["rows"], mesh.shape["cols"]),
        mesh=mesh, in_specs=in_specs, out_specs=out_specs, check_vma=False,
    )
```

```python
import functools

import jax
import jax.numpy as jnp
from jax import lax
from jax.experimental import pallas as pl
from jax.experimental.pallas import tpu as pltpu
from jax.sharding import PartitionSpec as P

F32 = jnp.float32
BF16 = jnp.bfloat16
NEIGHBOURS = ((-1, 0), (1, 0), (0, -1), (0, 1), (-1, -1), (-1, 1), (1, -1), (1, 1))
OPPOSITE = (1, 0, 3, 2, 7, 6, 5, 4)
STRIP = 16
LANES = 128
PIECES = ((0, 2), (2, 2), (4, 2), (6, 2))
CHUNKS = len(PIECES)
ADDED = 3
LENGTHS = sorted({n for _, n in PIECES})
BATCH = 3
CORNERS = 4


def dot(a, b):
    return jnp.dot(a, b, preferred_element_type=F32)


def dot_nt(a, b):
    return lax.dot_general(a, b, (((1,), (1,)), ((), ())), preferred_element_type=F32)


def softplus(x):
    return jnp.maximum(x, 0.0) + jnp.log1p(jnp.exp(-jnp.abs(x)))


def silu(x):
    return x / (1.0 + jnp.exp(-x))


def kernel(
    nr, nc, R, C, heads,
    tok_h, top_h, win_h, wbc_h, wout_h, conv_h, wst_h, bias_h, rate_a_h, rate_d_h, skip_h, gain_h, out,
    conv, wst_t, step_bias, rate_a, rate_d, skip, gain,
    tok, top, win, wbc, wout, wall, param, edge, halo, halo_f, pad, inner_sum, sides, side_sum, gate, vals, rva, rvd, acc_a, acc_d,
    weighted, y_ref, masks, mask_d, mask_a, same_a, same_f, upto_f, spread_r, moves_r, top_r, grow_a, grow_d, exit_y, exit_d,
    cbuf, ysend, yrecv, corner, far_corner,
    ld_sem, sm_sem, hs_sem, hr_sem, as_sem, ar_sem, ds_sem, dr_sem, rl_sem, q_sem, ys_sem, yr_sem, far_sem,
):
    count = R * C
    inner = wout.shape[0]
    state = wbc.shape[1] // 4
    width = inner // heads
    group = 2 * heads
    penult, last = nc - 2, nc - 1
    before = nc - 2
    i = lax.axis_index("rows")
    j = lax.axis_index("cols")
    mesh = pl.DeviceIdType.MESH

    def exists(k):
        di, dj = NEIGHBOURS[k]
        a, b = i + di, j + dj
        return (a >= 0) & (a < nr) & (b >= 0) & (b < nc)

    def target(k):
        di, dj = NEIGHBOURS[k]
        return {"rows": i + di, "cols": j + dj}

    loads = [
        pltpu.make_async_copy(a, b, ld_sem.at[n])
        for n, (a, b) in enumerate(
            ((tok_h, tok), (win_h, win), (wbc_h, wbc), (top_h, top), (wout_h, wout))
        )
    ]
    small = [
        pltpu.make_async_copy(a, b, sm_sem.at[n])
        for n, (a, b) in enumerate(
            (
                (wst_h, wst_t), (bias_h, step_bias), (rate_a_h, rate_a), (rate_d_h, rate_d),
                (skip_h, skip), (conv_h, conv), (gain_h, gain),
            )
        )
    ]
    loads[0].start()
    loads[1].start()
    for load in small:
        load.start()
    for load in loads[2:]:
        load.start()

    barrier = pltpu.get_barrier_semaphore()
    for d in range(1, nr):
        pl.semaphore_signal(
            barrier, inc=1, device_id={"rows": lax.rem(i + d, nr)}, device_id_type=mesh
        )
    for k in range(2, 8):
        @pl.when(exists(k))
        def _(k=k):
            pl.semaphore_signal(barrier, inc=1, device_id=target(k), device_id_type=mesh)

    def as_mask(m):
        return jnp.where(m, 1.0, 0.0).astype(BF16)

    pos = lax.broadcasted_iota(jnp.int32, (2 * R, count), 0)
    src = lax.broadcasted_iota(jnp.int32, (2 * R, count), 1)
    wanted = jnp.where(pos < R, pos * C, (pos - R) * C + C - 1)
    param[...] = jnp.zeros_like(param)
    loads[0].wait()
    edge[...] = dot(as_mask(src == wanted), tok[...]).astype(BF16)
    slot_at = lax.broadcasted_iota(jnp.int32, (CORNERS * STRIP, count), 0)
    token_at = lax.broadcasted_iota(jnp.int32, (CORNERS * STRIP, count), 1)
    which = lax.div(slot_at, STRIP)
    at_corner = token_at == lax.div(which, 2) * (count - C) + lax.rem(which, 2) * (C - 1)
    corner[...] = sum(
        dot(as_mask(at_corner & (lax.rem(slot_at, STRIP) == n)), tok[:, n * LANES : (n + 1) * LANES])
        for n in range(tok.shape[1] // LANES)
    ).astype(BF16)
    around = sum(jnp.where(exists(k), 1, 0) for k in range(2, 8))
    pl.semaphore_wait(barrier, nr - 1 + around)

    def halo_copy(k):
        di, dj = NEIGHBOURS[k]
        if k >= CORNERS:
            piece = corner.at[pl.ds((k - CORNERS) * STRIP, STRIP)]
            place = far_corner.at[pl.ds((OPPOSITE[k] - CORNERS) * STRIP, STRIP)]
        else:
            if di < 0:
                piece = tok.at[pl.ds(0, STRIP)]
            elif di > 0:
                piece = tok.at[pl.ds(count - STRIP, STRIP)]
            else:
                piece = edge.at[pl.ds(0 if dj < 0 else R, STRIP)]
            place = halo.at[pl.ds(OPPOSITE[k] * STRIP, STRIP)]
        return pltpu.make_async_remote_copy(
            src_ref=piece,
            dst_ref=place,
            send_sem=hs_sem.at[k],
            recv_sem=hr_sem.at[OPPOSITE[k]],
            device_id=target(k),
            device_id_type=mesh,
        )

    for k in (4, 5, 6, 7, 2, 3, 0, 1):
        @pl.when(exists(k))
        def _(k=k):
            halo_copy(k).start()

    for k in range(8):
        @pl.when(jnp.logical_not(exists(k)))
        def _(k=k):
            if k >= CORNERS:
                far_corner[pl.ds((k - CORNERS) * STRIP, STRIP)] = jnp.zeros((STRIP, LANES), BF16)
            else:
                halo[pl.ds(k * STRIP, STRIP)] = jnp.zeros((STRIP, halo.shape[1]), BF16)

    def tell_left(amount):
        pl.semaphore_signal(far_sem, inc=amount, device_id={"cols": j - 1}, device_id_type=mesh)

    @pl.when((j >= 1) & (j <= penult))
    def _():
        tell_left(1)

    loads[1].wait()
    projected = dot(tok[...], win[...])
    gate[...] = silu(projected[:, inner:].astype(BF16).astype(F32))
    mixer = projected[:, :inner].astype(BF16).astype(F32)
    pad[...] = jnp.zeros_like(pad)
    sides[...] = jnp.zeros_like(sides)
    side_sum[...] = jnp.zeros_like(side_sum)
    pad[pl.ds(1, R), pl.ds(8, C), :] = mixer.reshape(R, C, inner)
    small[5].wait()

    def tap(a, b):
        return conv[pl.ds(3 * a + b, 1), :]

    own = jnp.zeros((R, C, inner), F32)
    for b in range(3):
        moved = pad[:, pl.ds(7 + b, C), :]
        for a in range(3):
            own = own + tap(a, b).reshape(1, 1, inner) * moved[a : a + R]
    inner_sum[...] = own

    for n in range(1, nc - 1):
        @pl.when(penult - j == n)
        def _(n=n):
            pl.semaphore_wait(far_sem, n)

            @pl.when(j >= 1)
            def _():
                tell_left(n)

    for load in small[:5]:
        load.wait()
    for g in range(LANES // group):
        param[0:1, g * group : (g + 1) * group] = step_bias[...]
        param[1:2, g * group : g * group + heads] = rate_a[...]
        param[1:2, g * group + heads : (g + 1) * group] = rate_d[...]
    param[2:3, 0:heads] = skip[...]
    bias = param[0:1, :]
    rate = param[1:2, :]
    loads[2].wait()
    wall[:, 0:LANES] = wbc[:, 0:LANES]
    wall[:, LANES : 2 * LANES] = jnp.concatenate([wst_t[...]] * (LANES // group), axis=0).astype(F32).T.astype(BF16)
    wall[:, 2 * LANES : 3 * LANES] = wbc[:, LANES : 2 * LANES]

    q = lax.broadcasted_iota(jnp.int32, (count, count), 0)
    k_ = lax.broadcasted_iota(jnp.int32, (count, count), 1)
    same_row = lax.div(q, C) == lax.div(k_, C)
    same_col = lax.rem(q, C) == lax.rem(k_, C)
    for n, same in enumerate((same_row, same_col)):
        masks[n, pl.ds(0, count), :] = as_mask(same & (k_ <= q))
        masks[n, pl.ds(count, count), :] = as_mask(same & (k_ > q))
        masks[n, pl.ds(2 * count, count), :] = as_mask(same)
        same_f[n] = jnp.where(same, 1.0, 0.0)
        upto_f[n] = jnp.where(same & (k_ <= q), 1.0, 0.0)
    p_d = lax.broadcasted_iota(jnp.int32, (BATCH * count, BATCH * count), 0)
    o_d = lax.broadcasted_iota(jnp.int32, (BATCH * count, BATCH * count), 1)
    near_d = lax.rem(p_d, C) == lax.rem(o_d, C)
    mask_d[pl.ds(0, BATCH * count), :] = as_mask(near_d & (o_d > p_d))
    mask_d[pl.ds(BATCH * count, count), :] = as_mask(near_d[:count])
    stacked = last * LENGTHS[-1] * STRIP
    p_a = lax.broadcasted_iota(jnp.int32, (stacked, stacked), 0)
    o_a = lax.broadcasted_iota(jnp.int32, (stacked, stacked), 1)
    p_q = lax.broadcasted_iota(jnp.int32, same_a.shape[1:], 0)
    o_q = lax.broadcasted_iota(jnp.int32, same_a.shape[1:], 1)
    for n, length in enumerate(LENGTHS):
        size = length * STRIP
        near_a = lax.div(lax.rem(p_a, size), C) == lax.div(lax.rem(o_a, size), C)
        mask_a[n] = as_mask(near_a & (o_a > p_a))
        near_q = lax.div(lax.rem(p_q, size), C) == lax.div(lax.rem(o_q, size), C)
        same_a[n] = jnp.where(near_q, 1.0, 0.0)
    spot = lax.broadcasted_iota(jnp.int32, (LANES, inner), 0)
    head = lax.div(lax.broadcasted_iota(jnp.int32, (LANES, inner), 1), width)
    for n in range(2):
        row = head + n * heads
        spread_r[n] = as_mask((spot == row) | (spot == row + group))
    lane_from = lax.broadcasted_iota(jnp.int32, (inner, inner), 0)
    lane_to = lax.broadcasted_iota(jnp.int32, (inner, inner), 1)
    pairs = width * state // LANES
    half_size = pairs * heads
    parity = lax.div(lane_from, half_size)
    pair = lax.div(lax.rem(lane_from, half_size), heads)
    moves_r[...] = as_mask(lax.rem(lane_from, heads) * width + 2 * pair + parity == lane_to)
    loads[3].wait()
    for c in range(C):
        for n in range(pairs):
            top_r[pl.ds(n * heads, heads), c * LANES : (c + 1) * LANES] = top[c, :, n * LANES : (n + 1) * LANES]

    lane = lax.broadcasted_iota(jnp.int32, (count, LANES), 1)
    low_lanes = lax.rem(lax.div(lax.broadcasted_iota(jnp.int32, (1, LANES), 1), group), 2) == 1

    def halves_of(x):
        return jnp.where(low_lanes, x - x.astype(BF16).astype(F32), x).astype(BF16)

    def masked_sum(mask, x):
        r = dot(mask, x)
        return r + pltpu.roll(r, group, 1)

    for k in range(8):
        @pl.when(exists(k))
        def _(k=k):
            if k >= CORNERS:
                piece = corner.at[pl.ds(0, STRIP)]
                place = far_corner.at[pl.ds((k - CORNERS) * STRIP, STRIP)]
            else:
                piece = edge.at[pl.ds(0, STRIP)]
                place = halo.at[pl.ds(k * STRIP, STRIP)]
            pltpu.make_async_remote_copy(
                src_ref=piece,
                dst_ref=place,
                send_sem=hs_sem.at[k],
                recv_sem=hr_sem.at[k],
                device_id=target(k),
                device_id_type=mesh,
            ).wait_recv()

    packed = far_corner[...].astype(F32)
    rows = [
        jnp.concatenate(
            [packed[t * STRIP + n : t * STRIP + n + 1] for n in range(tok.shape[1] // LANES)], axis=1
        )
        for t in range(CORNERS)
    ]
    rows.append(jnp.zeros((STRIP - CORNERS, tok.shape[1]), F32))
    halo[pl.ds(4 * STRIP, STRIP), :] = jnp.concatenate(rows, axis=0).astype(BF16)
    halo_f[...] = dot(halo[...], win[:, :inner]).astype(BF16).astype(F32)

    def halo_rows(k, first, n):
        return halo_f[pl.ds(k * STRIP + first, n), :]

    pad[0, pl.ds(8, C), :] = halo_rows(0, STRIP - C, C)
    pad[R + 1, pl.ds(8, C), :] = halo_rows(1, 0, C)
    pad[0, pl.ds(7, 1), :] = halo_rows(4, 0, 1)
    pad[0, pl.ds(8 + C, 1), :] = halo_rows(4, 1, 1)
    pad[R + 1, pl.ds(7, 1), :] = halo_rows(4, 2, 1)
    pad[R + 1, pl.ds(8 + C, 1), :] = halo_rows(4, 3, 1)
    for n in range(2):
        sides[n, pl.ds(8, R), :] = halo_rows(2 + n, 0, R)
        side = sum(tap(a, 2 * n) * sides[n, pl.ds(7 + a, R), :] for a in range(3))
        for r in range(R):
            side_sum[r, pl.ds(n * (C - 1), 1), :] = side[r : r + 1]
    small[6].wait()
    for a, r in ((0, 0), (2, R - 1)):
        inner_sum[r] += sum(tap(a, b) * pad[r + a, pl.ds(7 + b, C), :] for b in range(3))
    def chunk_a(buffer, slot, c):
        rows = pl.ds(PIECES[c][0] * STRIP, PIECES[c][1] * STRIP)
        return buffer.at[rows] if slot is None else buffer.at[slot, rows]

    def send_a(d, c):
        return pltpu.make_async_remote_copy(
            src_ref=chunk_a(vals, None, c), dst_ref=chunk_a(rva, j, c), send_sem=as_sem.at[d, c],
            recv_sem=ar_sem.at[j, c], device_id={"cols": j + d}, device_id_type=mesh,
        )

    def arrival_a(slot, c):
        return pltpu.make_async_remote_copy(
            src_ref=chunk_a(vals, None, c), dst_ref=chunk_a(rva, slot, c), send_sem=as_sem.at[0, c],
            recv_sem=ar_sem.at[slot, c], device_id={"cols": slot}, device_id_type=mesh,
        )

    def send_d(d):
        return pltpu.make_async_remote_copy(
            src_ref=vals, dst_ref=rvd.at[i], send_sem=ds_sem.at[d], recv_sem=dr_sem.at[i],
            device_id={"rows": i + d}, device_id_type=mesh,
        )

    def sends_d(d):
        return (i + d < nr) & (lax.rem(i, 2) == 0) if d == 1 else i + d < nr

    hops_d = [1] + list(range(2, nr, 2))
    sibling = i + 1 - 2 * lax.rem(i, 2)

    def relay_d(slot):
        return pltpu.make_async_remote_copy(
            src_ref=rvd.at[slot], dst_ref=rvd.at[slot], send_sem=rl_sem.at[slot],
            recv_sem=dr_sem.at[slot], device_id={"rows": sibling}, device_id_type=mesh,
        )

    def arrival_d(slot):
        return pltpu.make_async_remote_copy(
            src_ref=vals, dst_ref=rvd.at[slot], send_sem=ds_sem.at[0],
            recv_sem=dr_sem.at[slot], device_id={"rows": slot}, device_id_type=mesh,
        )

    query = pltpu.make_async_remote_copy(
        src_ref=cbuf.at[pl.ds(0, count)], dst_ref=cbuf.at[pl.ds(count, count)], send_sem=q_sem.at[0],
        recv_sem=q_sem.at[1], device_id={"cols": j - 1}, device_id_type=mesh,
    )
    def answer(c):
        return pltpu.make_async_remote_copy(
            src_ref=chunk_a(ysend, None, c), dst_ref=chunk_a(yrecv, None, c), send_sem=ys_sem.at[c],
            recv_sem=yr_sem.at[c], device_id={"cols": j + 1}, device_id_type=mesh,
        )

    def furthest(c):
        return penult if c < ADDED else last

    for c, (first, length) in enumerate(PIECES):
        grid_rows = pl.ds(first * STRIP // C, length * STRIP // C)
        summed = inner_sum[grid_rows] + side_sum[grid_rows]
        vals[pl.ds(first * STRIP, length * STRIP), :] = silu(summed).reshape(length * STRIP, inner).astype(BF16)
        for d in range(1, nc) if c > 1 else range(nc - 1, 0, -1):
            @pl.when(j + d <= furthest(c))
            def _(d=d, c=c):
                send_a(d, c).start()

    for d in hops_d[1:] + hops_d[:1]:
        @pl.when(sends_d(d))
        def _(d=d):
            send_d(d).start()

    full = dot(vals[...], wall[...])
    values_f = vals[...].astype(F32)
    map_a = full[:, :LANES]
    map_d = full[:, 2 * LANES :]
    c_a = jnp.where(lane < state, pltpu.roll(map_a, state, 1), 0.0).astype(BF16)
    c_d = jnp.where(lane < state, pltpu.roll(map_d, state, 1), 0.0).astype(BF16)
    cbuf[pl.ds(0, count), :] = c_a

    @pl.when(j == last)
    def _():
        query.start()

    steps = softplus(full[:, LANES : 2 * LANES] + bias)
    log_decay = halves_of(-steps * rate)
    cum_a = masked_sum(masks[0, pl.ds(0, count), :], log_decay)
    cum_d = masked_sum(masks[1, pl.ds(0, count), :], log_decay)
    score_a = dot_nt(c_a, map_a.astype(BF16)) * upto_f[0]
    score_d = dot_nt(c_d, map_d.astype(BF16)) * upto_f[1]
    step_halves = halves_of(steps)
    weighted[pl.ds(0, count), :] = (values_f * dot(step_halves, spread_r[0])).astype(BF16)
    weighted[pl.ds(count, count), :] = (values_f * dot(step_halves, spread_r[1])).astype(BF16)
    cum_at = cum_a.T
    cum_dt = cum_d.T
    per_group = LANES // width
    for g in range(inner // LANES):
        total = jnp.zeros((count, LANES), F32)
        for e in range(per_group):
            h = g * per_group + e
            diff_a = cum_a[:, h : h + 1] - cum_at[h : h + 1, :]
            hd = heads + h
            diff_d = cum_d[:, hd : hd + 1] - cum_dt[hd : hd + 1, :]
            mix_a = (jnp.exp(jnp.minimum(diff_a, 0.0)) * score_a).astype(BF16)
            mix_d = (jnp.exp(jnp.minimum(diff_d, 0.0)) * score_d).astype(BF16)
            mix = jnp.concatenate([mix_a, mix_d], axis=1)
            part = dot(mix, weighted[:, g * LANES : (g + 1) * LANES])
            total = jnp.where(lax.div(lane, width) == e, part, total)
        y_ref[:, g * LANES : (g + 1) * LANES] = total

    column = lax.rem(q, C)
    c_low = c_d.astype(F32)
    c_high = pltpu.roll(c_low, state, 1)
    picked = jnp.concatenate(
        [
            jnp.concatenate([jnp.where(column == c, h, 0.0).astype(BF16) for c in range(C)], axis=1)
            for h in (c_low, c_high)
        ],
        axis=0,
    )
    halves = dot_nt(picked, top_r[...])
    acc_d[...] = dot(
        jnp.concatenate([halves[:count], halves[count:]], axis=1).astype(BF16), moves_r[...]
    )
    grow_a[...] = dot(halves_of(jnp.exp(cum_a)), spread_r[0])
    grow_d[...] = dot(halves_of(jnp.exp(cum_d)), spread_r[1])
    skips = dot(halves_of(jnp.broadcast_to(param[2:3, :], (count, LANES))), spread_r[0])
    y_ref[...] += skips * vals[...].astype(F32)

    def leaving(n, steps, log_decay):
        r = masked_sum(masks[n, pl.ds(count, 2 * count), :], log_decay)
        weight = halves_of(steps * jnp.exp(r[:count]))
        whole = halves_of(jnp.exp(r[count:]))
        return dot(jnp.concatenate([weight, whole], axis=0), spread_r[n])

    def across(slot):
        block = rva[slot]
        made = dot(block, wall[:, : 2 * LANES])
        s = softplus(made[:, LANES:] + bias)
        e = leaving(0, s, halves_of(-s * rate))
        entry = (block.astype(F32) * e[:count]).astype(BF16)
        score = dot_nt(cbuf[pl.ds(0, count), :], made[:, :LANES].astype(BF16)) * same_f[0]
        rows = pl.ds(0, count)
        acc_a[rows, :] = acc_a[rows, :] * e[count:] + dot(score.astype(BF16), entry)

    def down(first, m):
        total = m * count
        block = rvd[pl.ds(first, m)].reshape(total, inner)
        made = dot(block, wall[:, LANES:])
        s = softplus(made[:, :LANES] + bias)
        mask = jnp.concatenate(
            [mask_d[pl.ds(0, total), :total], mask_d[pl.ds(BATCH * count, count), :total]], axis=0
        )
        r = masked_sum(mask, halves_of(-s * rate))
        weight = halves_of(s * jnp.exp(r[:total]))
        whole = halves_of(jnp.exp(r[total:]))
        e = dot(jnp.concatenate([weight, whole], axis=0), spread_r[1])
        entry = (block.astype(F32) * e[:total]).astype(BF16)
        score = dot_nt(c_d, made[:, LANES:].astype(BF16))
        near = jnp.concatenate([same_f[1]] * m, axis=1)
        acc_d[...] = acc_d[...] * e[total:] + dot((score * near).astype(BF16), entry)

    def left(c, blocks, added):
        first, size = PIECES[c][0] * STRIP, PIECES[c][1] * STRIP
        kind = LENGTHS.index(PIECES[c][1])
        rows = pl.ds(first, size)
        total = blocks * size
        block = rva[pl.ds(0, blocks), rows, :].reshape(total, inner)
        made = dot(block, wall[:, : 2 * LANES])
        s = softplus(made[:, LANES:] + bias)
        r = masked_sum(mask_a[kind, pl.ds(0, total), :total], halves_of(-s * rate))
        e = dot(halves_of(s * jnp.exp(r)), spread_r[0])
        entry = (block.astype(F32) * e).astype(BF16)
        queries = cbuf[rows, :]
        if added:
            queries = jnp.concatenate([queries, cbuf[pl.ds(count + first, size), :]], axis=0)
        near = same_a[kind, pl.ds(0, queries.shape[0]), :total]
        score = dot_nt(queries, made[:, :LANES].astype(BF16)) * near
        part = dot(score.astype(BF16), entry)
        if added:
            ysend[rows, :] = (part[size:] * exit_d[rows, :] + exit_y[rows, :]).astype(BF16)
            answer(c).start()
        acc_a[rows, :] = part[:size]

    acc_a[...] = jnp.zeros_like(acc_a)
    loads[4].wait()

    @pl.when(j == penult)
    def _():
        e = leaving(0, steps, log_decay)
        entry = (vals[...].astype(F32) * e[:count]).astype(BF16)
        exit_d[...] = e[count:]
        query.wait_recv()
        score = dot_nt(cbuf[pl.ds(count, count), :], map_a.astype(BF16)) * same_f[0]
        exit_y[...] = dot(score.astype(BF16), entry)

    def pass_on(t, carry):
        slot = lax.rem(i, 2) + 2 * t
        arrival_d(slot).wait_recv()
        relay_d(slot).start()
        return carry

    straight = lax.div(i, 2)

    @pl.when(j != penult)
    def _():
        lax.fori_loop(0, straight, pass_on, 0)

    @pl.when(j == penult)
    def _():
        for c in range(ADDED):
            if c == ADDED - 1:
                lax.fori_loop(0, straight, pass_on, 0)
            for slot in range(before):
                arrival_a(slot, c).wait_recv()
            left(c, before, True)

    def batch(b, carry):
        first = b * BATCH
        for m in range(BATCH):
            @pl.when((first + m < i) & (lax.rem(first + m + i, 2) == 1))
            def _(m=m):
                arrival_d(first + m).wait_recv()
        for m in range(1, BATCH + 1):
            @pl.when(i - first == m if m < BATCH else i - first >= m)
            def _(m=m):
                down(first, m)
        return carry

    lax.fori_loop(0, lax.div(i + BATCH - 1, BATCH), batch, 0)

    @pl.when(j == penult)
    def _():
        for c in range(ADDED, CHUNKS):
            for slot in range(before):
                arrival_a(slot, c).wait_recv()
            left(c, before, False)

    @pl.when(j < penult)
    def _():
        def hop(slot, carry):
            for c in range(CHUNKS):
                arrival_a(slot, c).wait_recv()
            across(slot)
            return carry

        lax.fori_loop(0, j, hop, 0)

    y_ref[...] = (y_ref[...] + grow_d[...] * acc_d[...]) * gate[...]
    grow_a[...] = grow_a[...] * gate[...]

    def finish(first, size, across_sum):
        rows = pl.ds(first, size)
        gated = y_ref[rows, :] + grow_a[rows, :] * across_sum[rows, :].astype(F32)
        scale = lax.rsqrt(jnp.mean(gated * gated, axis=-1, keepdims=True) + 1e-05)
        out[rows, :] = (dot((gated * gain[...]).astype(BF16), wout[...]) * scale).astype(BF16)

    @pl.when(j != last)
    def _():
        finish(0, count, acc_a)

    @pl.when(j == last)
    def _():
        for c in range(ADDED - 1):
            answer(c).wait_recv()
        final, after = PIECES[ADDED - 1][0] * STRIP, PIECES[ADDED][0] * STRIP
        finish(0, final, yrecv)
        for c in range(ADDED, CHUNKS):
            for slot in range(last):
                arrival_a(slot, c).wait_recv()
            left(c, last, False)
        answer(ADDED - 1).wait_recv()
        rows = pl.ds(final, after - final)
        acc_a[rows, :] = yrecv[rows, :].astype(F32)
        finish(final, count - final, acc_a)

    for k in range(8):
        @pl.when(exists(k))
        def _(k=k):
            halo_copy(k).wait_send()
    for c in range(CHUNKS):
        for d in range(1, nc):
            @pl.when(j + d <= furthest(c))
            def _(d=d, c=c):
                send_a(d, c).wait_send()

    for d in hops_d:
        @pl.when(sends_d(d))
        def _(d=d):
            send_d(d).wait_send()

    def passed_on(t, carry):
        relay_d(lax.rem(i, 2) + 2 * t).wait_send()
        return carry

    lax.fori_loop(0, straight, passed_on, 0)

    @pl.when(j == last)
    def _():
        query.wait_send()

    @pl.when(j == penult)
    def _():
        for c in range(ADDED):
            answer(c).wait_send()


def shards(
    nr, nc,
    tokens, top_state, in_weight, conv_weight, bc_weight, step_weight, step_bias,
    across_rate, down_rate, skip_gain, norm_gain, out_weight,
):
    R, C, model = tokens.shape
    inner = out_weight.shape[0]
    heads = across_rate.shape[0]
    count = R * C
    vmem = pl.BlockSpec(memory_space=pltpu.VMEM)
    stacked = (nc - 1) * LENGTHS[-1] * STRIP
    result = pl.pallas_call(
        functools.partial(kernel, nr, nc, R, C, heads),
        out_shape=jax.ShapeDtypeStruct((count, model), BF16),
        in_specs=[pl.BlockSpec(memory_space=pltpu.HBM)] * 12,
        out_specs=vmem,
        scratch_shapes=[
            pltpu.VMEM(conv_weight.shape, F32),
            pltpu.VMEM((2 * heads, inner), BF16),
            pltpu.VMEM((1, 2 * heads), F32),
            pltpu.VMEM((1, heads), F32),
            pltpu.VMEM((1, heads), F32),
            pltpu.VMEM((1, heads), F32),
            pltpu.VMEM((1, inner), F32),
            pltpu.VMEM((count, model), BF16),
            pltpu.VMEM(top_state.shape, BF16),
            pltpu.VMEM(in_weight.shape, BF16),
            pltpu.VMEM(bc_weight.shape, BF16),
            pltpu.VMEM(out_weight.shape, BF16),
            pltpu.VMEM((inner, 3 * LANES), BF16),
            pltpu.VMEM((8, LANES), F32),
            pltpu.VMEM((2 * R, model), BF16),
            pltpu.VMEM((5 * STRIP, model), BF16),
            pltpu.VMEM((5 * STRIP, inner), F32),
            pltpu.VMEM((R + 2, 24, inner), F32),
            pltpu.VMEM((R, C, inner), F32),
            pltpu.VMEM((2, R + 16, inner), F32),
            pltpu.VMEM((R, C, inner), F32),
            pltpu.VMEM((count, inner), F32),
            pltpu.VMEM((count, inner), BF16),
            pltpu.VMEM((nc, count, inner), BF16),
            pltpu.VMEM((nr, count, inner), BF16),
            pltpu.VMEM((count, inner), F32),
            pltpu.VMEM((count, inner), F32),
            pltpu.VMEM((2 * count, inner), BF16),
            pltpu.VMEM((count, inner), F32),
            pltpu.VMEM((2, 3 * count, count), BF16),
            pltpu.VMEM(((BATCH + 1) * count, BATCH * count), BF16),
            pltpu.VMEM((len(LENGTHS), stacked, stacked), BF16),
            pltpu.VMEM((len(LENGTHS), 2 * LENGTHS[-1] * STRIP, stacked), F32),
            pltpu.VMEM((2, count, count), F32),
            pltpu.VMEM((2, count, count), F32),
            pltpu.VMEM((2, LANES, inner), BF16),
            pltpu.VMEM((inner, inner), BF16),
            pltpu.VMEM((top_state.shape[2] // LANES * heads, C * LANES), BF16),
            pltpu.VMEM((count, inner), F32),
            pltpu.VMEM((count, inner), F32),
            pltpu.VMEM((count, inner), F32),
            pltpu.VMEM((count, inner), F32),
            pltpu.VMEM((2 * count, LANES), BF16),
            pltpu.VMEM((count, inner), BF16),
            pltpu.VMEM((count, inner), BF16),
            pltpu.VMEM((CORNERS * STRIP, LANES), BF16),
            pltpu.VMEM((CORNERS * STRIP, LANES), BF16),
            pltpu.SemaphoreType.DMA((5,)),
            pltpu.SemaphoreType.DMA((7,)),
            pltpu.SemaphoreType.DMA((8,)),
            pltpu.SemaphoreType.DMA((8,)),
            pltpu.SemaphoreType.DMA((nc, CHUNKS)),
            pltpu.SemaphoreType.DMA((nc, CHUNKS)),
            pltpu.SemaphoreType.DMA((nr,)),
            pltpu.SemaphoreType.DMA((nr,)),
            pltpu.SemaphoreType.DMA((nr,)),
            pltpu.SemaphoreType.DMA((2,)),
            pltpu.SemaphoreType.DMA((CHUNKS,)),
            pltpu.SemaphoreType.DMA((CHUNKS,)),
            pltpu.SemaphoreType.REGULAR,
        ],
        compiler_params=pltpu.CompilerParams(
            collective_id=0, has_side_effects=True, vmem_limit_bytes=48000 * 1024
        ),
    )(
        *(
            pltpu.with_memory_space_constraint(x, pltpu.HBM)
            for x in (
                tokens.reshape(count, model),
                top_state,
                in_weight,
                bc_weight,
                out_weight,
                conv_weight,
                step_weight.T,
                step_bias[None],
                across_rate[None],
                down_rate[None],
                skip_gain[None],
                norm_gain[None],
            )
        )
    )
    return result.reshape(R, C, model)


def solution(mesh):
    in_specs = (
        P(("groups", "rows"), "cols", None),
        P(("groups", "cols"), None, None),
    ) + (P(),) * 10
    out_specs = P(("groups", "rows"), "cols", None)
    return jax.shard_map(
        functools.partial(shards, mesh.shape["rows"], mesh.shape["cols"]),
        mesh=mesh, in_specs=in_specs, out_specs=out_specs, check_vma=False,
    )
```

```python
import functools

import jax
import jax.numpy as jnp
from jax import lax
from jax.experimental import pallas as pl
from jax.experimental.pallas import tpu as pltpu
from jax.sharding import PartitionSpec as P

F32 = jnp.float32
BF16 = jnp.bfloat16
NEIGHBOURS = ((-1, 0), (1, 0), (0, -1), (0, 1), (-1, -1), (-1, 1), (1, -1), (1, 1))
OPPOSITE = (1, 0, 3, 2, 7, 6, 5, 4)
STRIP = 16
LANES = 128
PIECES = ((0, 2), (2, 2), (4, 2), (6, 2))
CHUNKS = len(PIECES)
ADDED = 3
LENGTHS = sorted({n for _, n in PIECES})
BATCH = 3
CORNERS = 4


def dot(a, b):
    return jnp.dot(a, b, preferred_element_type=F32)


def dot_nt(a, b):
    return lax.dot_general(a, b, (((1,), (1,)), ((), ())), preferred_element_type=F32)


def softplus(x):
    return jnp.maximum(x, 0.0) + jnp.log1p(jnp.exp(-jnp.abs(x)))


def silu(x):
    return x / (1.0 + jnp.exp(-x))


def kernel(
    nr, nc, R, C, heads,
    tok_h, top_h, win_h, wbc_h, wout_h, conv_h, wst_h, bias_h, rate_a_h, rate_d_h, skip_h, gain_h, out,
    conv, wst_t, step_bias, rate_a, rate_d, skip, gain,
    tok, top, win, wbc, wout, wall, param, edge, halo, halo_f, pad, inner_sum, sides, side_sum, gate, vals, rva, rvd, acc_a, acc_d,
    weighted, y_ref, masks, mask_d, mask_a, same_a, same_f, upto_f, spread_r, moves_r, top_r, grow_a, grow_d, exit_y, exit_d,
    cbuf, ysend, yrecv, corner, far_corner,
    ld_sem, sm_sem, hs_sem, hr_sem, as_sem, ar_sem, ds_sem, dr_sem, rl_sem, q_sem, ys_sem, yr_sem, far_sem,
):
    count = R * C
    inner = wout.shape[0]
    state = wbc.shape[1] // 4
    width = inner // heads
    group = 2 * heads
    penult, last = nc - 2, nc - 1
    before = nc - 2
    i = lax.axis_index("rows")
    j = lax.axis_index("cols")
    mesh = pl.DeviceIdType.MESH

    def exists(k):
        di, dj = NEIGHBOURS[k]
        a, b = i + di, j + dj
        return (a >= 0) & (a < nr) & (b >= 0) & (b < nc)

    def target(k):
        di, dj = NEIGHBOURS[k]
        return {"rows": i + di, "cols": j + dj}

    loads = [
        pltpu.make_async_copy(a, b, ld_sem.at[n])
        for n, (a, b) in enumerate(
            ((tok_h, tok), (win_h, win), (wbc_h, wbc), (top_h, top), (wout_h, wout))
        )
    ]
    small = [
        pltpu.make_async_copy(a, b, sm_sem.at[n])
        for n, (a, b) in enumerate(
            (
                (wst_h, wst_t), (bias_h, step_bias), (rate_a_h, rate_a), (rate_d_h, rate_d),
                (skip_h, skip), (conv_h, conv), (gain_h, gain),
            )
        )
    ]
    loads[0].start()
    loads[1].start()
    for load in small:
        load.start()
    for load in loads[2:]:
        load.start()

    barrier = pltpu.get_barrier_semaphore()
    for d in range(1, nr):
        pl.semaphore_signal(
            barrier, inc=1, device_id={"rows": lax.rem(i + d, nr)}, device_id_type=mesh
        )
    for k in range(2, 8):
        @pl.when(exists(k))
        def _(k=k):
            pl.semaphore_signal(barrier, inc=1, device_id=target(k), device_id_type=mesh)

    def as_mask(m):
        return jnp.where(m, 1.0, 0.0).astype(BF16)

    pos = lax.broadcasted_iota(jnp.int32, (2 * R, count), 0)
    src = lax.broadcasted_iota(jnp.int32, (2 * R, count), 1)
    wanted = jnp.where(pos < R, pos * C, (pos - R) * C + C - 1)
    param[...] = jnp.zeros_like(param)
    loads[0].wait()
    edge[...] = dot(as_mask(src == wanted), tok[...]).astype(BF16)
    slot_at = lax.broadcasted_iota(jnp.int32, (CORNERS * STRIP, count), 0)
    token_at = lax.broadcasted_iota(jnp.int32, (CORNERS * STRIP, count), 1)
    which = lax.div(slot_at, STRIP)
    at_corner = token_at == lax.div(which, 2) * (count - C) + lax.rem(which, 2) * (C - 1)
    corner[...] = sum(
        dot(as_mask(at_corner & (lax.rem(slot_at, STRIP) == n)), tok[:, n * LANES : (n + 1) * LANES])
        for n in range(tok.shape[1] // LANES)
    ).astype(BF16)
    around = sum(jnp.where(exists(k), 1, 0) for k in range(2, 8))
    pl.semaphore_wait(barrier, nr - 1 + around)

    def halo_copy(k):
        di, dj = NEIGHBOURS[k]
        if k >= CORNERS:
            piece = corner.at[pl.ds((k - CORNERS) * STRIP, STRIP)]
            place = far_corner.at[pl.ds((OPPOSITE[k] - CORNERS) * STRIP, STRIP)]
        else:
            if di < 0:
                piece = tok.at[pl.ds(0, STRIP)]
            elif di > 0:
                piece = tok.at[pl.ds(count - STRIP, STRIP)]
            else:
                piece = edge.at[pl.ds(0 if dj < 0 else R, STRIP)]
            place = halo.at[pl.ds(OPPOSITE[k] * STRIP, STRIP)]
        return pltpu.make_async_remote_copy(
            src_ref=piece,
            dst_ref=place,
            send_sem=hs_sem.at[k],
            recv_sem=hr_sem.at[OPPOSITE[k]],
            device_id=target(k),
            device_id_type=mesh,
        )

    for k in (4, 5, 6, 7, 2, 3, 0, 1):
        @pl.when(exists(k))
        def _(k=k):
            halo_copy(k).start()

    for k in range(8):
        @pl.when(jnp.logical_not(exists(k)))
        def _(k=k):
            if k >= CORNERS:
                far_corner[pl.ds((k - CORNERS) * STRIP, STRIP)] = jnp.zeros((STRIP, LANES), BF16)
            else:
                halo[pl.ds(k * STRIP, STRIP)] = jnp.zeros((STRIP, halo.shape[1]), BF16)

    def tell_left(amount):
        pl.semaphore_signal(far_sem, inc=amount, device_id={"cols": j - 1}, device_id_type=mesh)

    @pl.when((j >= 1) & (j <= penult))
    def _():
        tell_left(1)

    loads[1].wait()
    projected = dot(tok[...], win[...])
    gate[...] = silu(projected[:, inner:].astype(BF16).astype(F32))
    mixer = projected[:, :inner].astype(BF16).astype(F32)
    pad[...] = jnp.zeros_like(pad)
    sides[...] = jnp.zeros_like(sides)
    side_sum[...] = jnp.zeros_like(side_sum)
    pad[pl.ds(1, R), pl.ds(8, C), :] = mixer.reshape(R, C, inner)
    small[5].wait()

    def tap(a, b):
        return conv[pl.ds(3 * a + b, 1), :]

    own = jnp.zeros((R, C, inner), F32)
    for b in range(3):
        moved = pad[:, pl.ds(7 + b, C), :]
        for a in range(3):
            own = own + tap(a, b).reshape(1, 1, inner) * moved[a : a + R]
    inner_sum[...] = own

    for n in range(1, nc - 1):
        @pl.when(penult - j == n)
        def _(n=n):
            pl.semaphore_wait(far_sem, n)

            @pl.when(j >= 1)
            def _():
                tell_left(n)

    for load in small[:5]:
        load.wait()
    for g in range(LANES // group):
        param[0:1, g * group : (g + 1) * group] = step_bias[...]
        param[1:2, g * group : g * group + heads] = rate_a[...]
        param[1:2, g * group + heads : (g + 1) * group] = rate_d[...]
    param[2:3, 0:heads] = skip[...]
    bias = param[0:1, :]
    rate = param[1:2, :]
    loads[2].wait()
    wall[:, 0:LANES] = wbc[:, 0:LANES]
    wall[:, LANES : 2 * LANES] = jnp.concatenate([wst_t[...]] * (LANES // group), axis=0).astype(F32).T.astype(BF16)
    wall[:, 2 * LANES : 3 * LANES] = wbc[:, LANES : 2 * LANES]

    q = lax.broadcasted_iota(jnp.int32, (count, count), 0)
    k_ = lax.broadcasted_iota(jnp.int32, (count, count), 1)
    same_row = lax.div(q, C) == lax.div(k_, C)
    same_col = lax.rem(q, C) == lax.rem(k_, C)
    for n, same in enumerate((same_row, same_col)):
        masks[n, pl.ds(0, count), :] = as_mask(same & (k_ <= q))
        masks[n, pl.ds(count, count), :] = as_mask(same & (k_ > q))
        masks[n, pl.ds(2 * count, count), :] = as_mask(same)
        same_f[n] = jnp.where(same, 1.0, 0.0)
        upto_f[n] = jnp.where(same & (k_ <= q), 1.0, 0.0)
    p_d = lax.broadcasted_iota(jnp.int32, (BATCH * count, BATCH * count), 0)
    o_d = lax.broadcasted_iota(jnp.int32, (BATCH * count, BATCH * count), 1)
    near_d = lax.rem(p_d, C) == lax.rem(o_d, C)
    mask_d[pl.ds(0, BATCH * count), :] = as_mask(near_d & (o_d > p_d))
    mask_d[pl.ds(BATCH * count, count), :] = as_mask(near_d[:count])
    stacked = last * LENGTHS[-1] * STRIP
    p_a = lax.broadcasted_iota(jnp.int32, (stacked, stacked), 0)
    o_a = lax.broadcasted_iota(jnp.int32, (stacked, stacked), 1)
    p_q = lax.broadcasted_iota(jnp.int32, same_a.shape[1:], 0)
    o_q = lax.broadcasted_iota(jnp.int32, same_a.shape[1:], 1)
    for n, length in enumerate(LENGTHS):
        size = length * STRIP
        near_a = lax.div(lax.rem(p_a, size), C) == lax.div(lax.rem(o_a, size), C)
        mask_a[n] = as_mask(near_a & (o_a > p_a))
        near_q = lax.div(lax.rem(p_q, size), C) == lax.div(lax.rem(o_q, size), C)
        same_a[n] = jnp.where(near_q, 1.0, 0.0)
    spot = lax.broadcasted_iota(jnp.int32, (LANES, inner), 0)
    head = lax.div(lax.broadcasted_iota(jnp.int32, (LANES, inner), 1), width)
    for n in range(2):
        row = head + n * heads
        spread_r[n] = as_mask((spot == row) | (spot == row + group))
    lane_from = lax.broadcasted_iota(jnp.int32, (inner, inner), 0)
    lane_to = lax.broadcasted_iota(jnp.int32, (inner, inner), 1)
    pairs = width * state // LANES
    half_size = pairs * heads
    parity = lax.div(lane_from, half_size)
    pair = lax.div(lax.rem(lane_from, half_size), heads)
    moves_r[...] = as_mask(lax.rem(lane_from, heads) * width + 2 * pair + parity == lane_to)
    loads[3].wait()
    for c in range(C):
        for n in range(pairs):
            top_r[pl.ds(n * heads, heads), c * LANES : (c + 1) * LANES] = top[c, :, n * LANES : (n + 1) * LANES]

    lane = lax.broadcasted_iota(jnp.int32, (count, LANES), 1)
    low_lanes = lax.rem(lax.div(lax.broadcasted_iota(jnp.int32, (1, LANES), 1), group), 2) == 1

    def halves_of(x):
        return jnp.where(low_lanes, x - x.astype(BF16).astype(F32), x).astype(BF16)

    def masked_sum(mask, x):
        r = dot(mask, x)
        return r + pltpu.roll(r, group, 1)

    for k in range(8):
        @pl.when(exists(k))
        def _(k=k):
            if k >= CORNERS:
                piece = corner.at[pl.ds(0, STRIP)]
                place = far_corner.at[pl.ds((k - CORNERS) * STRIP, STRIP)]
            else:
                piece = edge.at[pl.ds(0, STRIP)]
                place = halo.at[pl.ds(k * STRIP, STRIP)]
            pltpu.make_async_remote_copy(
                src_ref=piece,
                dst_ref=place,
                send_sem=hs_sem.at[k],
                recv_sem=hr_sem.at[k],
                device_id=target(k),
                device_id_type=mesh,
            ).wait_recv()

    packed = far_corner[...].astype(F32)
    rows = [
        jnp.concatenate(
            [packed[t * STRIP + n : t * STRIP + n + 1] for n in range(tok.shape[1] // LANES)], axis=1
        )
        for t in range(CORNERS)
    ]
    rows.append(jnp.zeros((STRIP - CORNERS, tok.shape[1]), F32))
    halo[pl.ds(4 * STRIP, STRIP), :] = jnp.concatenate(rows, axis=0).astype(BF16)
    halo_f[...] = dot(halo[...], win[:, :inner]).astype(BF16).astype(F32)

    def halo_rows(k, first, n):
        return halo_f[pl.ds(k * STRIP + first, n), :]

    pad[0, pl.ds(8, C), :] = halo_rows(0, STRIP - C, C)
    pad[R + 1, pl.ds(8, C), :] = halo_rows(1, 0, C)
    pad[0, pl.ds(7, 1), :] = halo_rows(4, 0, 1)
    pad[0, pl.ds(8 + C, 1), :] = halo_rows(4, 1, 1)
    pad[R + 1, pl.ds(7, 1), :] = halo_rows(4, 2, 1)
    pad[R + 1, pl.ds(8 + C, 1), :] = halo_rows(4, 3, 1)
    for n in range(2):
        sides[n, pl.ds(8, R), :] = halo_rows(2 + n, 0, R)
        side = sum(tap(a, 2 * n) * sides[n, pl.ds(7 + a, R), :] for a in range(3))
        for r in range(R):
            side_sum[r, pl.ds(n * (C - 1), 1), :] = side[r : r + 1]
    small[6].wait()
    for a, r in ((0, 0), (2, R - 1)):
        inner_sum[r] += sum(tap(a, b) * pad[r + a, pl.ds(7 + b, C), :] for b in range(3))
    def chunk_a(buffer, slot, c):
        rows = pl.ds(PIECES[c][0] * STRIP, PIECES[c][1] * STRIP)
        return buffer.at[rows] if slot is None else buffer.at[slot, rows]

    def send_a(d, c):
        return pltpu.make_async_remote_copy(
            src_ref=chunk_a(vals, None, c), dst_ref=chunk_a(rva, j, c), send_sem=as_sem.at[d, c],
            recv_sem=ar_sem.at[j, c], device_id={"cols": j + d}, device_id_type=mesh,
        )

    def arrival_a(slot, c):
        return pltpu.make_async_remote_copy(
            src_ref=chunk_a(vals, None, c), dst_ref=chunk_a(rva, slot, c), send_sem=as_sem.at[0, c],
            recv_sem=ar_sem.at[slot, c], device_id={"cols": slot}, device_id_type=mesh,
        )

    def send_d(d):
        return pltpu.make_async_remote_copy(
            src_ref=vals, dst_ref=rvd.at[i], send_sem=ds_sem.at[d], recv_sem=dr_sem.at[i],
            device_id={"rows": i + d}, device_id_type=mesh,
        )

    def sends_d(d):
        return (i + d < nr) & (lax.rem(i, 2) == 0) if d == 1 else i + d < nr

    hops_d = [1] + list(range(2, nr, 2))
    sibling = i + 1 - 2 * lax.rem(i, 2)

    def relay_d(slot):
        return pltpu.make_async_remote_copy(
            src_ref=rvd.at[slot], dst_ref=rvd.at[slot], send_sem=rl_sem.at[slot],
            recv_sem=dr_sem.at[slot], device_id={"rows": sibling}, device_id_type=mesh,
        )

    def arrival_d(slot):
        return pltpu.make_async_remote_copy(
            src_ref=vals, dst_ref=rvd.at[slot], send_sem=ds_sem.at[0],
            recv_sem=dr_sem.at[slot], device_id={"rows": slot}, device_id_type=mesh,
        )

    query = pltpu.make_async_remote_copy(
        src_ref=cbuf.at[pl.ds(0, count)], dst_ref=cbuf.at[pl.ds(count, count)], send_sem=q_sem.at[0],
        recv_sem=q_sem.at[1], device_id={"cols": j - 1}, device_id_type=mesh,
    )
    def answer(c):
        return pltpu.make_async_remote_copy(
            src_ref=chunk_a(ysend, None, c), dst_ref=chunk_a(yrecv, None, c), send_sem=ys_sem.at[c],
            recv_sem=yr_sem.at[c], device_id={"cols": j + 1}, device_id_type=mesh,
        )

    def furthest(c):
        return penult if c < ADDED else last

    for c, (first, length) in enumerate(PIECES):
        grid_rows = pl.ds(first * STRIP // C, length * STRIP // C)
        summed = inner_sum[grid_rows] + side_sum[grid_rows]
        vals[pl.ds(first * STRIP, length * STRIP), :] = silu(summed).reshape(length * STRIP, inner).astype(BF16)
        for d in range(1, nc) if c > 1 else range(nc - 1, 0, -1):
            @pl.when(j + d <= furthest(c))
            def _(d=d, c=c):
                send_a(d, c).start()

    full = dot(vals[...], wall[...])
    values_f = vals[...].astype(F32)
    map_a = full[:, :LANES]
    map_d = full[:, 2 * LANES :]
    c_a = jnp.where(lane < state, pltpu.roll(map_a, state, 1), 0.0).astype(BF16)
    c_d = jnp.where(lane < state, pltpu.roll(map_d, state, 1), 0.0).astype(BF16)
    cbuf[pl.ds(0, count), :] = c_a

    @pl.when(j == last)
    def _():
        query.start()

    for d in hops_d[1:] + hops_d[:1]:
        @pl.when(sends_d(d))
        def _(d=d):
            send_d(d).start()

    steps = softplus(full[:, LANES : 2 * LANES] + bias)
    log_decay = halves_of(-steps * rate)
    cum_a = masked_sum(masks[0, pl.ds(0, count), :], log_decay)
    cum_d = masked_sum(masks[1, pl.ds(0, count), :], log_decay)
    score_a = dot_nt(c_a, map_a.astype(BF16)) * upto_f[0]
    score_d = dot_nt(c_d, map_d.astype(BF16)) * upto_f[1]
    step_halves = halves_of(steps)
    weighted[pl.ds(0, count), :] = (values_f * dot(step_halves, spread_r[0])).astype(BF16)
    weighted[pl.ds(count, count), :] = (values_f * dot(step_halves, spread_r[1])).astype(BF16)
    cum_at = cum_a.T
    cum_dt = cum_d.T
    per_group = LANES // width
    for g in range(inner // LANES):
        total = jnp.zeros((count, LANES), F32)
        for e in range(per_group):
            h = g * per_group + e
            diff_a = cum_a[:, h : h + 1] - cum_at[h : h + 1, :]
            hd = heads + h
            diff_d = cum_d[:, hd : hd + 1] - cum_dt[hd : hd + 1, :]
            mix_a = (jnp.exp(jnp.minimum(diff_a, 0.0)) * score_a).astype(BF16)
            mix_d = (jnp.exp(jnp.minimum(diff_d, 0.0)) * score_d).astype(BF16)
            mix = jnp.concatenate([mix_a, mix_d], axis=1)
            part = dot(mix, weighted[:, g * LANES : (g + 1) * LANES])
            total = jnp.where(lax.div(lane, width) == e, part, total)
        y_ref[:, g * LANES : (g + 1) * LANES] = total

    column = lax.rem(q, C)
    c_low = c_d.astype(F32)
    c_high = pltpu.roll(c_low, state, 1)
    picked = jnp.concatenate(
        [
            jnp.concatenate([jnp.where(column == c, h, 0.0).astype(BF16) for c in range(C)], axis=1)
            for h in (c_low, c_high)
        ],
        axis=0,
    )
    halves = dot_nt(picked, top_r[...])
    acc_d[...] = dot(
        jnp.concatenate([halves[:count], halves[count:]], axis=1).astype(BF16), moves_r[...]
    )
    grow_a[...] = dot(halves_of(jnp.exp(cum_a)), spread_r[0])
    grow_d[...] = dot(halves_of(jnp.exp(cum_d)), spread_r[1])
    skips = dot(halves_of(jnp.broadcast_to(param[2:3, :], (count, LANES))), spread_r[0])
    y_ref[...] += skips * vals[...].astype(F32)

    def leaving(n, steps, log_decay):
        r = masked_sum(masks[n, pl.ds(count, 2 * count), :], log_decay)
        weight = halves_of(steps * jnp.exp(r[:count]))
        whole = halves_of(jnp.exp(r[count:]))
        return dot(jnp.concatenate([weight, whole], axis=0), spread_r[n])

    def across(slot):
        block = rva[slot]
        made = dot(block, wall[:, : 2 * LANES])
        s = softplus(made[:, LANES:] + bias)
        e = leaving(0, s, halves_of(-s * rate))
        entry = (block.astype(F32) * e[:count]).astype(BF16)
        score = dot_nt(cbuf[pl.ds(0, count), :], made[:, :LANES].astype(BF16)) * same_f[0]
        rows = pl.ds(0, count)
        acc_a[rows, :] = acc_a[rows, :] * e[count:] + dot(score.astype(BF16), entry)

    def down(first, m):
        total = m * count
        block = rvd[pl.ds(first, m)].reshape(total, inner)
        made = dot(block, wall[:, LANES:])
        s = softplus(made[:, :LANES] + bias)
        mask = jnp.concatenate(
            [mask_d[pl.ds(0, total), :total], mask_d[pl.ds(BATCH * count, count), :total]], axis=0
        )
        r = masked_sum(mask, halves_of(-s * rate))
        weight = halves_of(s * jnp.exp(r[:total]))
        whole = halves_of(jnp.exp(r[total:]))
        e = dot(jnp.concatenate([weight, whole], axis=0), spread_r[1])
        entry = (block.astype(F32) * e[:total]).astype(BF16)
        score = dot_nt(c_d, made[:, LANES:].astype(BF16))
        near = jnp.concatenate([same_f[1]] * m, axis=1)
        acc_d[...] = acc_d[...] * e[total:] + dot((score * near).astype(BF16), entry)

    def left(c, blocks, added):
        first, size = PIECES[c][0] * STRIP, PIECES[c][1] * STRIP
        kind = LENGTHS.index(PIECES[c][1])
        rows = pl.ds(first, size)
        total = blocks * size
        block = rva[pl.ds(0, blocks), rows, :].reshape(total, inner)
        made = dot(block, wall[:, : 2 * LANES])
        s = softplus(made[:, LANES:] + bias)
        r = masked_sum(mask_a[kind, pl.ds(0, total), :total], halves_of(-s * rate))
        e = dot(halves_of(s * jnp.exp(r)), spread_r[0])
        entry = (block.astype(F32) * e).astype(BF16)
        queries = cbuf[rows, :]
        if added:
            queries = jnp.concatenate([queries, cbuf[pl.ds(count + first, size), :]], axis=0)
        near = same_a[kind, pl.ds(0, queries.shape[0]), :total]
        score = dot_nt(queries, made[:, :LANES].astype(BF16)) * near
        part = dot(score.astype(BF16), entry)
        if added:
            ysend[rows, :] = (part[size:] * exit_d[rows, :] + exit_y[rows, :]).astype(BF16)
            answer(c).start()
        acc_a[rows, :] = part[:size]

    acc_a[...] = jnp.zeros_like(acc_a)
    loads[4].wait()

    @pl.when(j == penult)
    def _():
        e = leaving(0, steps, log_decay)
        entry = (vals[...].astype(F32) * e[:count]).astype(BF16)
        exit_d[...] = e[count:]
        query.wait_recv()
        score = dot_nt(cbuf[pl.ds(count, count), :], map_a.astype(BF16)) * same_f[0]
        exit_y[...] = dot(score.astype(BF16), entry)

    def pass_on(t, carry):
        slot = lax.rem(i, 2) + 2 * t
        arrival_d(slot).wait_recv()
        relay_d(slot).start()
        return carry

    straight = lax.div(i, 2)

    @pl.when(j != penult)
    def _():
        lax.fori_loop(0, straight, pass_on, 0)

    @pl.when(j == penult)
    def _():
        for c in range(ADDED):
            if c == ADDED - 1:
                lax.fori_loop(0, straight, pass_on, 0)
            for slot in range(before):
                arrival_a(slot, c).wait_recv()
            left(c, before, True)

    def batch(b, carry):
        first = b * BATCH
        for m in range(BATCH):
            @pl.when((first + m < i) & (lax.rem(first + m + i, 2) == 1))
            def _(m=m):
                arrival_d(first + m).wait_recv()
        for m in range(1, BATCH + 1):
            @pl.when(i - first == m if m < BATCH else i - first >= m)
            def _(m=m):
                down(first, m)
        return carry

    lax.fori_loop(0, lax.div(i + BATCH - 1, BATCH), batch, 0)

    @pl.when(j == penult)
    def _():
        for c in range(ADDED, CHUNKS):
            for slot in range(before):
                arrival_a(slot, c).wait_recv()
            left(c, before, False)

    @pl.when(j < penult)
    def _():
        def hop(slot, carry):
            for c in range(CHUNKS):
                arrival_a(slot, c).wait_recv()
            across(slot)
            return carry

        lax.fori_loop(0, j, hop, 0)

    y_ref[...] = (y_ref[...] + grow_d[...] * acc_d[...]) * gate[...]
    grow_a[...] = grow_a[...] * gate[...]

    @pl.when(j == last)
    def _():
        for c in range(ADDED, CHUNKS):
            for slot in range(last):
                arrival_a(slot, c).wait_recv()
            left(c, last, False)
        for c in range(ADDED):
            answer(c).wait_recv()
        rows = pl.ds(0, PIECES[ADDED][0] * STRIP)
        acc_a[rows, :] = yrecv[rows, :].astype(F32)

    gated = y_ref[...] + grow_a[...] * acc_a[...]
    scale = lax.rsqrt(jnp.mean(gated * gated, axis=-1, keepdims=True) + 1e-05)
    out[...] = (dot((gated * gain[...]).astype(BF16), wout[...]) * scale).astype(BF16)

    for k in range(8):
        @pl.when(exists(k))
        def _(k=k):
            halo_copy(k).wait_send()
    for c in range(CHUNKS):
        for d in range(1, nc):
            @pl.when(j + d <= furthest(c))
            def _(d=d, c=c):
                send_a(d, c).wait_send()

    for d in hops_d:
        @pl.when(sends_d(d))
        def _(d=d):
            send_d(d).wait_send()

    def passed_on(t, carry):
        relay_d(lax.rem(i, 2) + 2 * t).wait_send()
        return carry

    lax.fori_loop(0, straight, passed_on, 0)

    @pl.when(j == last)
    def _():
        query.wait_send()

    @pl.when(j == penult)
    def _():
        for c in range(ADDED):
            answer(c).wait_send()


def shards(
    nr, nc,
    tokens, top_state, in_weight, conv_weight, bc_weight, step_weight, step_bias,
    across_rate, down_rate, skip_gain, norm_gain, out_weight,
):
    R, C, model = tokens.shape
    inner = out_weight.shape[0]
    heads = across_rate.shape[0]
    count = R * C
    vmem = pl.BlockSpec(memory_space=pltpu.VMEM)
    stacked = (nc - 1) * LENGTHS[-1] * STRIP
    result = pl.pallas_call(
        functools.partial(kernel, nr, nc, R, C, heads),
        out_shape=jax.ShapeDtypeStruct((count, model), BF16),
        in_specs=[pl.BlockSpec(memory_space=pltpu.HBM)] * 12,
        out_specs=vmem,
        scratch_shapes=[
            pltpu.VMEM(conv_weight.shape, F32),
            pltpu.VMEM((2 * heads, inner), BF16),
            pltpu.VMEM((1, 2 * heads), F32),
            pltpu.VMEM((1, heads), F32),
            pltpu.VMEM((1, heads), F32),
            pltpu.VMEM((1, heads), F32),
            pltpu.VMEM((1, inner), F32),
            pltpu.VMEM((count, model), BF16),
            pltpu.VMEM(top_state.shape, BF16),
            pltpu.VMEM(in_weight.shape, BF16),
            pltpu.VMEM(bc_weight.shape, BF16),
            pltpu.VMEM(out_weight.shape, BF16),
            pltpu.VMEM((inner, 3 * LANES), BF16),
            pltpu.VMEM((8, LANES), F32),
            pltpu.VMEM((2 * R, model), BF16),
            pltpu.VMEM((5 * STRIP, model), BF16),
            pltpu.VMEM((5 * STRIP, inner), F32),
            pltpu.VMEM((R + 2, 24, inner), F32),
            pltpu.VMEM((R, C, inner), F32),
            pltpu.VMEM((2, R + 16, inner), F32),
            pltpu.VMEM((R, C, inner), F32),
            pltpu.VMEM((count, inner), F32),
            pltpu.VMEM((count, inner), BF16),
            pltpu.VMEM((nc, count, inner), BF16),
            pltpu.VMEM((nr, count, inner), BF16),
            pltpu.VMEM((count, inner), F32),
            pltpu.VMEM((count, inner), F32),
            pltpu.VMEM((2 * count, inner), BF16),
            pltpu.VMEM((count, inner), F32),
            pltpu.VMEM((2, 3 * count, count), BF16),
            pltpu.VMEM(((BATCH + 1) * count, BATCH * count), BF16),
            pltpu.VMEM((len(LENGTHS), stacked, stacked), BF16),
            pltpu.VMEM((len(LENGTHS), 2 * LENGTHS[-1] * STRIP, stacked), F32),
            pltpu.VMEM((2, count, count), F32),
            pltpu.VMEM((2, count, count), F32),
            pltpu.VMEM((2, LANES, inner), BF16),
            pltpu.VMEM((inner, inner), BF16),
            pltpu.VMEM((top_state.shape[2] // LANES * heads, C * LANES), BF16),
            pltpu.VMEM((count, inner), F32),
            pltpu.VMEM((count, inner), F32),
            pltpu.VMEM((count, inner), F32),
            pltpu.VMEM((count, inner), F32),
            pltpu.VMEM((2 * count, LANES), BF16),
            pltpu.VMEM((count, inner), BF16),
            pltpu.VMEM((count, inner), BF16),
            pltpu.VMEM((CORNERS * STRIP, LANES), BF16),
            pltpu.VMEM((CORNERS * STRIP, LANES), BF16),
            pltpu.SemaphoreType.DMA((5,)),
            pltpu.SemaphoreType.DMA((7,)),
            pltpu.SemaphoreType.DMA((8,)),
            pltpu.SemaphoreType.DMA((8,)),
            pltpu.SemaphoreType.DMA((nc, CHUNKS)),
            pltpu.SemaphoreType.DMA((nc, CHUNKS)),
            pltpu.SemaphoreType.DMA((nr,)),
            pltpu.SemaphoreType.DMA((nr,)),
            pltpu.SemaphoreType.DMA((nr,)),
            pltpu.SemaphoreType.DMA((2,)),
            pltpu.SemaphoreType.DMA((CHUNKS,)),
            pltpu.SemaphoreType.DMA((CHUNKS,)),
            pltpu.SemaphoreType.REGULAR,
        ],
        compiler_params=pltpu.CompilerParams(
            collective_id=0, has_side_effects=True, vmem_limit_bytes=48000 * 1024
        ),
    )(
        *(
            pltpu.with_memory_space_constraint(x, pltpu.HBM)
            for x in (
                tokens.reshape(count, model),
                top_state,
                in_weight,
                bc_weight,
                out_weight,
                conv_weight,
                step_weight.T,
                step_bias[None],
                across_rate[None],
                down_rate[None],
                skip_gain[None],
                norm_gain[None],
            )
        )
    )
    return result.reshape(R, C, model)


def solution(mesh):
    in_specs = (
        P(("groups", "rows"), "cols", None),
        P(("groups", "cols"), None, None),
    ) + (P(),) * 10
    out_specs = P(("groups", "rows"), "cols", None)
    return jax.shard_map(
        functools.partial(shards, mesh.shape["rows"], mesh.shape["cols"]),
        mesh=mesh, in_specs=in_specs, out_specs=out_specs, check_vma=False,
    )
```
